512 devices in a mesh: depth: 8 (over y, core), gx: 16 (over z), gy: 4 (over x).
Axes of the slice: x: 4, y: 4, z: 16, core: 2. Of those that a mesh axis runs over, the one named last changes fastest.
Arguments:
- slowness: float32 [16, 256, 1024], P('depth', 'gx', 'gy'), may hold values from 0.5 to 1.5
- air_mask: int32 [16, 256, 1024], P('depth', 'gx', 'gy'), may hold values from 0 to 1, as said below
- reflector: int32 [256, 1024], P('gx', 'gy'), may hold values from 4 to 15
- shot_cells: int32 [8, 2], replicated, may hold values from 0 to 255
- receiver_mask: int32 [8, 256, 1024], P(None, 'gx', 'gy'), may hold values 0 or 1
- residual: float32 [8, 256, 1024], P(None, 'gx', 'gy'), may hold values from -6 to 6
Outputs:
- gradient: float32 [16, 256, 1024], P('depth', 'gx', 'gy')
The draws below stay inside these ranges and needn't reach their ends.
Inputs may be any that keep to these rules, and one draw needn't show every extreme that they name: `air_mask`: each lateral column is air in a top run of 0 to 2 cells and earth below; some column has exactly 2 air cells.
All inputs are finite; a program needn't handle non-finite values. No bound on the sum of `receiver_mask` on one device may be relied on, other than what follows from the above.
Results may differ from the reference program's by a relative error of at most 0.0003.
Values sent between devices are 32-bit elements; how exact they have to be, the bound alone decides.
No kernel may reach another device: no remote copies, remote signals or barrier semaphores. Data moves between devices by JAX's collectives and lax.ppermute only.
A program may use at most 64 MiB of HBM per device.

```python
import math
import jax
import jax.numpy as jnp
from jax import lax

SHOTS = 8
NX = 256
NY = 1024
NZ = 16


def draw_air_mask(key, part):
    heights = jax.random.randint(jax.random.fold_in(key, 11), (NX, NY), 0, NZ // 8 + 1)
    heights = heights.at[0, 0].set(NZ // 8)
    zpos = jnp.arange(NZ, dtype=jnp.int32)[:, None, None]
    return (zpos < heights[None]).astype(jnp.int32)


def touch_ends(values, key, least, high):
    spot = [jax.random.randint(jax.random.fold_in(key, axis), (), 0, length) for axis, length in enumerate(values.shape)]
    widest = values.shape.index(max(values.shape))
    next_to = spot[:widest] + [(spot[widest] + 1) % values.shape[widest]] + spot[widest + 1:]
    return values.at[tuple(spot)].set(least).at[tuple(next_to)].set(high)


def block_scale(key, dims, pieces, least, high):
    factor_of, own = 1.0, jax.random.fold_in(key, 6)
    for dim, blocks in pieces:
        draws = jnp.exp(jax.random.uniform(jax.random.fold_in(own, dim), (blocks,), jnp.float32, least / len(pieces), high / len(pieces)))
        factor_of = factor_of * jnp.repeat(draws, dims[dim] // blocks).reshape([-1 if axis == dim else 1 for axis in range(len(dims))])
    return factor_of


def scatter_about(stream_key, extent, deviation, bound, shards=(), kind=jnp.bfloat16):
    entries = deviation * jax.random.normal(stream_key, extent, jnp.float32)
    if shards:
        entries = entries * block_scale(stream_key, extent, shards, -0.22, 0.18)
    return jnp.clip(entries, -bound, bound).astype(kind)


def setup_inputs(seed: int = 0) -> dict:
    streams_of = jax.random.split(jax.random.key(seed), 7)
    slowness = jnp.clip(0.5 + 1.0 * jax.random.uniform(streams_of[0], (NZ, NX, NY), jnp.float32) ** block_scale(streams_of[0], (NZ, NX, NY), ((0, 8), (1, 16), (2, 4)), -0.2, 0.2), 0.5, 1.5)
    air_mask = draw_air_mask(jax.random.fold_in(streams_of[6], 71), 0)
    reflector = touch_ends(jax.random.randint(streams_of[2], (NX, NY), NZ // 4, NZ), jax.random.fold_in(streams_of[2], 1), NZ // 4, NZ - 1).astype(jnp.int32)
    shot_cells = touch_ends(jax.random.randint(streams_of[3], (SHOTS, 2), 0, min(NX, NY)), jax.random.fold_in(streams_of[3], 1), 0, (min(NX, NY)) - 1).astype(jnp.int32)
    receiver_mask = touch_ends((jax.random.randint(streams_of[4], (SHOTS, NX, NY), 0, 2) < 1).astype(jnp.int32), jax.random.fold_in(streams_of[4], 1), 0, 1)
    residual = scatter_about(streams_of[5], (SHOTS, NX, NY), 1.0, 6.0, ((1, 16), (2, 4)), jnp.float32)
    return {"slowness": slowness, "air_mask": air_mask, "reflector": reflector, "shot_cells": shot_cells, "receiver_mask": receiver_mask, "residual": residual}


SOFTMIN_TEMPER = 0.5
SURF = 0.7
AIR_SLOW = 2.5
STEP_PENALTY = 10000.0
STENCIL_SHIFTS = [(first_term, second_term) for first_term in (-1, 0, 1) for second_term in (-1, 0, 1)]

def neighbour_value(field, first_term, second_term):
    padded_layer = jnp.pad(field, ((0, 0), (1, 1), (1, 1)))
    return padded_layer[:, 1 + first_term:1 + first_term + NX, 1 + second_term:1 + second_term + NY]

def backshift(field, first_term, second_term):
    padded_layer = jnp.pad(field, ((0, 0), (1, 1), (1, 1)))
    return padded_layer[:, 1 - first_term:1 - first_term + NX, 1 - second_term:1 - second_term + NY]

def reference(slowness, air_mask, reflector, shot_cells, receiver_mask, residual):
    speed = jnp.where(air_mask == 1, jnp.float32(AIR_SLOW), slowness)
    xpos = jnp.arange(NX, dtype=jnp.int32)
    ypos = jnp.arange(NY, dtype=jnp.int32)
    shot_x = shot_cells[:, 0].astype(jnp.float32)
    shot_y = shot_cells[:, 1].astype(jnp.float32)
    surface = SURF * jnp.sqrt((xpos.astype(jnp.float32)[None, :, None] - shot_x[:, None, None]) ** 2 + (ypos.astype(jnp.float32)[None, None, :] - shot_y[:, None, None]) ** 2)
    penalty_terms = []
    span_lengths = []
    for first_term, second_term in STENCIL_SHIFTS:
        valid_mask = ((xpos + first_term >= 0) & (xpos + first_term < NX))[:, None] & ((ypos + second_term >= 0) & (ypos + second_term < NY))[None, :]
        penalty_terms.append(jnp.where(valid_mask, jnp.float32(0.0), jnp.float32(STEP_PENALTY)))
        span_lengths.append(math.sqrt(1.0 + first_term * first_term + second_term * second_term))

    def forward(prior_layer, depth_layer):
        candidate_times = [neighbour_value(prior_layer, first_term, second_term) + depth_layer * span_lengths[stencil_index] + penalty_terms[stencil_index] for stencil_index, (first_term, second_term) in enumerate(STENCIL_SHIFTS)]
        lowest = candidate_times[0]
        for c in candidate_times[1:]:
            lowest = jnp.minimum(lowest, c)
        total = jnp.exp(-(candidate_times[0] - lowest) / SOFTMIN_TEMPER)
        for c in candidate_times[1:]:
            total = total + jnp.exp(-(c - lowest) / SOFTMIN_TEMPER)
        nxt = lowest - SOFTMIN_TEMPER * jnp.log(total)
        return (nxt, nxt)
    unused, times = lax.scan(forward, surface, speed)
    source = jnp.where(receiver_mask == 1, residual, jnp.float32(0.0))

    def adjoint(back, k):
        current_layer = lax.dynamic_index_in_dim(times, k, 0, keepdims=False)
        earlier = lax.dynamic_index_in_dim(times, jnp.maximum(k - 1, 0).astype(jnp.int32), 0, keepdims=False)
        previous_times = jnp.where(k > 0, earlier, surface)
        depth_layer = lax.dynamic_index_in_dim(speed, k, 0, keepdims=False)
        hit = (reflector == k).astype(jnp.float32)
        lam = source * hit[None] + back
        weight_sum = jnp.zeros_like(lam)
        back_new = jnp.zeros_like(lam)
        for stencil_index, (first_term, second_term) in enumerate(STENCIL_SHIFTS):
            softmin_weight = jnp.exp(-(neighbour_value(previous_times, first_term, second_term) + depth_layer * span_lengths[stencil_index] + penalty_terms[stencil_index] - current_layer) / SOFTMIN_TEMPER)
            weight_sum = weight_sum + softmin_weight * span_lengths[stencil_index]
            back_new = back_new + backshift(lam * softmin_weight, first_term, second_term)
        return (back_new, lax.optimization_barrier(jnp.sum(lam * weight_sum, axis=0)))
    unused2, grads = lax.scan(adjoint, jnp.zeros_like(surface), jnp.arange(NZ, dtype=jnp.int32), reverse=True)
    earth = air_mask == 0
    zpos = jnp.arange(NZ, dtype=jnp.int32)
    colsum = lax.optimization_barrier(jnp.sum(source, axis=0))
    below = zpos[:, None, None] <= reflector[None]
    raw = jnp.where(earth, grads, jnp.float32(0.0)) + jnp.where(earth & below, colsum[None], jnp.float32(0.0))
    padded_layer = jnp.pad(raw, ((0, 0), (1, 1), (1, 1)))
    beside_all = jnp.zeros_like(raw)
    for first_term, second_term in STENCIL_SHIFTS:
        if first_term != 0 or second_term != 0:
            beside_all = beside_all + padded_layer[:, 1 + first_term:1 + first_term + NX, 1 + second_term:1 + second_term + NY]
    return 0.5 * raw + 0.0625 * beside_all
```

```python
import math

import jax
import jax.numpy as jnp
from jax import lax
from jax.experimental import pallas as pl
from jax.experimental.pallas import tpu as pltpu
from jax.sharding import PartitionSpec as P

SOFTMIN_TEMPER = 0.5
SURF = 0.7
AIR_SLOW = 2.5
AIR_TEST = 2.0
STEP_PENALTY = 10000.0
RATE = 1.0 / SOFTMIN_TEMPER
ROOT2 = math.sqrt(2.0)
ROOT3 = math.sqrt(3.0)

LANES = 128
STRIP = 32
ROWS = 16
PLANES = 16
SHOTS = 8
FRAME = 80
PAD = 8
FULL = FRAME + 2 * PAD
A_ROWS = 64
S_ROWS = 40
A_AT = (0, A_ROWS, 2 * A_ROWS + S_ROWS, 3 * A_ROWS + 2 * S_ROWS, 4 * A_ROWS + 3 * S_ROWS)
S_AT = (2 * A_ROWS, 3 * A_ROWS + S_ROWS, 4 * A_ROWS + 2 * S_ROWS)
HALF = 8
VMEM_BYTES = 40 * 1024 * 1024


def rolled(value, shift):
    shift = shift % LANES
    return value if shift == 0 else pltpu.roll(value, shift, value.ndim - 1)


def lane_index(rows=8):
    return lax.broadcasted_iota(jnp.int32, (rows, LANES), 1)


def quarters(parts, lane):
    out = parts[0]
    for j in range(1, len(parts)):
        out = jnp.where(lane >= STRIP * j, parts[j], out)
    return out


def pack_kernel(pos, slow_ref, air_ref, refl_ref, mask_ref, resid_ref, a_ref, s_ref):
    lane = lane_index()
    speed = {}
    for p in range(2):
        for h in range(2):
            for c in range(2):
                at = (p, pl.ds(HALF * h, HALF), pl.ds(LANES * c, LANES))
                speed[p, h, c] = jnp.where(air_ref[at] == 1, jnp.float32(AIR_SLOW), slow_ref[at])
    for target in range(8):
        c, q = divmod(target, 4)
        parts = [rolled(speed[j // 2, j % 2, c], STRIP * (j - q)) for j in range(4)]
        a_ref[pl.ds(HALF * target, HALF), :] = quarters(parts, lane)
    depth_pos = pos[0]
    high = depth_pos >= 4
    back = (LANES - STRIP * (depth_pos % 4)) % LANES

    def strip(low_part, high_part):
        return pltpu.roll(jnp.where(high, high_part, low_part), back, 1)

    for v in range(4):
        parts = []
        for i in range(4):
            x = 4 * v + i
            pieces = [
                jnp.where(
                    mask_ref[:, x, pl.ds(LANES * c, LANES)] == 1,
                    resid_ref[:, x, pl.ds(LANES * c, LANES)],
                    jnp.float32(0.0),
                )
                for c in range(2)
            ]
            parts.append(rolled(strip(*pieces), STRIP * i))
        s_ref[pl.ds(HALF * v, HALF), :] = quarters(parts, lane)
    parts = []
    for h in range(2):
        pieces = [
            refl_ref[pl.ds(HALF * h, HALF), pl.ds(LANES * c, LANES)].astype(jnp.float32)
            for c in range(2)
        ]
        parts.append(rolled(strip(*pieces), STRIP * h))
    s_ref[pl.ds(32, HALF), :] = quarters(parts, lane)


def sweep_kernel(
    pos,
    shot_ref,
    left_ref,
    here_ref,
    right_ref,
    out_ref,
    w_ref,
    e1_ref,
    e2_ref,
    e3_ref,
    gm_ref,
    gp_ref,
    hm_ref,
    hp_ref,
    head_ref,
    mu_ref,
    src_ref,
    refl_ref,
    wsel_ref,
    earth_ref,
    grad_ref,
    col_ref,
    raw_ref,
    nx_total,
    ny_total,
):
    lane = lane_index()
    sub = lax.broadcasted_iota(jnp.int32, (8, LANES), 0)
    x_base = pos[1] * ROWS - 2 * ROWS
    y_base = pos[2] * (8 * STRIP) + pos[0] * STRIP - STRIP
    y_cell = y_base + lane
    y_inside = (y_cell >= 0) & (y_cell < ny_total)
    zero = jnp.zeros((8, LANES), jnp.float32)

    def row_of(ref, lead, r):
        if lead is None:
            return ref[pl.ds(r, 8, stride=0), :]
        return ref[lead, pl.ds(r, 8, stride=0), :]

    def rim_factor(x_cell):
        inside = (x_cell >= 0) & (x_cell < nx_total) & y_inside
        penalty = jnp.where(inside, jnp.float32(0.0), jnp.float32(STEP_PENALTY))
        return jnp.exp(-penalty * RATE)

    shot_x = jnp.broadcast_to(shot_ref[:, 0:1].astype(jnp.float32), (8, LANES))
    shot_y = jnp.broadcast_to(shot_ref[:, 1:2].astype(jnp.float32), (8, LANES))
    y_square = (y_cell.astype(jnp.float32) - shot_y) ** 2

    def surface(r):
        x_cell = (x_base + r).astype(jnp.float32)
        return SURF * jnp.sqrt((x_cell - shot_x) ** 2 + y_square)

    def weight(diff):
        return jnp.exp(-diff * RATE)

    def near(diff):
        return jnp.clip(diff, -1.0, 1.0)

    def geometry(block, carry):
        before, now = carry
        for i in range(8):
            r = block * 8 + i
            after = surface(r + 1)
            gm_ref[r + PAD] = weight(near(pltpu.roll(now, 1, 1) - now))
            gp_ref[r + PAD] = weight(near(pltpu.roll(now, LANES - 1, 1) - now))
            hm_ref[r + PAD] = weight(before - now)
            hp_ref[r + PAD] = weight(after - now)
            w_ref[0, r + PAD] = rim_factor(x_base + r)
            before, now = now, after
        return before, now

    lax.fori_loop(0, FRAME // 8, geometry, (surface(-1), surface(0)))
    for ref in (gm_ref, gp_ref, hm_ref, hp_ref):
        ref[PAD - 1] = zero
        ref[PAD + FRAME] = zero
    for k in range(PLANES + 1):
        low, high = (-1, FRAME) if k < 8 else (7, FRAME - 8)
        w_ref[k, low + PAD] = zero
        w_ref[k, high + PAD] = zero

    def merged(tiles, j):
        part = tiles[0]
        one, two = (j + 1) % 4, (j + 2) % 4
        part = jnp.where((lane >= STRIP * one) & (lane < STRIP * (one + 1)), tiles[1], part)
        part = jnp.where((lane >= STRIP * two) & (lane < STRIP * (two + 1)), tiles[2], part)
        return rolled(part, -STRIP * j)

    def strips(row):
        at = (pl.ds(row, HALF), slice(None))
        return left_ref[at], rolled(here_ref[at], STRIP), rolled(right_ref[at], 2 * STRIP)

    rims = [rim_factor(x_base + HALF * g + sub) for g in range(FRAME // HALF)]

    def exponents(pair, carry):
        for offset in range(5):
            tiles = strips(pl.multiple_of(A_AT[offset] + HALF * pair, HALF))
            for j in range(4):
                p, h = divmod(j, 2)
                group = 2 * offset + h
                speed = merged(tiles, j)
                at = (2 * pair + p, pl.ds(HALF * group, HALF), slice(None))
                e1_ref[at] = jnp.exp(-speed * RATE) * rims[group]
                e2_ref[at] = jnp.exp(-(speed * ROOT2) * RATE) * rims[group]
                e3_ref[at] = jnp.exp(-(speed * ROOT3) * RATE) * rims[group]
                if 3 <= group < 7:
                    here = (2 * pair + p, pl.ds(HALF * (group - 3), HALF), slice(None))
                    earth_ref[here] = speed
        return carry

    lax.fori_loop(0, PLANES // 2, exponents, 0)

    for offset in range(3):
        for v in range(4):
            tiles = strips(S_AT[offset] + HALF * v)
            for i in range(4):
                src_ref[ROWS * offset + 4 * v + i] = merged(tiles, i)
        tiles = strips(S_AT[offset] + 32)
        for h in range(2):
            inside = rims[2 + 2 * offset + h] > 0.5
            refl_ref[pl.ds(ROWS * offset + HALF * h, HALF), :] = jnp.where(
                inside, merged(tiles, h), jnp.float32(-1.0)
            )

    def clear(r, carry):
        wsel_ref[r] = zero + 1.0
        return carry

    lax.fori_loop(0, 48, clear, 0)

    def along_y(value, r):
        return (
            gm_ref[r + PAD] * pltpu.roll(value, 1, 1)
            + gp_ref[r + PAD] * pltpu.roll(value, LANES - 1, 1)
        )

    def down_rows(k, first, last, carry, select, keep):
        level = k.astype(jnp.float32)

        def block(b, carry):
            w_before, q_before, w_now, q_now = carry
            for i in range(8):
                r = b * 8 + i
                w_after = w_ref[k, r + 1 + PAD]
                q_after = along_y(w_after, r + 1)
                hm = hm_ref[r + PAD]
                hp = hp_ref[r + PAD]
                edge = q_now + (hm * w_before + hp * w_after)
                corner = hm * q_before + hp * q_after
                part1 = row_of(e1_ref, k, r) * w_now
                part2 = row_of(e2_ref, k, r) * edge
                part3 = row_of(e3_ref, k, r) * corner
                w_next = part1 + part2 + part3
                w_ref[k + 1, r + PAD] = w_next
                if keep:
                    head_ref[k, r - 24] = part1 + ROOT2 * part2 + ROOT3 * part3
                if select:
                    hit = row_of(refl_ref, None, r - 16) == level
                    wsel_ref[r - 16] = jnp.where(hit, w_next, wsel_ref[r - 16])
                w_before, q_before, w_now, q_now = w_now, q_now, w_after, q_after
            return w_before, q_before, w_now, q_now

        return lax.fori_loop(first, last, block, carry)

    def down(first_block, segments):
        def plane(k, carry):
            r = first_block * 8
            w_before, w_now = w_ref[k, r - 1 + PAD], w_ref[k, r + PAD]
            state = (w_before, along_y(w_before, r - 1), w_now, along_y(w_now, r))
            for first, last, select, keep in segments:
                state = down_rows(k, first, last, state, select, keep)
            return carry

        return plane

    lax.fori_loop(
        0, 4, down(0, ((0, 3, False, False), (3, 7, False, True), (7, 10, False, False))), 0
    )
    hits = ((2, 3, True, False), (3, 7, True, True), (7, 8, True, False))
    lax.fori_loop(
        4, 7, down(0, ((0, 2, False, False), *hits, (8, 10, False, False))), 0
    )
    lax.fori_loop(
        7, PLANES, down(1, ((1, 2, False, False), *hits, (8, 9, False, False))), 0
    )

    mu_ref[15 + PAD] = zero
    mu_ref[64 + PAD] = zero

    def start(r, carry):
        share = src_ref[r] / wsel_ref[r]
        wsel_ref[r] = share
        hit = row_of(refl_ref, None, r) == float(PLANES - 1)
        mu_ref[r + 16 + PAD] = jnp.where(hit, share, jnp.float32(0.0))
        return carry

    lax.fori_loop(0, 48, start, 0)
    for i in range(18):
        col_ref[i : i + 1, :] = jnp.sum(src_ref[15 + i], axis=0, keepdims=True)

    def gradient_rows(k):
        for i in range(18):
            product = mu_ref[31 + i + PAD] * head_ref[k, 7 + i]
            grad_ref[k, i : i + 1, :] = jnp.sum(product, axis=0, keepdims=True)

    def spread(k, r):
        mu = mu_ref[r + PAD]
        u2 = row_of(e2_ref, k, r) * mu
        u3 = row_of(e3_ref, k, r) * mu
        hm = hm_ref[r + PAD]
        hp = hp_ref[r + PAD]
        return row_of(e1_ref, k, r) * mu, u2, hp * u2, hp * u3, hm * u2, hm * u3

    def up(first_block, last_block, base):
        def plane(step, carry):
            k = base - step
            gradient_rows(k)
            level = (k - 1).astype(jnp.float32)

            def block(b, carry):
                a_before, c_before, u1, u2, a_now, c_now = carry
                for i in range(8):
                    r = b * 8 + i
                    n1, n2, a_next, c_next, a_back, c_back = spread(k, r + 1)
                    both = u2 + (c_before + c_back)
                    side = pltpu.roll(gp_ref[r + PAD] * both, 1, 1) + pltpu.roll(
                        gm_ref[r + PAD] * both, LANES - 1, 1
                    )
                    hit = row_of(refl_ref, None, r - 16) == level
                    own = jnp.where(hit, wsel_ref[r - 16], jnp.float32(0.0))
                    mu_ref[r + PAD] = (u1 + own) + (a_before + a_back) + side
                    a_before, c_before, u1, u2, a_now, c_now = a_now, c_now, n1, n2, a_next, c_next
                return a_before, c_before, u1, u2, a_now, c_now

            _, _, a_before, c_before, _, _ = spread(k, first_block * 8 - 1)
            u1, u2, a_now, c_now, _, _ = spread(k, first_block * 8)
            lax.fori_loop(
                first_block, last_block, block, (a_before, c_before, u1, u2, a_now, c_now)
            )
            return carry

        return plane

    lax.fori_loop(0, 7, up(2, 8, 15), 0)
    lax.fori_loop(0, 8, up(3, 7, 8), 0)
    gradient_rows(0)

    def finish(pair, carry):
        parts = []
        for p in range(2):
            k = 2 * pair + p
            shown = jnp.where(
                k.astype(jnp.float32) <= refl_ref[15:33, :], col_ref[0:18, :], jnp.float32(0.0)
            )
            raw_ref[p, 0:18, :] = jnp.where(
                earth_ref[k, 7:25, :] < AIR_TEST, grad_ref[k, 0:18, :] + shown, jnp.float32(0.0)
            )
            for h in range(2):
                mid = raw_ref[p, HALF * h + 1 : HALF * h + 9, :]
                column = (raw_ref[p, HALF * h : HALF * h + 8, :] + mid) + raw_ref[
                    p, HALF * h + 2 : HALF * h + 10, :
                ]
                total = column + (pltpu.roll(column, 1, 1) + pltpu.roll(column, LANES - 1, 1))
                smooth = 0.4375 * mid + 0.0625 * total
                parts.append(rolled(smooth, STRIP * (2 * p + h - 1)))
        out_ref[pl.ds(pl.multiple_of(HALF * pair, HALF), HALF), :] = quarters(parts, lane)
        return carry

    lax.fori_loop(0, PLANES // 2, finish, 0)


def unpack_kernel(in_ref, out_ref):
    lane = lane_index()
    for c in range(2):
        tiles = [in_ref[pl.ds(HALF * (4 * c + q), HALF), :] for q in range(4)]
        for j in range(4):
            parts = [rolled(tiles[q], STRIP * (q - j)) for q in range(4)]
            out_ref[j // 2, pl.ds(HALF * (j % 2), HALF), pl.ds(LANES * c, LANES)] = quarters(
                parts, lane
            )


def in_vmem(count):
    return [pl.BlockSpec(memory_space=pltpu.VMEM)] * count


def line(count, shift):
    return [(i, i + shift) for i in range(count) if 0 <= i + shift < count]


def local(slowness, air_mask, reflector, shot_cells, receiver_mask, residual):
    depth_count = lax.axis_size("depth")
    x_count = lax.axis_size("gx")
    y_count = lax.axis_size("gy")
    nx_total = ROWS * x_count
    ny_total = STRIP * depth_count * y_count
    pos = jnp.stack(
        [lax.axis_index("depth"), lax.axis_index("gx"), lax.axis_index("gy")]
    ).astype(jnp.int32)
    smem = pl.BlockSpec(memory_space=pltpu.SMEM)
    f32 = jnp.float32

    packed, sources = pl.pallas_call(
        pack_kernel,
        out_shape=(
            jax.ShapeDtypeStruct((A_ROWS, LANES), f32),
            jax.ShapeDtypeStruct((S_ROWS, LANES), f32),
        ),
        in_specs=[smem, *in_vmem(5)],
        out_specs=tuple(in_vmem(2)),
        name="pack",
    )(pos, slowness, air_mask, reflector, receiver_mask, residual)

    strip = lax.all_to_all(
        packed.reshape(8, HALF, LANES), "depth", 0, 0, tiled=True
    ).reshape(A_ROWS, LANES)
    whole = jnp.concatenate([strip, sources], 0)
    above1 = lax.ppermute(whole, "gx", line(x_count, 1))
    below1 = lax.ppermute(whole, "gx", line(x_count, -1))
    above2 = lax.ppermute(strip, "gx", line(x_count, 2))
    below2 = lax.ppermute(strip, "gx", line(x_count, -2))
    column = jnp.concatenate([above2, above1, whole, below1, below2], 0)

    def place(q):
        return (q % depth_count) * y_count + q // depth_count

    def along(shift):
        return [(place(i), place(j)) for i, j in line(depth_count * y_count, shift)]

    left = lax.ppermute(column, ("depth", "gy"), along(1))
    right = lax.ppermute(column, ("depth", "gy"), along(-1))

    def kernel(*refs):
        sweep_kernel(*refs, nx_total=nx_total, ny_total=ny_total)

    field = (FULL, SHOTS, LANES)
    strips_out = pl.pallas_call(
        kernel,
        out_shape=jax.ShapeDtypeStruct((A_ROWS, LANES), f32),
        in_specs=[smem, *in_vmem(4)],
        out_specs=in_vmem(1)[0],
        scratch_shapes=[
            pltpu.VMEM((PLANES + 1, *field), f32),
            *[pltpu.VMEM((PLANES, FULL, LANES), f32)] * 3,
            *[pltpu.VMEM(field, f32)] * 4,
            pltpu.VMEM((PLANES, 32, SHOTS, LANES), f32),
            pltpu.VMEM(field, f32),
            pltpu.VMEM((48, SHOTS, LANES), f32),
            pltpu.VMEM((56, LANES), f32),
            pltpu.VMEM((48, SHOTS, LANES), f32),
            pltpu.VMEM((PLANES, 32, LANES), f32),
            pltpu.VMEM((PLANES, 24, LANES), f32),
            pltpu.VMEM((24, LANES), f32),
            pltpu.VMEM((2, 24, LANES), f32),
        ],
        compiler_params=pltpu.CompilerParams(vmem_limit_bytes=VMEM_BYTES),
        name="sweep",
    )(pos, shot_cells, left, column, right)

    parts = lax.all_to_all(
        strips_out.reshape(8, HALF, LANES), "depth", 0, 0, tiled=True
    ).reshape(A_ROWS, LANES)
    return pl.pallas_call(
        unpack_kernel,
        out_shape=jax.ShapeDtypeStruct(slowness.shape, f32),
        in_specs=in_vmem(1),
        out_specs=in_vmem(1)[0],
        name="unpack",
    )(parts)


def solution(mesh):
    in_specs = (
        P("depth", "gx", "gy"),
        P("depth", "gx", "gy"),
        P("gx", "gy"),
        P(),
        P(None, "gx", "gy"),
        P(None, "gx", "gy"),
    )
    out_specs = P("depth", "gx", "gy")
    return jax.shard_map(local, mesh=mesh, in_specs=in_specs, out_specs=out_specs, check_vma=False)
```

```python
import math

import jax
import jax.numpy as jnp
from jax import lax
from jax.experimental import pallas as pl
from jax.experimental.pallas import tpu as pltpu
from jax.sharding import PartitionSpec as P

SOFTMIN_TEMPER = 0.5
SURF = 0.7
AIR_SLOW = 2.5
AIR_TEST = 2.0
STEP_PENALTY = 10000.0
RATE = 1.0 / SOFTMIN_TEMPER
ROOT2 = math.sqrt(2.0)
ROOT3 = math.sqrt(3.0)

LANES = 128
STRIP = 32
ROWS = 16
PLANES = 16
SHOTS = 8
FRAME = 80
PAD = 8
FULL = FRAME + 2 * PAD
A_ROWS = 64
S_ROWS = 40
A_AT = (0, A_ROWS, 2 * A_ROWS + S_ROWS, 3 * A_ROWS + 2 * S_ROWS, 4 * A_ROWS + 3 * S_ROWS)
S_AT = (2 * A_ROWS, 3 * A_ROWS + S_ROWS, 4 * A_ROWS + 2 * S_ROWS)
GEOMETRY = 40
HALF = 8
VMEM_BYTES = 40 * 1024 * 1024


def rolled(value, shift):
    shift = shift % LANES
    return value if shift == 0 else pltpu.roll(value, shift, value.ndim - 1)


def lane_index(rows=8):
    return lax.broadcasted_iota(jnp.int32, (rows, LANES), 1)


def quarters(parts, lane):
    out = parts[0]
    for j in range(1, len(parts)):
        out = jnp.where(lane >= STRIP * j, parts[j], out)
    return out


def pack_kernel(pos, slow_ref, air_ref, refl_ref, mask_ref, resid_ref, a_ref, s_ref):
    lane = lane_index()
    speed = {}
    for p in range(2):
        for h in range(2):
            for c in range(2):
                at = (p, pl.ds(HALF * h, HALF), pl.ds(LANES * c, LANES))
                speed[p, h, c] = jnp.where(air_ref[at] == 1, jnp.float32(AIR_SLOW), slow_ref[at])
    for target in range(8):
        c, q = divmod(target, 4)
        parts = [rolled(speed[j // 2, j % 2, c], STRIP * (j - q)) for j in range(4)]
        a_ref[pl.ds(HALF * target, HALF), :] = quarters(parts, lane)
    depth_pos = pos[0]
    high = depth_pos >= 4
    back = (LANES - STRIP * (depth_pos % 4)) % LANES

    def strip(low_part, high_part):
        return pltpu.roll(jnp.where(high, high_part, low_part), back, 1)

    for v in range(4):
        parts = []
        for i in range(4):
            x = 4 * v + i
            pieces = [
                jnp.where(
                    mask_ref[:, x, pl.ds(LANES * c, LANES)] == 1,
                    resid_ref[:, x, pl.ds(LANES * c, LANES)],
                    jnp.float32(0.0),
                )
                for c in range(2)
            ]
            parts.append(rolled(strip(*pieces), STRIP * i))
        s_ref[pl.ds(HALF * v, HALF), :] = quarters(parts, lane)
    parts = []
    for h in range(2):
        pieces = [
            refl_ref[pl.ds(HALF * h, HALF), pl.ds(LANES * c, LANES)].astype(jnp.float32)
            for c in range(2)
        ]
        parts.append(rolled(strip(*pieces), STRIP * h))
    s_ref[pl.ds(32, HALF), :] = quarters(parts, lane)


def sweep_kernel(
    pos,
    shot_ref,
    left_ref,
    here_ref,
    right_ref,
    out_ref,
    wa_ref,
    wb_ref,
    e1_ref,
    e2_ref,
    e3_ref,
    gm_ref,
    gp_ref,
    hm_ref,
    hp_ref,
    head_ref,
    ma_ref,
    mb_ref,
    src_ref,
    refl_ref,
    wsel_ref,
    earth_ref,
    grad_ref,
    col_ref,
    raw_ref,
    nx_total,
    ny_total,
):
    lane = lane_index()
    sub = lax.broadcasted_iota(jnp.int32, (8, LANES), 0)
    x_base = pos[1] * ROWS - 2 * ROWS
    y_base = pos[2] * (8 * STRIP) + pos[0] * STRIP - STRIP
    y_cell = y_base + lane
    y_inside = (y_cell >= 0) & (y_cell < ny_total)
    zero = jnp.zeros((8, LANES), jnp.float32)

    def row_of(ref, lead, r):
        if lead is None:
            return ref[pl.ds(r, 8, stride=0), :]
        return ref[lead, pl.ds(r, 8, stride=0), :]

    def rim_factor(x_cell):
        inside = (x_cell >= 0) & (x_cell < nx_total) & y_inside
        penalty = jnp.where(inside, jnp.float32(0.0), jnp.float32(STEP_PENALTY))
        return jnp.exp(-penalty * RATE)

    shot_x = jnp.broadcast_to(shot_ref[:, 0:1].astype(jnp.float32), (8, LANES))
    shot_y = jnp.broadcast_to(shot_ref[:, 1:2].astype(jnp.float32), (8, LANES))
    y_square = (y_cell.astype(jnp.float32) - shot_y) ** 2

    def surface(r):
        x_cell = (x_base + r).astype(jnp.float32)
        return SURF * jnp.sqrt((x_cell - shot_x) ** 2 + y_square)

    def weight(diff):
        return jnp.exp(-diff * RATE)

    def near(diff):
        return jnp.clip(diff, -1.0, 1.0)

    def geometry(block, carry):
        before, now = carry
        for i in range(GEOMETRY):
            r = block * GEOMETRY + i
            after = surface(r + 1)
            gm_ref[r + PAD] = weight(near(pltpu.roll(now, 1, 1) - now))
            gp_ref[r + PAD] = weight(near(pltpu.roll(now, LANES - 1, 1) - now))
            hm_ref[r + PAD] = weight(before - now)
            hp_ref[r + PAD] = weight(after - now)
            wa_ref[r + PAD] = rim_factor(x_base + r)
            before, now = now, after
        return before, now

    lax.fori_loop(0, FRAME // GEOMETRY, geometry, (surface(-1), surface(0)))
    for ref in (gm_ref, gp_ref, hm_ref, hp_ref):
        ref[PAD - 1] = zero
        ref[PAD + FRAME] = zero
    for ref in (wa_ref, wb_ref):
        ref[PAD - 1] = zero
        ref[PAD + FRAME] = zero

    def merged(tiles, j):
        part = tiles[0]
        one, two = (j + 1) % 4, (j + 2) % 4
        part = jnp.where((lane >= STRIP * one) & (lane < STRIP * (one + 1)), tiles[1], part)
        part = jnp.where((lane >= STRIP * two) & (lane < STRIP * (two + 1)), tiles[2], part)
        return rolled(part, -STRIP * j)

    def strips(row):
        at = (pl.ds(row, HALF), slice(None))
        return left_ref[at], rolled(here_ref[at], STRIP), rolled(right_ref[at], 2 * STRIP)

    rims = [rim_factor(x_base + HALF * g + sub) for g in range(FRAME // HALF)]

    def exponents(pair, carry):
        for offset in range(5):
            tiles = strips(pl.multiple_of(A_AT[offset] + HALF * pair, HALF))
            for j in range(4):
                p, h = divmod(j, 2)
                group = 2 * offset + h
                speed = merged(tiles, j)
                at = (2 * pair + p, pl.ds(HALF * group, HALF), slice(None))
                e1_ref[at] = jnp.exp(-speed * RATE) * rims[group]
                e2_ref[at] = jnp.exp(-(speed * ROOT2) * RATE) * rims[group]
                e3_ref[at] = jnp.exp(-(speed * ROOT3) * RATE) * rims[group]
                if 3 <= group < 7:
                    here = (2 * pair + p, pl.ds(HALF * (group - 3), HALF), slice(None))
                    earth_ref[here] = speed
        return carry

    lax.fori_loop(0, PLANES // 2, exponents, 0)

    for offset in range(3):
        for v in range(4):
            tiles = strips(S_AT[offset] + HALF * v)
            for i in range(4):
                src_ref[ROWS * offset + 4 * v + i] = merged(tiles, i)
        tiles = strips(S_AT[offset] + 32)
        for h in range(2):
            inside = rims[2 + 2 * offset + h] > 0.5
            refl_ref[pl.ds(ROWS * offset + HALF * h, HALF), :] = jnp.where(
                inside, merged(tiles, h), jnp.float32(-1.0)
            )

    for r in range(48):
        wsel_ref[r] = zero + 1.0

    def along_y(value, r):
        return (
            gm_ref[r + PAD] * pltpu.roll(value, 1, 1)
            + gp_ref[r + PAD] * pltpu.roll(value, LANES - 1, 1)
        )

    def down_plane(k, w_ref, next_ref, first, last, select):
        level = k.astype(jnp.float32)
        w_before, w_now = w_ref[first - 1 + PAD], w_ref[first + PAD]
        q_before, q_now = along_y(w_before, first - 1), along_y(w_now, first)
        for r in range(first, last):
            w_after = w_ref[r + 1 + PAD]
            q_after = along_y(w_after, r + 1)
            hm = hm_ref[r + PAD]
            hp = hp_ref[r + PAD]
            edge = q_now + (hm * w_before + hp * w_after)
            corner = hm * q_before + hp * q_after
            part1 = row_of(e1_ref, k, r) * w_now
            part2 = row_of(e2_ref, k, r) * edge
            part3 = row_of(e3_ref, k, r) * corner
            w_next = part1 + part2 + part3
            next_ref[r + PAD] = w_next
            if 31 <= r < 49:
                head_ref[k, r - 31] = part1 + ROOT2 * part2 + ROOT3 * part3
            if select and 16 <= r < 64:
                hit = row_of(refl_ref, None, r - 16) == level
                wsel_ref[r - 16] = jnp.where(hit, w_next, wsel_ref[r - 16])
            w_before, q_before, w_now, q_now = w_now, q_now, w_after, q_after

    def down(first, last, select):
        def two(i, carry):
            down_plane(2 * i, wa_ref, wb_ref, first, last, select)
            down_plane(2 * i + 1, wb_ref, wa_ref, first, last, select)
            return carry

        return two

    lax.fori_loop(0, 2, down(1, 79, False), 0)
    lax.fori_loop(2, 4, down(5, 75, True), 0)
    lax.fori_loop(4, 8, down(9, 71, True), 0)

    for ref in (ma_ref, mb_ref):
        ref[15 + PAD] = zero
        ref[64 + PAD] = zero

    for r in range(48):
        share = src_ref[r] / wsel_ref[r]
        wsel_ref[r] = share
        hit = row_of(refl_ref, None, r) == float(PLANES - 1)
        ma_ref[r + 16 + PAD] = jnp.where(hit, share, jnp.float32(0.0))
    for i in range(18):
        col_ref[i : i + 1, :] = jnp.sum(src_ref[15 + i], axis=0, keepdims=True)

    def gradient_rows(k, mu_ref):
        for i in range(18):
            product = mu_ref[31 + i + PAD] * head_ref[k, i]
            grad_ref[k, i : i + 1, :] = jnp.sum(product, axis=0, keepdims=True)

    def up(k, mu_ref, next_ref, first, last):
        gradient_rows(k, mu_ref)
        level = (k - 1).astype(jnp.float32)

        def spread(r):
            mu = mu_ref[r + PAD]
            u2 = row_of(e2_ref, k, r) * mu
            u3 = row_of(e3_ref, k, r) * mu
            hm = hm_ref[r + PAD]
            hp = hp_ref[r + PAD]
            return row_of(e1_ref, k, r) * mu, u2, hp * u2, hp * u3, hm * u2, hm * u3

        _, _, a_before, c_before, _, _ = spread(first - 1)
        u1, u2, a_now, c_now, _, _ = spread(first)
        for r in range(first, last):
            n1, n2, a_next, c_next, a_back, c_back = spread(r + 1)
            both = u2 + (c_before + c_back)
            side = pltpu.roll(gp_ref[r + PAD] * both, 1, 1) + pltpu.roll(
                gm_ref[r + PAD] * both, LANES - 1, 1
            )
            hit = row_of(refl_ref, None, r - 16) == level
            own = jnp.where(hit, wsel_ref[r - 16], jnp.float32(0.0))
            next_ref[r + PAD] = (u1 + own) + (a_before + a_back) + side
            a_before, c_before, u1, u2, a_now, c_now = a_now, c_now, n1, n2, a_next, c_next

    def up_two(top, first, last):
        def two(step, carry):
            k = top - 2 * step
            up(k, ma_ref, mb_ref, first, last)
            up(k - 1, mb_ref, ma_ref, first, last)
            return carry

        return two

    lax.fori_loop(0, 2, up_two(15, 17, 63), 0)
    lax.fori_loop(0, 2, up_two(11, 21, 59), 0)
    lax.fori_loop(0, 2, up_two(7, 25, 55), 0)
    up_two(3, 29, 51)(jnp.int32(0), 0)
    up(jnp.int32(1), ma_ref, mb_ref, 31, 49)
    gradient_rows(0, mb_ref)

    for pair in range(PLANES // 2):
        parts = []
        for p in range(2):
            k = 2 * pair + p
            shown = jnp.where(
                float(k) <= refl_ref[15:33, :], col_ref[0:18, :], jnp.float32(0.0)
            )
            raw_ref[k, 0:18, :] = jnp.where(
                earth_ref[k, 7:25, :] < AIR_TEST, grad_ref[k, 0:18, :] + shown, jnp.float32(0.0)
            )
            for h in range(2):
                mid = raw_ref[k, HALF * h + 1 : HALF * h + 9, :]
                column = (raw_ref[k, HALF * h : HALF * h + 8, :] + mid) + raw_ref[
                    k, HALF * h + 2 : HALF * h + 10, :
                ]
                total = column + (pltpu.roll(column, 1, 1) + pltpu.roll(column, LANES - 1, 1))
                smooth = 0.4375 * mid + 0.0625 * total
                parts.append(rolled(smooth, STRIP * (2 * p + h - 1)))
        out_ref[pl.ds(HALF * pair, HALF), :] = quarters(parts, lane)


def unpack_kernel(in_ref, out_ref):
    lane = lane_index()
    for c in range(2):
        tiles = [in_ref[pl.ds(HALF * (4 * c + q), HALF), :] for q in range(4)]
        for j in range(4):
            parts = [rolled(tiles[q], STRIP * (q - j)) for q in range(4)]
            out_ref[j // 2, pl.ds(HALF * (j % 2), HALF), pl.ds(LANES * c, LANES)] = quarters(
                parts, lane
            )


def in_vmem(count):
    return [pl.BlockSpec(memory_space=pltpu.VMEM)] * count


def line(count, shift):
    return [(i, i + shift) for i in range(count) if 0 <= i + shift < count]


def sweep_call(pos, shot_cells, left, column, right, nx_total, ny_total):
    def kernel(*refs):
        sweep_kernel(*refs, nx_total=nx_total, ny_total=ny_total)

    field = (FULL, SHOTS, LANES)
    return pl.pallas_call(
        kernel,
        out_shape=jax.ShapeDtypeStruct((A_ROWS, LANES), jnp.float32),
        in_specs=[pl.BlockSpec(memory_space=pltpu.SMEM), *in_vmem(4)],
        out_specs=in_vmem(1)[0],
        scratch_shapes=[
            *[pltpu.VMEM(field, jnp.float32)] * 2,
            *[pltpu.VMEM((PLANES, FULL, LANES), jnp.float32)] * 3,
            *[pltpu.VMEM(field, jnp.float32)] * 4,
            pltpu.VMEM((PLANES, 18, SHOTS, LANES), jnp.float32),
            *[pltpu.VMEM(field, jnp.float32)] * 2,
            pltpu.VMEM((48, SHOTS, LANES), jnp.float32),
            pltpu.VMEM((56, LANES), jnp.float32),
            pltpu.VMEM((48, SHOTS, LANES), jnp.float32),
            pltpu.VMEM((PLANES, 32, LANES), jnp.float32),
            pltpu.VMEM((PLANES, 24, LANES), jnp.float32),
            pltpu.VMEM((24, LANES), jnp.float32),
            pltpu.VMEM((PLANES, 24, LANES), jnp.float32),
        ],
        compiler_params=pltpu.CompilerParams(vmem_limit_bytes=VMEM_BYTES),
        name="sweep",
    )(pos, shot_cells, left, column, right)


def local(slowness, air_mask, reflector, shot_cells, receiver_mask, residual):
    depth_count = lax.axis_size("depth")
    x_count = lax.axis_size("gx")
    y_count = lax.axis_size("gy")
    nx_total = ROWS * x_count
    ny_total = STRIP * depth_count * y_count
    pos = jnp.stack(
        [lax.axis_index("depth"), lax.axis_index("gx"), lax.axis_index("gy")]
    ).astype(jnp.int32)
    smem = pl.BlockSpec(memory_space=pltpu.SMEM)
    f32 = jnp.float32

    packed, sources = pl.pallas_call(
        pack_kernel,
        out_shape=(
            jax.ShapeDtypeStruct((A_ROWS, LANES), f32),
            jax.ShapeDtypeStruct((S_ROWS, LANES), f32),
        ),
        in_specs=[smem, *in_vmem(5)],
        out_specs=tuple(in_vmem(2)),
        name="pack",
    )(pos, slowness, air_mask, reflector, receiver_mask, residual)

    strip = lax.all_to_all(
        packed.reshape(8, HALF, LANES), "depth", 0, 0, tiled=True
    ).reshape(A_ROWS, LANES)
    whole = jnp.concatenate([strip, sources], 0)
    above1 = lax.ppermute(whole, "gx", line(x_count, 1))
    below1 = lax.ppermute(whole, "gx", line(x_count, -1))
    above2 = lax.ppermute(strip, "gx", line(x_count, 2))
    below2 = lax.ppermute(strip, "gx", line(x_count, -2))
    column = jnp.concatenate([above2, above1, whole, below1, below2], 0)

    def place(q):
        return (q % depth_count) * y_count + q // depth_count

    def along(shift):
        return [(place(i), place(j)) for i, j in line(depth_count * y_count, shift)]

    left = lax.ppermute(column, ("depth", "gy"), along(1))
    right = lax.ppermute(column, ("depth", "gy"), along(-1))

    strips_out = sweep_call(pos, shot_cells, left, column, right, nx_total, ny_total)
    parts = lax.all_to_all(
        strips_out.reshape(8, HALF, LANES), "depth", 0, 0, tiled=True
    ).reshape(A_ROWS, LANES)
    return pl.pallas_call(
        unpack_kernel,
        out_shape=jax.ShapeDtypeStruct(slowness.shape, f32),
        in_specs=in_vmem(1),
        out_specs=in_vmem(1)[0],
        name="unpack",
    )(parts)


def solution(mesh):
    in_specs = (
        P("depth", "gx", "gy"),
        P("depth", "gx", "gy"),
        P("gx", "gy"),
        P(),
        P(None, "gx", "gy"),
        P(None, "gx", "gy"),
    )
    out_specs = P("depth", "gx", "gy")
    return jax.shard_map(local, mesh=mesh, in_specs=in_specs, out_specs=out_specs, check_vma=False)
```

```python
import math

import jax
import jax.numpy as jnp
from jax import lax
from jax.experimental import pallas as pl
from jax.experimental.pallas import tpu as pltpu
from jax.sharding import PartitionSpec as P

SOFTMIN_TEMPER = 0.5
SURF = 0.7
AIR_SLOW = 2.5
AIR_TEST = 2.0
STEP_PENALTY = 10000.0
RATE = 1.0 / SOFTMIN_TEMPER
ROOT2 = math.sqrt(2.0)
ROOT3 = math.sqrt(3.0)

LANES = 128
STRIP = 32
ROWS = 16
PLANES = 16
SHOTS = 8
FRAME = 80
PAD = 8
FULL = FRAME + 2 * PAD
A_ROWS = 64
S_ROWS = 40
A_AT = (0, A_ROWS, 2 * A_ROWS + S_ROWS, 3 * A_ROWS + 2 * S_ROWS, 4 * A_ROWS + 3 * S_ROWS)
S_AT = (2 * A_ROWS, 3 * A_ROWS + S_ROWS, 4 * A_ROWS + 2 * S_ROWS)
MIDDLE = 40
HALF = 8
VMEM_BYTES = 40 * 1024 * 1024


def position(axis):
    return lax.axis_index(axis)


def rolled(value, shift):
    shift = shift % LANES
    return value if shift == 0 else pltpu.roll(value, shift, value.ndim - 1)


def lane_index(rows=8):
    return lax.broadcasted_iota(jnp.int32, (rows, LANES), 1)


def quarters(parts, lane):
    out = parts[0]
    for j in range(1, len(parts)):
        out = jnp.where(lane >= STRIP * j, parts[j], out)
    return out


def pack_kernel(slow_ref, air_ref, refl_ref, mask_ref, resid_ref, a_ref, s_ref):
    lane = lane_index()
    speed = {}
    for p in range(2):
        for h in range(2):
            for c in range(2):
                at = (p, pl.ds(HALF * h, HALF), pl.ds(LANES * c, LANES))
                speed[p, h, c] = jnp.where(air_ref[at] == 1, jnp.float32(AIR_SLOW), slow_ref[at])
    for target in range(8):
        c, q = divmod(target, 4)
        parts = [rolled(speed[j // 2, j % 2, c], STRIP * (j - q)) for j in range(4)]
        a_ref[pl.ds(HALF * target, HALF), :] = quarters(parts, lane)
    depth_pos = position("depth")
    high = depth_pos >= 4
    back = (LANES - STRIP * (depth_pos % 4)) % LANES

    def strip(low_part, high_part):
        return pltpu.roll(jnp.where(high, high_part, low_part), back, 1)

    for v in range(4):
        parts = []
        for i in range(4):
            x = 4 * v + i
            pieces = [
                jnp.where(
                    mask_ref[:, x, pl.ds(LANES * c, LANES)] == 1,
                    resid_ref[:, x, pl.ds(LANES * c, LANES)],
                    jnp.float32(0.0),
                )
                for c in range(2)
            ]
            parts.append(rolled(strip(*pieces), STRIP * i))
        s_ref[pl.ds(HALF * v, HALF), :] = quarters(parts, lane)
    parts = []
    for h in range(2):
        pieces = [
            refl_ref[pl.ds(HALF * h, HALF), pl.ds(LANES * c, LANES)].astype(jnp.float32)
            for c in range(2)
        ]
        parts.append(rolled(strip(*pieces), STRIP * h))
    s_ref[pl.ds(32, HALF), :] = quarters(parts, lane)


def sweep_kernel(
    shot_ref,
    near_ref,
    here_ref,
    far_ref,
    out_ref,
    wa_ref,
    wb_ref,
    e1_ref,
    e2_ref,
    e3_ref,
    head_ref,
    ma_ref,
    mb_ref,
    src_ref,
    refl_ref,
    wsel_ref,
    earth_ref,
    grad_ref,
    col_ref,
    raw_ref,
    nx_total,
    ny_total,
):
    lane = lane_index()
    sub = lax.broadcasted_iota(jnp.int32, (8, LANES), 0)
    depth_pos = position("depth")
    x_base = position("gx") * ROWS - 2 * ROWS
    y_base = position("gy") * (8 * STRIP) + depth_pos * STRIP - STRIP
    odd = depth_pos % 2 == 1
    y_cell = y_base + lane
    y_inside = (y_cell >= 0) & (y_cell < ny_total)
    zero = jnp.zeros((8, LANES), jnp.float32)

    def row_of(ref, lead, r):
        if lead is None:
            return ref[pl.ds(r, 8, stride=0), :]
        return ref[lead, pl.ds(r, 8, stride=0), :]

    def rim_factor(x_cell):
        inside = (x_cell >= 0) & (x_cell < nx_total) & y_inside
        penalty = jnp.where(inside, jnp.float32(0.0), jnp.float32(STEP_PENALTY))
        return jnp.exp(-penalty * RATE)

    shot_x = jnp.broadcast_to(shot_ref[:, 0:1].astype(jnp.float32), (8, LANES))
    shot_y = jnp.broadcast_to(shot_ref[:, 1:2].astype(jnp.float32), (8, LANES))
    y_square = (y_cell.astype(jnp.float32) - shot_y) ** 2

    def surface(r):
        x_cell = (x_base + r).astype(jnp.float32)
        return SURF * jnp.sqrt((x_cell - shot_x) ** 2 + y_square)

    def weight(diff):
        return jnp.exp(-diff * RATE)

    def near(diff):
        return jnp.clip(diff, -1.0, 1.0)

    middle = surface(MIDDLE)
    weight_minus = weight(near(pltpu.roll(middle, 1, 1) - middle))
    weight_plus = weight(near(pltpu.roll(middle, LANES - 1, 1) - middle))
    for r in range(FRAME):
        wa_ref[r + PAD] = weight(surface(r) - middle) * rim_factor(x_base + r)
    for ref in (wa_ref, wb_ref):
        ref[PAD - 1] = zero
        ref[PAD + FRAME] = zero

    def merged(tiles, j):
        part = tiles[0]
        one, two = (j + 1) % 4, (j + 2) % 4
        part = jnp.where((lane >= STRIP * one) & (lane < STRIP * (one + 1)), tiles[1], part)
        part = jnp.where((lane >= STRIP * two) & (lane < STRIP * (two + 1)), tiles[2], part)
        return rolled(part, -STRIP * j)

    def strips(row):
        at = (pl.ds(row, HALF), slice(None))
        one, two = near_ref[at], far_ref[at]
        left = jnp.where(odd, one, two)
        right = jnp.where(odd, two, one)
        return left, rolled(here_ref[at], STRIP), rolled(right, 2 * STRIP)

    rims = [rim_factor(x_base + HALF * g + sub) for g in range(FRAME // HALF)]

    for pair in range(PLANES // 2):
        for offset in range(5):
            tiles = strips(A_AT[offset] + HALF * pair)
            for j in range(4):
                p, h = divmod(j, 2)
                group = 2 * offset + h
                if pair >= 4 and group in (0, 9):
                    continue
                speed = merged(tiles, j)
                at = (2 * pair + p, pl.ds(HALF * group, HALF), slice(None))
                e1_ref[at] = jnp.exp(-speed * RATE) * rims[group]
                e2_ref[at] = jnp.exp(-(speed * ROOT2) * RATE) * rims[group]
                e3_ref[at] = jnp.exp(-(speed * ROOT3) * RATE) * rims[group]
                if 3 <= group < 7:
                    here = (2 * pair + p, pl.ds(HALF * (group - 3), HALF), slice(None))
                    earth_ref[here] = speed

    for offset in range(3):
        for v in range(4):
            tiles = strips(S_AT[offset] + HALF * v)
            for i in range(4):
                src_ref[ROWS * offset + 4 * v + i] = merged(tiles, i)
        tiles = strips(S_AT[offset] + 32)
        for h in range(2):
            inside = rims[2 + 2 * offset + h] > 0.5
            refl_ref[pl.ds(ROWS * offset + HALF * h, HALF), :] = jnp.where(
                inside, merged(tiles, h), jnp.float32(-1.0)
            )

    for r in range(48):
        wsel_ref[r] = zero + 1.0

    def along_y(value):
        return weight_minus * pltpu.roll(value, 1, 1) + weight_plus * pltpu.roll(
            value, LANES - 1, 1
        )

    def down_plane(k, w_ref, next_ref, first, last, select):
        level = k.astype(jnp.float32)
        w_before, w_now = w_ref[first - 1 + PAD], w_ref[first + PAD]
        q_before, q_now = along_y(w_before), along_y(w_now)
        for r in range(first, last):
            w_after = w_ref[r + 1 + PAD]
            q_after = along_y(w_after)
            part1 = row_of(e1_ref, k, r) * w_now
            part2 = row_of(e2_ref, k, r) * (q_now + (w_before + w_after))
            part3 = row_of(e3_ref, k, r) * (q_before + q_after)
            w_next = part1 + part2 + part3
            next_ref[r + PAD] = w_next
            if 31 <= r < 49:
                head_ref[k, r - 31] = part1 + ROOT2 * part2 + ROOT3 * part3
            if select and 16 <= r < 64:
                hit = row_of(refl_ref, None, r - 16) == level
                wsel_ref[r - 16] = jnp.where(hit, w_next, wsel_ref[r - 16])
            w_before, q_before, w_now, q_now = w_now, q_now, w_after, q_after

    def down(first, last, select):
        def two(i, carry):
            down_plane(2 * i, wa_ref, wb_ref, first, last, select)
            down_plane(2 * i + 1, wb_ref, wa_ref, first, last, select)
            return carry

        return two

    lax.fori_loop(0, 2, down(1, 79, False), 0)
    lax.fori_loop(2, 4, down(5, 75, True), 0)
    lax.fori_loop(4, 6, down(9, 71, True), 0)
    lax.fori_loop(6, 8, down(13, 67, True), 0)

    for ref in (ma_ref, mb_ref):
        ref[15 + PAD] = zero
        ref[64 + PAD] = zero

    for r in range(48):
        share = src_ref[r] / wsel_ref[r]
        wsel_ref[r] = share
        hit = row_of(refl_ref, None, r) == float(PLANES - 1)
        ma_ref[r + 16 + PAD] = jnp.where(hit, share, jnp.float32(0.0))
    for i in range(18):
        col_ref[i : i + 1, :] = jnp.sum(src_ref[15 + i], axis=0, keepdims=True)

    def gradient_rows(k, mu_ref):
        for i in range(18):
            product = mu_ref[31 + i + PAD] * head_ref[k, i]
            grad_ref[k, i : i + 1, :] = jnp.sum(product, axis=0, keepdims=True)

    def up(k, mu_ref, next_ref, first, last):
        gradient_rows(k, mu_ref)
        level = (k - 1).astype(jnp.float32)

        def spread(r):
            mu = mu_ref[r + PAD]
            return row_of(e1_ref, k, r) * mu, row_of(e2_ref, k, r) * mu, row_of(e3_ref, k, r) * mu

        _, u2_before, u3_before = spread(first - 1)
        u1, u2, u3 = spread(first)
        for r in range(first, last):
            n1, n2, n3 = spread(r + 1)
            both = u2 + (u3_before + n3)
            side = pltpu.roll(weight_plus * both, 1, 1) + pltpu.roll(
                weight_minus * both, LANES - 1, 1
            )
            hit = row_of(refl_ref, None, r - 16) == level
            own = jnp.where(hit, wsel_ref[r - 16], jnp.float32(0.0))
            next_ref[r + PAD] = (u1 + own) + (u2_before + n2) + side
            u2_before, u3_before, u1, u2, u3 = u2, u3, n1, n2, n3

    def up_two(top, first, last):
        def two(step, carry):
            k = top - 2 * step
            up(k, ma_ref, mb_ref, first, last)
            up(k - 1, mb_ref, ma_ref, first, last)
            return carry

        return two

    lax.fori_loop(0, 2, up_two(15, 17, 63), 0)
    lax.fori_loop(0, 2, up_two(11, 21, 59), 0)
    lax.fori_loop(0, 2, up_two(7, 25, 55), 0)
    up_two(3, 29, 51)(jnp.int32(0), 0)
    up(jnp.int32(1), ma_ref, mb_ref, 31, 49)
    gradient_rows(0, mb_ref)

    for pair in range(PLANES // 2):
        parts = []
        for p in range(2):
            k = 2 * pair + p
            shown = jnp.where(
                float(k) <= refl_ref[15:33, :], col_ref[0:18, :], jnp.float32(0.0)
            )
            raw_ref[k, 0:18, :] = jnp.where(
                earth_ref[k, 7:25, :] < AIR_TEST, grad_ref[k, 0:18, :] + shown, jnp.float32(0.0)
            )
            for h in range(2):
                mid = raw_ref[k, HALF * h + 1 : HALF * h + 9, :]
                column = (raw_ref[k, HALF * h : HALF * h + 8, :] + mid) + raw_ref[
                    k, HALF * h + 2 : HALF * h + 10, :
                ]
                total = column + (pltpu.roll(column, 1, 1) + pltpu.roll(column, LANES - 1, 1))
                smooth = 0.4375 * mid + 0.0625 * total
                parts.append(rolled(smooth, STRIP * (2 * p + h - 1)))
        out_ref[pl.ds(HALF * pair, HALF), :] = quarters(parts, lane)


def unpack_kernel(in_ref, out_ref):
    lane = lane_index()
    for c in range(2):
        tiles = [in_ref[pl.ds(HALF * (4 * c + q), HALF), :] for q in range(4)]
        for j in range(4):
            parts = [rolled(tiles[q], STRIP * (q - j)) for q in range(4)]
            out_ref[j // 2, pl.ds(HALF * (j % 2), HALF), pl.ds(LANES * c, LANES)] = quarters(
                parts, lane
            )


def in_vmem(count):
    return [pl.BlockSpec(memory_space=pltpu.VMEM)] * count


def line(count, shift):
    return [(i, i + shift) for i in range(count) if 0 <= i + shift < count]


def sweep_call(shot_cells, near, column, far, nx_total, ny_total):
    def kernel(*refs):
        sweep_kernel(*refs, nx_total=nx_total, ny_total=ny_total)

    field = (FULL, SHOTS, LANES)
    return pl.pallas_call(
        kernel,
        out_shape=jax.ShapeDtypeStruct((A_ROWS, LANES), jnp.float32),
        in_specs=in_vmem(4),
        out_specs=in_vmem(1)[0],
        scratch_shapes=[
            *[pltpu.VMEM(field, jnp.float32)] * 2,
            *[pltpu.VMEM((PLANES, FULL, LANES), jnp.float32)] * 3,
            pltpu.VMEM((PLANES, 18, SHOTS, LANES), jnp.float32),
            *[pltpu.VMEM(field, jnp.float32)] * 2,
            pltpu.VMEM((48, SHOTS, LANES), jnp.float32),
            pltpu.VMEM((56, LANES), jnp.float32),
            pltpu.VMEM((48, SHOTS, LANES), jnp.float32),
            pltpu.VMEM((PLANES, 32, LANES), jnp.float32),
            pltpu.VMEM((PLANES, 24, LANES), jnp.float32),
            pltpu.VMEM((24, LANES), jnp.float32),
            pltpu.VMEM((PLANES, 24, LANES), jnp.float32),
        ],
        compiler_params=pltpu.CompilerParams(vmem_limit_bytes=VMEM_BYTES),
        name="sweep",
    )(shot_cells, near, column, far)


def local(slowness, air_mask, reflector, shot_cells, receiver_mask, residual):
    depth_count = lax.axis_size("depth")
    x_count = lax.axis_size("gx")
    y_count = lax.axis_size("gy")
    nx_total = ROWS * x_count
    ny_total = STRIP * depth_count * y_count
    f32 = jnp.float32

    packed, sources = pl.pallas_call(
        pack_kernel,
        out_shape=(
            jax.ShapeDtypeStruct((A_ROWS, LANES), f32),
            jax.ShapeDtypeStruct((S_ROWS, LANES), f32),
        ),
        in_specs=in_vmem(5),
        out_specs=tuple(in_vmem(2)),
        name="pack",
    )(slowness, air_mask, reflector, receiver_mask, residual)

    strip = lax.all_to_all(
        packed.reshape(8, HALF, LANES), "depth", 0, 0, tiled=True
    ).reshape(A_ROWS, LANES)
    whole = jnp.concatenate([strip, sources], 0)
    above1 = lax.ppermute(whole, "gx", line(x_count, 1))
    below1 = lax.ppermute(whole, "gx", line(x_count, -1))
    above2 = lax.ppermute(strip, "gx", line(x_count, 2))
    below2 = lax.ppermute(strip, "gx", line(x_count, -2))
    column = jnp.concatenate([above2, above1, whole, below1, below2], 0)

    def place(q):
        return (q % depth_count) * y_count + q // depth_count

    def swapped(first):
        pairs = [(q, q + 1) for q in range(first, depth_count * y_count - 1, 2)]
        return [(place(i), place(j)) for a, b in pairs for i, j in ((a, b), (b, a))]

    near = lax.ppermute(column, ("depth", "gy"), swapped(0))
    far = lax.ppermute(column, ("depth", "gy"), swapped(1))

    strips_out = sweep_call(shot_cells, near, column, far, nx_total, ny_total)
    parts = lax.all_to_all(
        strips_out.reshape(8, HALF, LANES), "depth", 0, 0, tiled=True
    ).reshape(A_ROWS, LANES)
    return pl.pallas_call(
        unpack_kernel,
        out_shape=jax.ShapeDtypeStruct(slowness.shape, f32),
        in_specs=in_vmem(1),
        out_specs=in_vmem(1)[0],
        name="unpack",
    )(parts)


def solution(mesh):
    in_specs = (
        P("depth", "gx", "gy"),
        P("depth", "gx", "gy"),
        P("gx", "gy"),
        P(),
        P(None, "gx", "gy"),
        P(None, "gx", "gy"),
    )
    out_specs = P("depth", "gx", "gy")
    return jax.shard_map(local, mesh=mesh, in_specs=in_specs, out_specs=out_specs, check_vma=False)
```

```python
import math

import jax
import jax.numpy as jnp
from jax import lax
from jax.experimental import pallas as pl
from jax.experimental.pallas import tpu as pltpu
from jax.sharding import PartitionSpec as P

SOFTMIN_TEMPER = 0.5
SURF = 0.7
AIR_SLOW = 2.5
AIR_TEST = 2.0
STEP_PENALTY = 10000.0
RATE = 1.0 / SOFTMIN_TEMPER
ROOT2 = math.sqrt(2.0)
ROOT3 = math.sqrt(3.0)

LANES = 128
STRIP = 32
ROWS = 16
PLANES = 16
SHOTS = 8
FRAME = 80
PAD = 8
FULL = FRAME + 2 * PAD
TILE = 64
A_AT = (0, 32, 96, 160, 224)
SHARED_AT = 256
S_AT = (288, 328, 368)
COLUMN = 408
MIDDLE = 40
HALF = 8
SWEEP_VMEM = 16 * 1024 * 1024
SMALL_VMEM = 4 * 1024 * 1024


def position(axis):
    return lax.axis_index(axis)


def rolled(value, shift):
    shift = shift % LANES
    return value if shift == 0 else pltpu.roll(value, shift, value.ndim - 1)


def lane_index(rows=8):
    return lax.broadcasted_iota(jnp.int32, (rows, LANES), 1)


def quarters(parts, lane):
    out = parts[0]
    for j in range(1, len(parts)):
        out = jnp.where(lane >= STRIP * j, parts[j], out)
    return out


def pack_kernel(
    slow_ref, air_ref, refl_ref, mask_ref, resid_ref, out_ref, live_ref, level_ref
):
    lane = lane_index()
    sub = lax.broadcasted_iota(jnp.int32, (8, LANES), 0)
    first = 2 * position("depth")
    speed = {}
    for p in range(2):
        for h in range(2):
            for c in range(2):
                at = (p, pl.ds(HALF * h, HALF), pl.ds(LANES * c, LANES))
                speed[p, h, c] = jnp.where(air_ref[at] == 1, jnp.float32(AIR_SLOW), slow_ref[at])
    for h in range(2):
        for c in range(2):
            here = pl.ds(HALF * h, HALF)
            at = (here, pl.ds(LANES * c, LANES))
            level_ref[c, here, :] = refl_ref[at].astype(jnp.float32)
            for shot in range(SHOTS):
                live_ref[c, shot, here, :] = jnp.where(
                    mask_ref[shot, *at] == 1, resid_ref[shot, *at], jnp.float32(0.0)
                )
    rows = {}
    for i in range(2):
        for c in range(2):
            at = (pl.ds(first + i, 8, stride=0), slice(None))
            rows[2 + i, c] = level_ref[c, *at]
            row = live_ref[c, 0, *at]
            for shot in range(1, SHOTS):
                row = jnp.where(sub >= shot, live_ref[c, shot, *at], row)
            rows[i, c] = row
    for target in range(8):
        c, q = divmod(target, 4)
        planes = quarters(
            [rolled(speed[j // 2, j % 2, c], STRIP * (j - q)) for j in range(4)], lane
        )
        sources = quarters([rolled(rows[j, c], STRIP * (j - q)) for j in range(4)], lane)
        for member in range(2):
            at = 2 * HALF * (2 * target + member)
            out_ref[pl.ds(at, HALF), :] = planes
            out_ref[pl.ds(at + HALF, HALF), :] = sources


def arrange_kernel(above_ref, own_ref, below_ref, out_ref):
    lane = lane_index()
    sub = lax.broadcasted_iota(jnp.int32, (8, LANES), 0)
    second = position("gx") % 2 == 1
    speeds = [(ref, i) for ref in (above_ref, own_ref, below_ref) for i in range(2)]
    sources = [(above_ref, 2), (own_ref, 2), (own_ref, 3), (below_ref, 2)]

    def picked(choices, i, part):
        at = pl.ds(HALF * part, HALF)
        (ref0, tile0), (ref1, tile1) = choices[i], choices[i + 1]
        return jnp.where(second, ref1[tile1, at, :], ref0[tile0, at, :])

    for offset in range(5):
        for part in range(4 if offset in (0, 4) else 8):
            out_ref[pl.ds(A_AT[offset] + HALF * part, HALF), :] = picked(speeds, offset, part)
    lower = (lane // STRIP) % 2 == 1
    for part in range(4, 8):
        out_ref[pl.ds(SHARED_AT + HALF * (part - 4), HALF), :] = jnp.where(
            lower, picked(speeds, 0, part), picked(speeds, 4, part)
        )
    for offset in range(3):
        parts = [picked(sources, offset, d) for d in range(8)]
        for v in range(4):
            out_ref[pl.ds(S_AT[offset] + HALF * v, HALF), :] = jnp.where(
                lane < 2 * STRIP, parts[2 * v], rolled(parts[2 * v + 1], 2 * STRIP)
            )
        levels = []
        for h in range(2):
            rows = parts[4 * h]
            for d in range(1, 4):
                rows = jnp.where(sub >= 2 * d, parts[4 * h + d], rows)
            even, odd = rolled(rows, 2 * STRIP), rolled(rows, STRIP)
            levels.append(jnp.where(sub % 2 == 1, odd, even))
        out_ref[pl.ds(S_AT[offset] + 4 * HALF, HALF), :] = jnp.where(
            lane < STRIP, levels[0], rolled(levels[1], STRIP)
        )


def sweep_kernel(
    shot_ref,
    near_ref,
    here_ref,
    far_ref,
    out_ref,
    wa_ref,
    wb_ref,
    e1_ref,
    e2_ref,
    e3_ref,
    head_ref,
    ma_ref,
    mb_ref,
    src_ref,
    refl_ref,
    wsel_ref,
    earth_ref,
    grad_ref,
    col_ref,
    raw_ref,
    nx_total,
    ny_total,
):
    lane = lane_index()
    sub = lax.broadcasted_iota(jnp.int32, (8, LANES), 0)
    depth_pos = position("depth")
    x_base = position("gx") * ROWS - 2 * ROWS
    y_base = position("gy") * (8 * STRIP) + depth_pos * STRIP - STRIP
    odd = depth_pos % 2 == 1
    y_cell = y_base + lane
    y_inside = (y_cell >= 0) & (y_cell < ny_total)
    zero = jnp.zeros((8, LANES), jnp.float32)

    def row_of(ref, lead, r):
        if lead is None:
            return ref[pl.ds(r, 8, stride=0), :]
        return ref[lead, pl.ds(r, 8, stride=0), :]

    def rim_factor(x_cell):
        inside = (x_cell >= 0) & (x_cell < nx_total) & y_inside
        penalty = jnp.where(inside, jnp.float32(0.0), jnp.float32(STEP_PENALTY))
        return jnp.exp(-penalty * RATE)

    shot_x = jnp.broadcast_to(shot_ref[:, 0:1].astype(jnp.float32), (8, LANES))
    shot_y = jnp.broadcast_to(shot_ref[:, 1:2].astype(jnp.float32), (8, LANES))
    y_square = (y_cell.astype(jnp.float32) - shot_y) ** 2

    def surface(r):
        x_cell = (x_base + r).astype(jnp.float32)
        return SURF * jnp.sqrt((x_cell - shot_x) ** 2 + y_square)

    def weight(diff):
        return jnp.exp(-diff * RATE)

    def near(diff):
        return jnp.clip(diff, -1.0, 1.0)

    middle = surface(MIDDLE)
    weight_minus = weight(near(pltpu.roll(middle, 1, 1) - middle))
    weight_plus = weight(near(pltpu.roll(middle, LANES - 1, 1) - middle))
    for r in range(FRAME):
        wa_ref[r + PAD] = weight(surface(r) - middle) * rim_factor(x_base + r)
    for ref in (wa_ref, wb_ref):
        ref[PAD - 1] = zero
        ref[PAD + FRAME] = zero

    def merged(tiles, j):
        part = tiles[0]
        one, two = (j + 1) % 4, (j + 2) % 4
        part = jnp.where((lane >= STRIP * one) & (lane < STRIP * (one + 1)), tiles[1], part)
        part = jnp.where((lane >= STRIP * two) & (lane < STRIP * (two + 1)), tiles[2], part)
        return rolled(part, -STRIP * j)

    def strips(row):
        at = (pl.ds(row, HALF), slice(None))
        one, two = near_ref[at], far_ref[at]
        left = jnp.where(odd, one, two)
        right = jnp.where(odd, two, one)
        return left, rolled(here_ref[at], STRIP), rolled(right, 2 * STRIP)

    rims = [rim_factor(x_base + HALF * g + sub) for g in range(FRAME // HALF)]

    for pair in range(PLANES // 2):
        for offset in range(5):
            if pair >= 4 and offset in (0, 4):
                tiles = strips(SHARED_AT + HALF * (pair - 4))
            else:
                tiles = strips(A_AT[offset] + HALF * pair)
            for j in range(4):
                p, h = divmod(j, 2)
                group = 2 * offset + h
                if pair >= 4 and group in (0, 9):
                    continue
                speed = merged(tiles, j)
                at = (2 * pair + p, pl.ds(HALF * group, HALF), slice(None))
                e1_ref[at] = jnp.exp(-speed * RATE) * rims[group]
                e2_ref[at] = jnp.exp(-(speed * ROOT2) * RATE) * rims[group]
                e3_ref[at] = jnp.exp(-(speed * ROOT3) * RATE) * rims[group]
                if 3 <= group < 7:
                    here = (2 * pair + p, pl.ds(HALF * (group - 3), HALF), slice(None))
                    earth_ref[here] = speed

    for offset in range(3):
        for v in range(4):
            tiles = strips(S_AT[offset] + HALF * v)
            for i in range(4):
                src_ref[ROWS * offset + 4 * v + i] = merged(tiles, i)
        tiles = strips(S_AT[offset] + 32)
        for h in range(2):
            inside = rims[2 + 2 * offset + h] > 0.5
            refl_ref[pl.ds(ROWS * offset + HALF * h, HALF), :] = jnp.where(
                inside, merged(tiles, h), jnp.float32(-1.0)
            )

    for r in range(48):
        wsel_ref[r] = zero + 1.0

    def along_y(value):
        return weight_minus * pltpu.roll(value, 1, 1) + weight_plus * pltpu.roll(
            value, LANES - 1, 1
        )

    def down_plane(k, w_ref, next_ref, first, last, select):
        level = k.astype(jnp.float32)
        w_before, w_now = w_ref[first - 1 + PAD], w_ref[first + PAD]
        q_before, q_now = along_y(w_before), along_y(w_now)
        for r in range(first, last):
            w_after = w_ref[r + 1 + PAD]
            q_after = along_y(w_after)
            part1 = row_of(e1_ref, k, r) * w_now
            part2 = row_of(e2_ref, k, r) * (q_now + (w_before + w_after))
            part3 = row_of(e3_ref, k, r) * (q_before + q_after)
            w_next = part1 + part2 + part3
            next_ref[r + PAD] = w_next
            if 31 <= r < 49:
                head_ref[k, r - 31] = part1 + ROOT2 * part2 + ROOT3 * part3
            if select and 16 <= r < 64:
                hit = row_of(refl_ref, None, r - 16) == level
                wsel_ref[r - 16] = jnp.where(hit, w_next, wsel_ref[r - 16])
            w_before, q_before, w_now, q_now = w_now, q_now, w_after, q_after

    def down(first, last, select):
        def two(i, carry):
            down_plane(2 * i, wa_ref, wb_ref, first, last, select)
            down_plane(2 * i + 1, wb_ref, wa_ref, first, last, select)
            return carry

        return two

    lax.fori_loop(0, 2, down(1, 79, False), 0)
    lax.fori_loop(2, 4, down(5, 75, True), 0)
    lax.fori_loop(4, 6, down(9, 71, True), 0)
    lax.fori_loop(6, 8, down(13, 67, True), 0)

    for ref in (ma_ref, mb_ref):
        ref[15 + PAD] = zero
        ref[64 + PAD] = zero

    for r in range(48):
        share = src_ref[r] / wsel_ref[r]
        wsel_ref[r] = share
        hit = row_of(refl_ref, None, r) == float(PLANES - 1)
        ma_ref[r + 16 + PAD] = jnp.where(hit, share, jnp.float32(0.0))
    for i in range(18):
        col_ref[i : i + 1, :] = jnp.sum(src_ref[15 + i], axis=0, keepdims=True)

    def gradient_rows(k, mu_ref):
        for i in range(18):
            product = mu_ref[31 + i + PAD] * head_ref[k, i]
            grad_ref[k, i : i + 1, :] = jnp.sum(product, axis=0, keepdims=True)

    def up(k, mu_ref, next_ref, first, last):
        gradient_rows(k, mu_ref)
        level = (k - 1).astype(jnp.float32)

        def spread(r):
            mu = mu_ref[r + PAD]
            return row_of(e1_ref, k, r) * mu, row_of(e2_ref, k, r) * mu, row_of(e3_ref, k, r) * mu

        _, u2_before, u3_before = spread(first - 1)
        u1, u2, u3 = spread(first)
        for r in range(first, last):
            n1, n2, n3 = spread(r + 1)
            both = u2 + (u3_before + n3)
            side = pltpu.roll(weight_plus * both, 1, 1) + pltpu.roll(
                weight_minus * both, LANES - 1, 1
            )
            hit = row_of(refl_ref, None, r - 16) == level
            own = jnp.where(hit, wsel_ref[r - 16], jnp.float32(0.0))
            next_ref[r + PAD] = (u1 + own) + (u2_before + n2) + side
            u2_before, u3_before, u1, u2, u3 = u2, u3, n1, n2, n3

    def up_two(top, first, last):
        def two(step, carry):
            k = top - 2 * step
            up(k, ma_ref, mb_ref, first, last)
            up(k - 1, mb_ref, ma_ref, first, last)
            return carry

        return two

    lax.fori_loop(0, 2, up_two(15, 17, 63), 0)
    lax.fori_loop(0, 2, up_two(11, 21, 59), 0)
    lax.fori_loop(0, 2, up_two(7, 25, 55), 0)
    up_two(3, 29, 51)(jnp.int32(0), 0)
    up(jnp.int32(1), ma_ref, mb_ref, 31, 49)
    gradient_rows(0, mb_ref)

    for pair in range(PLANES // 2):
        parts = []
        for p in range(2):
            k = 2 * pair + p
            shown = jnp.where(
                float(k) <= refl_ref[15:33, :], col_ref[0:18, :], jnp.float32(0.0)
            )
            raw_ref[k, 0:18, :] = jnp.where(
                earth_ref[k, 7:25, :] < AIR_TEST, grad_ref[k, 0:18, :] + shown, jnp.float32(0.0)
            )
            for h in range(2):
                mid = raw_ref[k, HALF * h + 1 : HALF * h + 9, :]
                column = (raw_ref[k, HALF * h : HALF * h + 8, :] + mid) + raw_ref[
                    k, HALF * h + 2 : HALF * h + 10, :
                ]
                total = column + (pltpu.roll(column, 1, 1) + pltpu.roll(column, LANES - 1, 1))
                smooth = 0.4375 * mid + 0.0625 * total
                parts.append(rolled(smooth, STRIP * (2 * p + h - 1)))
        out_ref[pl.ds(HALF * pair, HALF), :] = quarters(parts, lane)


def unpack_kernel(in_ref, out_ref):
    lane = lane_index()
    for c in range(2):
        tiles = [in_ref[pl.ds(HALF * (4 * c + q), HALF), :] for q in range(4)]
        for j in range(4):
            parts = [rolled(tiles[q], STRIP * (q - j)) for q in range(4)]
            out_ref[j // 2, pl.ds(HALF * (j % 2), HALF), pl.ds(LANES * c, LANES)] = quarters(
                parts, lane
            )


def in_vmem(count):
    return [pl.BlockSpec(memory_space=pltpu.VMEM)] * count


def line(count, shift):
    return [(i, i + shift) for i in range(count) if 0 <= i + shift < count]


def sweep_call(shot_cells, near, column, far, nx_total, ny_total):
    def kernel(*refs):
        sweep_kernel(*refs, nx_total=nx_total, ny_total=ny_total)

    field = (FULL, SHOTS, LANES)
    return pl.pallas_call(
        kernel,
        out_shape=jax.ShapeDtypeStruct((TILE, LANES), jnp.float32),
        in_specs=in_vmem(4),
        out_specs=in_vmem(1)[0],
        scratch_shapes=[
            *[pltpu.VMEM(field, jnp.float32)] * 2,
            *[pltpu.VMEM((PLANES, FULL, LANES), jnp.float32)] * 3,
            pltpu.VMEM((PLANES, 18, SHOTS, LANES), jnp.float32),
            *[pltpu.VMEM(field, jnp.float32)] * 2,
            pltpu.VMEM((48, SHOTS, LANES), jnp.float32),
            pltpu.VMEM((56, LANES), jnp.float32),
            pltpu.VMEM((48, SHOTS, LANES), jnp.float32),
            pltpu.VMEM((PLANES, 32, LANES), jnp.float32),
            pltpu.VMEM((PLANES, 24, LANES), jnp.float32),
            pltpu.VMEM((24, LANES), jnp.float32),
            pltpu.VMEM((PLANES, 24, LANES), jnp.float32),
        ],
        compiler_params=pltpu.CompilerParams(vmem_limit_bytes=SWEEP_VMEM),
        name="sweep",
    )(shot_cells, near, column, far)


def local(slowness, air_mask, reflector, shot_cells, receiver_mask, residual):
    depth_count = lax.axis_size("depth")
    x_count = lax.axis_size("gx")
    y_count = lax.axis_size("gy")
    nx_total = ROWS * x_count
    ny_total = STRIP * depth_count * y_count
    f32 = jnp.float32

    packed = pl.pallas_call(
        pack_kernel,
        out_shape=jax.ShapeDtypeStruct((4 * TILE, LANES), f32),
        in_specs=in_vmem(5),
        out_specs=in_vmem(1)[0],
        scratch_shapes=[
            pltpu.VMEM((2, SHOTS, ROWS + 8, LANES), f32),
            pltpu.VMEM((2, ROWS + 8, LANES), f32),
        ],
        compiler_params=pltpu.CompilerParams(vmem_limit_bytes=SMALL_VMEM),
        name="pack",
    )(slowness, air_mask, reflector, receiver_mask, residual)

    pairs = [
        [d * x_count + 2 * i + m for d in range(depth_count) for m in range(2)]
        for i in range(x_count // 2)
    ]
    got = lax.all_to_all(
        packed.reshape(16, 2 * HALF, LANES),
        ("depth", "gx"),
        0,
        0,
        tiled=True,
        axis_index_groups=pairs,
    )
    own = got.reshape(8, 2, 2, HALF, LANES).transpose(2, 1, 0, 3, 4)
    own = own.reshape(4, TILE, LANES)
    above = lax.ppermute(
        jnp.concatenate([own[0:2], own[3:4]], 0), "gx", line(x_count, 2)
    )
    below = lax.ppermute(own[0:3], "gx", line(x_count, -2))
    column = pl.pallas_call(
        arrange_kernel,
        out_shape=jax.ShapeDtypeStruct((COLUMN, LANES), f32),
        in_specs=in_vmem(3),
        out_specs=in_vmem(1)[0],
        compiler_params=pltpu.CompilerParams(vmem_limit_bytes=SMALL_VMEM),
        name="arrange",
    )(above, own, below)

    def place(q):
        return (q % depth_count) * y_count + q // depth_count

    def swapped(first):
        pairs = [(q, q + 1) for q in range(first, depth_count * y_count - 1, 2)]
        return [(place(i), place(j)) for a, b in pairs for i, j in ((a, b), (b, a))]

    near = lax.ppermute(column, ("depth", "gy"), swapped(0))
    far = lax.ppermute(column, ("depth", "gy"), swapped(1))

    strips_out = sweep_call(shot_cells, near, column, far, nx_total, ny_total)
    parts = lax.all_to_all(
        strips_out.reshape(8, HALF, LANES), "depth", 0, 0, tiled=True
    ).reshape(TILE, LANES)
    return pl.pallas_call(
        unpack_kernel,
        out_shape=jax.ShapeDtypeStruct(slowness.shape, f32),
        in_specs=in_vmem(1),
        out_specs=in_vmem(1)[0],
        compiler_params=pltpu.CompilerParams(vmem_limit_bytes=SMALL_VMEM),
        name="unpack",
    )(parts)


def solution(mesh):
    in_specs = (
        P("depth", "gx", "gy"),
        P("depth", "gx", "gy"),
        P("gx", "gy"),
        P(),
        P(None, "gx", "gy"),
        P(None, "gx", "gy"),
    )
    out_specs = P("depth", "gx", "gy")
    return jax.shard_map(local, mesh=mesh, in_specs=in_specs, out_specs=out_specs, check_vma=False)
```

```python
import math

import jax
import jax.numpy as jnp
from jax import lax
from jax.experimental import pallas as pl
from jax.experimental.pallas import tpu as pltpu
from jax.sharding import PartitionSpec as P

SOFTMIN_TEMPER = 0.5
SURF = 0.7
AIR_SLOW = 2.5
AIR_TEST = 2.0
STEP_PENALTY = 10000.0
RATE = 1.0 / SOFTMIN_TEMPER
ROOT2 = math.sqrt(2.0)
ROOT3 = math.sqrt(3.0)

LANES = 128
STRIP = 32
ROWS = 16
PLANES = 16
SHOTS = 8
FRAME = 80
PAD = 8
FULL = FRAME + 2 * PAD
TILE = 64
A_AT = (0, 32, 96, 160, 224)
SHARED_AT = 256
S_AT = (288, 328, 368)
COLUMN = 408
MIDDLE = 40
HALF = 8
SWEEP_VMEM = 16 * 1024 * 1024
SMALL_VMEM = 4 * 1024 * 1024
PACK_VMEM = 60 * 1024 * 1024


def position(axis):
    return lax.axis_index(axis)


def rolled(value, shift):
    shift = shift % LANES
    return value if shift == 0 else pltpu.roll(value, shift, value.ndim - 1)


def lane_index(rows=8):
    return lax.broadcasted_iota(jnp.int32, (rows, LANES), 1)


def quarters(parts, lane):
    out = parts[0]
    for j in range(1, len(parts)):
        out = jnp.where(lane >= STRIP * j, parts[j], out)
    return out


def pack_kernel(*refs):
    out_ref, live_ref, level_ref, sems = refs[5], refs[11], refs[12], refs[13]
    copies = [pltpu.make_async_copy(refs[i], refs[6 + i], sems.at[i]) for i in range(5)]
    for copy in copies:
        copy.start()
    for copy in copies:
        copy.wait()
    slow_ref, air_ref, refl_ref, mask_ref, resid_ref = refs[6:11]
    lane = lane_index()
    sub = lax.broadcasted_iota(jnp.int32, (8, LANES), 0)
    first = 2 * position("depth")
    speed = {}
    for p in range(2):
        for h in range(2):
            for c in range(2):
                at = (p, pl.ds(HALF * h, HALF), pl.ds(LANES * c, LANES))
                speed[p, h, c] = jnp.where(air_ref[at] == 1, jnp.float32(AIR_SLOW), slow_ref[at])
    for h in range(2):
        for c in range(2):
            here = pl.ds(HALF * h, HALF)
            at = (here, pl.ds(LANES * c, LANES))
            level_ref[c, here, :] = refl_ref[at].astype(jnp.float32)
            for shot in range(SHOTS):
                live_ref[c, shot, here, :] = jnp.where(
                    mask_ref[shot, *at] == 1, resid_ref[shot, *at], jnp.float32(0.0)
                )
    rows = {}
    for i in range(2):
        for c in range(2):
            at = (pl.ds(first + i, 8, stride=0), slice(None))
            rows[2 + i, c] = level_ref[c, *at]
            row = live_ref[c, 0, *at]
            for shot in range(1, SHOTS):
                row = jnp.where(sub >= shot, live_ref[c, shot, *at], row)
            rows[i, c] = row
    for target in range(8):
        c, q = divmod(target, 4)
        planes = quarters(
            [rolled(speed[j // 2, j % 2, c], STRIP * (j - q)) for j in range(4)], lane
        )
        sources = quarters([rolled(rows[j, c], STRIP * (j - q)) for j in range(4)], lane)
        for member in range(2):
            at = 2 * HALF * (2 * target + member)
            out_ref[pl.ds(at, HALF), :] = planes
            out_ref[pl.ds(at + HALF, HALF), :] = sources


def stage_kernel(got_ref, own_ref, up_ref, down_ref):
    lane = lane_index()
    sub = lax.broadcasted_iota(jnp.int32, (8, LANES), 0)
    odd_quarter = (lane // STRIP) % 2 == 1
    speed = [[got_ref[4 * d + 2 * m] for d in range(8)] for m in range(2)]
    source = []
    for m in range(2):
        parts = [got_ref[4 * d + 2 * m + 1] for d in range(8)]
        tiles = [
            jnp.where(lane < 2 * STRIP, parts[2 * v], rolled(parts[2 * v + 1], 2 * STRIP))
            for v in range(4)
        ]
        levels = []
        for h in range(2):
            rows = parts[4 * h]
            for d in range(1, 4):
                rows = jnp.where(sub >= 2 * d, parts[4 * h + d], rows)
            even, odd = rolled(rows, 2 * STRIP), rolled(rows, STRIP)
            levels.append(jnp.where(sub % 2 == 1, odd, even))
        tiles.append(jnp.where(lane < STRIP, levels[0], rolled(levels[1], STRIP)))
        source.append(tiles)
    outer_up = [
        jnp.where(odd_quarter, speed[0][d], rolled(speed[0][d + 1], -STRIP)) for d in (4, 6)
    ]
    outer_down = [
        jnp.where(odd_quarter, rolled(speed[1][d + 1], STRIP), speed[1][d]) for d in (4, 6)
    ]
    for ref, tiles in (
        (own_ref, [*speed[0], *speed[1], *source[0], *source[1]]),
        (up_ref, [*speed[0][:4], *outer_up, *speed[1], *source[1]]),
        (down_ref, [*speed[0], *speed[1][:4], *outer_down, *source[0]]),
    ):
        for i, tile in enumerate(tiles):
            ref[i] = tile


def arrange_kernel(above_ref, own_ref, below_ref, out_ref):
    lane = lane_index()
    second = position("gx") % 2 == 1
    odd_quarter = (lane // STRIP) % 2 == 1

    def outer(ref, first, shift):
        tiles = [ref[first + i] for i in range(4)]
        for i in (4, 5):
            part = ref[first + i]
            moved = rolled(part, shift)
            tiles += [part, moved]
        return tiles

    speeds = [
        outer(above_ref, 0, STRIP),
        [above_ref[6 + i] for i in range(8)],
        [own_ref[i] for i in range(8)],
        [own_ref[8 + i] for i in range(8)],
        [below_ref[i] for i in range(8)],
        outer(below_ref, 8, -STRIP),
    ]
    sources = [
        [ref[first + i] for i in range(5)]
        for ref, first in ((above_ref, 14), (own_ref, 16), (own_ref, 21), (below_ref, 14))
    ]

    def picked(choices, i, part):
        return jnp.where(second, choices[i + 1][part], choices[i][part])

    for offset in range(5):
        for part in range(4 if offset in (0, 4) else 8):
            out_ref[pl.ds(A_AT[offset] + HALF * part, HALF), :] = picked(speeds, offset, part)
    for part in range(4, 8):
        out_ref[pl.ds(SHARED_AT + HALF * (part - 4), HALF), :] = jnp.where(
            odd_quarter, picked(speeds, 0, part), picked(speeds, 4, part)
        )
    for offset in range(3):
        for part in range(5):
            at = pl.ds(S_AT[offset] + HALF * part, HALF)
            out_ref[at, :] = picked(sources, offset, part)


def sweep_kernel(
    shot_ref,
    near_ref,
    here_ref,
    far_ref,
    out_ref,
    wa_ref,
    wb_ref,
    e1_ref,
    e2_ref,
    e3_ref,
    head_ref,
    ma_ref,
    mb_ref,
    src_ref,
    refl_ref,
    wsel_ref,
    earth_ref,
    grad_ref,
    col_ref,
    raw_ref,
    nx_total,
    ny_total,
):
    lane = lane_index()
    sub = lax.broadcasted_iota(jnp.int32, (8, LANES), 0)
    depth_pos = position("depth")
    x_base = position("gx") * ROWS - 2 * ROWS
    y_base = position("gy") * (8 * STRIP) + depth_pos * STRIP - STRIP
    odd = depth_pos % 2 == 1
    y_cell = y_base + lane
    y_inside = (y_cell >= 0) & (y_cell < ny_total)
    zero = jnp.zeros((8, LANES), jnp.float32)

    def row_of(ref, lead, r):
        if lead is None:
            return ref[pl.ds(r, 8, stride=0), :]
        return ref[lead, pl.ds(r, 8, stride=0), :]

    def rim_factor(x_cell):
        inside = (x_cell >= 0) & (x_cell < nx_total) & y_inside
        penalty = jnp.where(inside, jnp.float32(0.0), jnp.float32(STEP_PENALTY))
        return jnp.exp(-penalty * RATE)

    shot_x = jnp.broadcast_to(shot_ref[:, 0:1].astype(jnp.float32), (8, LANES))
    shot_y = jnp.broadcast_to(shot_ref[:, 1:2].astype(jnp.float32), (8, LANES))
    y_square = (y_cell.astype(jnp.float32) - shot_y) ** 2

    def surface(r):
        x_cell = (x_base + r).astype(jnp.float32)
        return SURF * jnp.sqrt((x_cell - shot_x) ** 2 + y_square)

    def weight(diff):
        return jnp.exp(-diff * RATE)

    def near(diff):
        return jnp.clip(diff, -1.0, 1.0)

    middle = surface(MIDDLE)
    weight_minus = weight(near(pltpu.roll(middle, 1, 1) - middle))
    weight_plus = weight(near(pltpu.roll(middle, LANES - 1, 1) - middle))
    for r in range(FRAME):
        wa_ref[r + PAD] = weight(surface(r) - middle) * rim_factor(x_base + r)
    for ref in (wa_ref, wb_ref):
        ref[PAD - 1] = zero
        ref[PAD + FRAME] = zero

    def merged(tiles, j):
        part = tiles[0]
        one, two = (j + 1) % 4, (j + 2) % 4
        part = jnp.where((lane >= STRIP * one) & (lane < STRIP * (one + 1)), tiles[1], part)
        part = jnp.where((lane >= STRIP * two) & (lane < STRIP * (two + 1)), tiles[2], part)
        return rolled(part, -STRIP * j)

    def strips(row):
        at = (pl.ds(row, HALF), slice(None))
        one, two = near_ref[at], far_ref[at]
        left = jnp.where(odd, one, two)
        right = jnp.where(odd, two, one)
        return left, rolled(here_ref[at], STRIP), rolled(right, 2 * STRIP)

    rims = [rim_factor(x_base + HALF * g + sub) for g in range(FRAME // HALF)]

    for pair in range(PLANES // 2):
        for offset in range(5):
            if pair >= 4 and offset in (0, 4):
                tiles = strips(SHARED_AT + HALF * (pair - 4))
            else:
                tiles = strips(A_AT[offset] + HALF * pair)
            for j in range(4):
                p, h = divmod(j, 2)
                group = 2 * offset + h
                if pair >= 4 and group in (0, 9):
                    continue
                speed = merged(tiles, j)
                at = (2 * pair + p, pl.ds(HALF * group, HALF), slice(None))
                e1_ref[at] = jnp.exp(-speed * RATE) * rims[group]
                e2_ref[at] = jnp.exp(-(speed * ROOT2) * RATE) * rims[group]
                e3_ref[at] = jnp.exp(-(speed * ROOT3) * RATE) * rims[group]
                if 3 <= group < 7:
                    here = (2 * pair + p, pl.ds(HALF * (group - 3), HALF), slice(None))
                    earth_ref[here] = speed

    for offset in range(3):
        for v in range(4):
            tiles = strips(S_AT[offset] + HALF * v)
            for i in range(4):
                src_ref[ROWS * offset + 4 * v + i] = merged(tiles, i)
        tiles = strips(S_AT[offset] + 32)
        for h in range(2):
            inside = rims[2 + 2 * offset + h] > 0.5
            refl_ref[pl.ds(ROWS * offset + HALF * h, HALF), :] = jnp.where(
                inside, merged(tiles, h), jnp.float32(-1.0)
            )

    for r in range(48):
        wsel_ref[r] = zero + 1.0

    def along_y(value):
        return weight_minus * pltpu.roll(value, 1, 1) + weight_plus * pltpu.roll(
            value, LANES - 1, 1
        )

    def down_plane(k, w_ref, next_ref, first, last, select):
        level = k.astype(jnp.float32)
        w_before, w_now = w_ref[first - 1 + PAD], w_ref[first + PAD]
        q_before, q_now = along_y(w_before), along_y(w_now)
        for r in range(first, last):
            w_after = w_ref[r + 1 + PAD]
            q_after = along_y(w_after)
            part1 = row_of(e1_ref, k, r) * w_now
            part2 = row_of(e2_ref, k, r) * (q_now + (w_before + w_after))
            part3 = row_of(e3_ref, k, r) * (q_before + q_after)
            w_next = part1 + part2 + part3
            next_ref[r + PAD] = w_next
            if 31 <= r < 49:
                head_ref[k, r - 31] = part1 + ROOT2 * part2 + ROOT3 * part3
            if select and 16 <= r < 64:
                hit = row_of(refl_ref, None, r - 16) == level
                wsel_ref[r - 16] = jnp.where(hit, w_next, wsel_ref[r - 16])
            w_before, q_before, w_now, q_now = w_now, q_now, w_after, q_after

    def down(first, last, select):
        def two(i, carry):
            down_plane(2 * i, wa_ref, wb_ref, first, last, select)
            down_plane(2 * i + 1, wb_ref, wa_ref, first, last, select)
            return carry

        return two

    lax.fori_loop(0, 2, down(1, 79, False), 0)
    lax.fori_loop(2, 4, down(5, 75, True), 0)
    lax.fori_loop(4, 6, down(9, 71, True), 0)
    lax.fori_loop(6, 8, down(13, 67, True), 0)

    for ref in (ma_ref, mb_ref):
        ref[15 + PAD] = zero
        ref[64 + PAD] = zero

    for r in range(48):
        share = src_ref[r] / wsel_ref[r]
        wsel_ref[r] = share
        hit = row_of(refl_ref, None, r) == float(PLANES - 1)
        ma_ref[r + 16 + PAD] = jnp.where(hit, share, jnp.float32(0.0))
    for i in range(18):
        col_ref[i : i + 1, :] = jnp.sum(src_ref[15 + i], axis=0, keepdims=True)

    def gradient_rows(k, mu_ref):
        for i in range(18):
            product = mu_ref[31 + i + PAD] * head_ref[k, i]
            grad_ref[k, i : i + 1, :] = jnp.sum(product, axis=0, keepdims=True)

    def up(k, mu_ref, next_ref, first, last):
        gradient_rows(k, mu_ref)
        level = (k - 1).astype(jnp.float32)

        def spread(r):
            mu = mu_ref[r + PAD]
            return row_of(e1_ref, k, r) * mu, row_of(e2_ref, k, r) * mu, row_of(e3_ref, k, r) * mu

        _, u2_before, u3_before = spread(first - 1)
        u1, u2, u3 = spread(first)
        for r in range(first, last):
            n1, n2, n3 = spread(r + 1)
            both = u2 + (u3_before + n3)
            side = pltpu.roll(weight_plus * both, 1, 1) + pltpu.roll(
                weight_minus * both, LANES - 1, 1
            )
            hit = row_of(refl_ref, None, r - 16) == level
            own = jnp.where(hit, wsel_ref[r - 16], jnp.float32(0.0))
            next_ref[r + PAD] = (u1 + own) + (u2_before + n2) + side
            u2_before, u3_before, u1, u2, u3 = u2, u3, n1, n2, n3

    def up_two(top, first, last):
        def two(step, carry):
            k = top - 2 * step
            up(k, ma_ref, mb_ref, first, last)
            up(k - 1, mb_ref, ma_ref, first, last)
            return carry

        return two

    lax.fori_loop(0, 2, up_two(15, 17, 63), 0)
    lax.fori_loop(0, 2, up_two(11, 21, 59), 0)
    lax.fori_loop(0, 2, up_two(7, 25, 55), 0)
    up_two(3, 29, 51)(jnp.int32(0), 0)
    up(jnp.int32(1), ma_ref, mb_ref, 31, 49)
    gradient_rows(0, mb_ref)

    for pair in range(PLANES // 2):
        parts = []
        for p in range(2):
            k = 2 * pair + p
            shown = jnp.where(
                float(k) <= refl_ref[15:33, :], col_ref[0:18, :], jnp.float32(0.0)
            )
            raw_ref[k, 0:18, :] = jnp.where(
                earth_ref[k, 7:25, :] < AIR_TEST, grad_ref[k, 0:18, :] + shown, jnp.float32(0.0)
            )
            for h in range(2):
                mid = raw_ref[k, HALF * h + 1 : HALF * h + 9, :]
                column = (raw_ref[k, HALF * h : HALF * h + 8, :] + mid) + raw_ref[
                    k, HALF * h + 2 : HALF * h + 10, :
                ]
                total = column + (pltpu.roll(column, 1, 1) + pltpu.roll(column, LANES - 1, 1))
                smooth = 0.4375 * mid + 0.0625 * total
                parts.append(rolled(smooth, STRIP * (2 * p + h - 1)))
        out_ref[pl.ds(HALF * pair, HALF), :] = quarters(parts, lane)


def unpack_kernel(in_ref, out_ref):
    lane = lane_index()
    for c in range(2):
        tiles = [in_ref[pl.ds(HALF * (4 * c + q), HALF), :] for q in range(4)]
        for j in range(4):
            parts = [rolled(tiles[q], STRIP * (q - j)) for q in range(4)]
            out_ref[j // 2, pl.ds(HALF * (j % 2), HALF), pl.ds(LANES * c, LANES)] = quarters(
                parts, lane
            )


def in_vmem(count):
    return [pl.BlockSpec(memory_space=pltpu.VMEM)] * count


def line(count, shift):
    return [(i, i + shift) for i in range(count) if 0 <= i + shift < count]


def sweep_call(shot_cells, near, column, far, nx_total, ny_total):
    def kernel(*refs):
        sweep_kernel(*refs, nx_total=nx_total, ny_total=ny_total)

    field = (FULL, SHOTS, LANES)
    return pl.pallas_call(
        kernel,
        out_shape=jax.ShapeDtypeStruct((TILE, LANES), jnp.float32),
        in_specs=in_vmem(4),
        out_specs=in_vmem(1)[0],
        scratch_shapes=[
            *[pltpu.VMEM(field, jnp.float32)] * 2,
            *[pltpu.VMEM((PLANES, FULL, LANES), jnp.float32)] * 3,
            pltpu.VMEM((PLANES, 18, SHOTS, LANES), jnp.float32),
            *[pltpu.VMEM(field, jnp.float32)] * 2,
            pltpu.VMEM((48, SHOTS, LANES), jnp.float32),
            pltpu.VMEM((56, LANES), jnp.float32),
            pltpu.VMEM((48, SHOTS, LANES), jnp.float32),
            pltpu.VMEM((PLANES, 32, LANES), jnp.float32),
            pltpu.VMEM((PLANES, 24, LANES), jnp.float32),
            pltpu.VMEM((24, LANES), jnp.float32),
            pltpu.VMEM((PLANES, 24, LANES), jnp.float32),
        ],
        compiler_params=pltpu.CompilerParams(vmem_limit_bytes=SWEEP_VMEM),
        name="sweep",
    )(shot_cells, near, column, far)


def local(slowness, air_mask, reflector, shot_cells, receiver_mask, residual):
    depth_count = lax.axis_size("depth")
    x_count = lax.axis_size("gx")
    y_count = lax.axis_size("gy")
    nx_total = ROWS * x_count
    ny_total = STRIP * depth_count * y_count
    f32 = jnp.float32

    packed = pl.pallas_call(
        pack_kernel,
        out_shape=jax.ShapeDtypeStruct((4 * TILE, LANES), f32),
        in_specs=[pl.BlockSpec(memory_space=pltpu.HBM)] * 5,
        out_specs=in_vmem(1)[0],
        scratch_shapes=[
            *[
                pltpu.VMEM(arg.shape, arg.dtype)
                for arg in (slowness, air_mask, reflector, receiver_mask, residual)
            ],
            pltpu.VMEM((2, SHOTS, ROWS + 8, LANES), f32),
            pltpu.VMEM((2, ROWS + 8, LANES), f32),
            pltpu.SemaphoreType.DMA((5,)),
        ],
        compiler_params=pltpu.CompilerParams(vmem_limit_bytes=PACK_VMEM),
        name="pack",
    )(slowness, air_mask, reflector, receiver_mask, residual)

    pairs = [
        [d * x_count + 2 * i + m for d in range(depth_count) for m in range(2)]
        for i in range(x_count // 2)
    ]
    got = lax.all_to_all(
        packed.reshape(16, 2 * HALF, LANES),
        ("depth", "gx"),
        0,
        0,
        tiled=True,
        axis_index_groups=pairs,
    )
    own, up, down = pl.pallas_call(
        stage_kernel,
        out_shape=tuple(jax.ShapeDtypeStruct((n, HALF, LANES), f32) for n in (26, 19, 19)),
        in_specs=in_vmem(1),
        out_specs=tuple(in_vmem(3)),
        compiler_params=pltpu.CompilerParams(vmem_limit_bytes=SMALL_VMEM),
        name="stage",
    )(got.reshape(32, HALF, LANES))
    above = lax.ppermute(up, "gx", line(x_count, 2))
    below = lax.ppermute(down, "gx", line(x_count, -2))
    column = pl.pallas_call(
        arrange_kernel,
        out_shape=jax.ShapeDtypeStruct((COLUMN, LANES), f32),
        in_specs=in_vmem(3),
        out_specs=in_vmem(1)[0],
        compiler_params=pltpu.CompilerParams(vmem_limit_bytes=SMALL_VMEM),
        name="arrange",
    )(above, own, below)

    def place(q):
        return (q % depth_count) * y_count + q // depth_count

    def swapped(first):
        pairs = [(q, q + 1) for q in range(first, depth_count * y_count - 1, 2)]
        return [(place(i), place(j)) for a, b in pairs for i, j in ((a, b), (b, a))]

    near = lax.ppermute(column, ("depth", "gy"), swapped(0))
    far = lax.ppermute(column, ("depth", "gy"), swapped(1))

    strips_out = sweep_call(shot_cells, near, column, far, nx_total, ny_total)
    parts = lax.all_to_all(
        strips_out.reshape(8, HALF, LANES), "depth", 0, 0, tiled=True
    ).reshape(TILE, LANES)
    return pl.pallas_call(
        unpack_kernel,
        out_shape=jax.ShapeDtypeStruct(slowness.shape, f32),
        in_specs=in_vmem(1),
        out_specs=in_vmem(1)[0],
        compiler_params=pltpu.CompilerParams(vmem_limit_bytes=SMALL_VMEM),
        name="unpack",
    )(parts)


def solution(mesh):
    in_specs = (
        P("depth", "gx", "gy"),
        P("depth", "gx", "gy"),
        P("gx", "gy"),
        P(),
        P(None, "gx", "gy"),
        P(None, "gx", "gy"),
    )
    out_specs = P("depth", "gx", "gy")
    return jax.shard_map(local, mesh=mesh, in_specs=in_specs, out_specs=out_specs, check_vma=False)
```

```python
import math

import jax
import jax.numpy as jnp
from jax import lax
from jax.experimental import pallas as pl
from jax.experimental.pallas import tpu as pltpu
from jax.sharding import PartitionSpec as P

SOFTMIN_TEMPER = 0.5
SURF = 0.7
AIR_SLOW = 2.5
AIR_TEST = 2.0
STEP_PENALTY = 10000.0
RATE = -1.0 / (SOFTMIN_TEMPER * math.log(2.0))
ROOT2 = math.sqrt(2.0)
ROOT3 = math.sqrt(3.0)

LANES = 128
STRIP = 32
ROWS = 16
PLANES = 16
SHOTS = 8
FRAME = 80
PAD = 8
FULL = FRAME + 2 * PAD
TILE = 64
A_AT = (0, 32, 96, 160, 224)
SHARED_AT = 256
S_AT = (288, 328, 368)
COLUMN = 408
MIDDLE = 40
HALF = 8
SWEEP_VMEM = 16 * 1024 * 1024
SMALL_VMEM = 4 * 1024 * 1024


def position(axis):
    return lax.axis_index(axis)


def rolled(value, shift):
    shift = shift % LANES
    return value if shift == 0 else pltpu.roll(value, shift, value.ndim - 1)


def lane_index(rows=8):
    return lax.broadcasted_iota(jnp.int32, (rows, LANES), 1)


def quarters(parts, lane):
    out = parts[0]
    for j in range(1, len(parts)):
        out = jnp.where(lane >= STRIP * j, parts[j], out)
    return out


def pack_kernel(*refs):
    out_ref, live_ref, level_ref, sems = refs[5], refs[11], refs[12], refs[13]
    copies = [pltpu.make_async_copy(refs[i], refs[6 + i], sems.at[i]) for i in range(5)]
    for copy in copies:
        copy.start()
    for copy in copies:
        copy.wait()
    slow_ref, air_ref, refl_ref, mask_ref, resid_ref = refs[6:11]
    lane = lane_index()
    sub = lax.broadcasted_iota(jnp.int32, (8, LANES), 0)
    first = 2 * position("depth")
    speed = {}
    for p in range(2):
        for h in range(2):
            for c in range(2):
                at = (p, pl.ds(HALF * h, HALF), pl.ds(LANES * c, LANES))
                speed[p, h, c] = jnp.where(air_ref[at] == 1, jnp.float32(AIR_SLOW), slow_ref[at])
    for h in range(2):
        for c in range(2):
            here = pl.ds(HALF * h, HALF)
            at = (here, pl.ds(LANES * c, LANES))
            level_ref[c, here, :] = refl_ref[at].astype(jnp.float32)
            for shot in range(SHOTS):
                live_ref[c, shot, here, :] = jnp.where(
                    mask_ref[shot, *at] == 1, resid_ref[shot, *at], jnp.float32(0.0)
                )
    rows = {}
    for i in range(2):
        for c in range(2):
            at = (pl.ds(first + i, 8, stride=0), slice(None))
            rows[2 + i, c] = level_ref[c, *at]
            row = live_ref[c, 0, *at]
            for shot in range(1, SHOTS):
                row = jnp.where(sub >= shot, live_ref[c, shot, *at], row)
            rows[i, c] = row
    for target in range(8):
        c, q = divmod(target, 4)
        planes = quarters(
            [rolled(speed[j // 2, j % 2, c], STRIP * (j - q)) for j in range(4)], lane
        )
        sources = quarters([rolled(rows[j, c], STRIP * (j - q)) for j in range(4)], lane)
        for member in range(2):
            at = 2 * HALF * (2 * target + member)
            out_ref[pl.ds(at, HALF), :] = planes
            out_ref[pl.ds(at + HALF, HALF), :] = sources


def stage_kernel(got_ref, own_ref, up_ref, down_ref):
    lane = lane_index()
    sub = lax.broadcasted_iota(jnp.int32, (8, LANES), 0)
    odd_quarter = (lane // STRIP) % 2 == 1
    speed = [[got_ref[4 * d + 2 * m] for d in range(8)] for m in range(2)]
    source = []
    for m in range(2):
        parts = [got_ref[4 * d + 2 * m + 1] for d in range(8)]
        tiles = [
            jnp.where(lane < 2 * STRIP, parts[2 * v], rolled(parts[2 * v + 1], 2 * STRIP))
            for v in range(4)
        ]
        levels = []
        for h in range(2):
            rows = parts[4 * h]
            for d in range(1, 4):
                rows = jnp.where(sub >= 2 * d, parts[4 * h + d], rows)
            even, odd = rolled(rows, 2 * STRIP), rolled(rows, STRIP)
            levels.append(jnp.where(sub % 2 == 1, odd, even))
        tiles.append(jnp.where(lane < STRIP, levels[0], rolled(levels[1], STRIP)))
        source.append(tiles)
    outer_up = [
        jnp.where(odd_quarter, speed[0][d], rolled(speed[0][d + 1], -STRIP)) for d in (4, 6)
    ]
    outer_down = [
        jnp.where(odd_quarter, rolled(speed[1][d + 1], STRIP), speed[1][d]) for d in (4, 6)
    ]
    for ref, tiles in (
        (own_ref, [*speed[0], *speed[1], *source[0], *source[1]]),
        (up_ref, [*speed[0][:4], *outer_up, *speed[1], *source[1]]),
        (down_ref, [*speed[0], *speed[1][:4], *outer_down, *source[0]]),
    ):
        for i, tile in enumerate(tiles):
            ref[i] = tile


def arrange_kernel(above_ref, own_ref, below_ref, out_ref):
    lane = lane_index()
    second = position("gx") % 2 == 1
    odd_quarter = (lane // STRIP) % 2 == 1

    def outer(ref, first, shift):
        tiles = [ref[first + i] for i in range(4)]
        for i in (4, 5):
            part = ref[first + i]
            moved = rolled(part, shift)
            tiles += [part, moved]
        return tiles

    speeds = [
        outer(above_ref, 0, STRIP),
        [above_ref[6 + i] for i in range(8)],
        [own_ref[i] for i in range(8)],
        [own_ref[8 + i] for i in range(8)],
        [below_ref[i] for i in range(8)],
        outer(below_ref, 8, -STRIP),
    ]
    sources = [
        [ref[first + i] for i in range(5)]
        for ref, first in ((above_ref, 14), (own_ref, 16), (own_ref, 21), (below_ref, 14))
    ]

    def picked(choices, i, part):
        return jnp.where(second, choices[i + 1][part], choices[i][part])

    for offset in range(5):
        for part in range(4 if offset in (0, 4) else 8):
            out_ref[pl.ds(A_AT[offset] + HALF * part, HALF), :] = picked(speeds, offset, part)
    for part in range(4, 8):
        out_ref[pl.ds(SHARED_AT + HALF * (part - 4), HALF), :] = jnp.where(
            odd_quarter, picked(speeds, 0, part), picked(speeds, 4, part)
        )
    for offset in range(3):
        for part in range(5):
            at = pl.ds(S_AT[offset] + HALF * part, HALF)
            out_ref[at, :] = picked(sources, offset, part)


def sweep_kernel(
    shot_ref,
    near_ref,
    here_ref,
    far_ref,
    out_ref,
    wa_ref,
    wb_ref,
    e1_ref,
    e2_ref,
    e3_ref,
    head_ref,
    ma_ref,
    mb_ref,
    src_ref,
    refl_ref,
    wsel_ref,
    earth_ref,
    grad_ref,
    col_ref,
    raw_ref,
    nx_total,
    ny_total,
):
    lane = lane_index()
    sub = lax.broadcasted_iota(jnp.int32, (8, LANES), 0)
    depth_pos = position("depth")
    x_base = position("gx") * ROWS - 2 * ROWS
    y_base = position("gy") * (8 * STRIP) + depth_pos * STRIP - STRIP
    odd = depth_pos % 2 == 1
    y_cell = y_base + lane
    y_inside = (y_cell >= 0) & (y_cell < ny_total)
    zero = jnp.zeros((8, LANES), jnp.float32)

    def row_of(ref, lead, r):
        if lead is None:
            return ref[pl.ds(r, 8, stride=0), :]
        return ref[lead, pl.ds(r, 8, stride=0), :]

    def penalty(x_cell):
        inside = (x_cell >= 0) & (x_cell < nx_total) & y_inside
        return jnp.where(inside, jnp.float32(0.0), jnp.float32(STEP_PENALTY))

    shot_x = jnp.broadcast_to(shot_ref[:, 0:1].astype(jnp.float32), (8, LANES))
    shot_y = jnp.broadcast_to(shot_ref[:, 1:2].astype(jnp.float32), (8, LANES))
    y_square = (y_cell.astype(jnp.float32) - shot_y) ** 2

    def surface(r):
        x_cell = (x_base + r).astype(jnp.float32)
        return SURF * jnp.sqrt((x_cell - shot_x) ** 2 + y_square)

    def weight(diff):
        return jnp.exp2(diff * RATE)

    def near(diff):
        return jnp.clip(diff, -1.0, 1.0)

    middle = surface(MIDDLE)
    weight_minus = weight(near(pltpu.roll(middle, 1, 1) - middle))
    weight_plus = weight(near(pltpu.roll(middle, LANES - 1, 1) - middle))
    for r in range(FRAME):
        wa_ref[r + PAD] = weight((surface(r) - middle) + penalty(x_base + r))
    for ref in (wa_ref, wb_ref):
        ref[PAD - 1] = zero
        ref[PAD + FRAME] = zero

    def merged(tiles, j):
        part = tiles[0]
        one, two = (j + 1) % 4, (j + 2) % 4
        part = jnp.where((lane >= STRIP * one) & (lane < STRIP * (one + 1)), tiles[1], part)
        part = jnp.where((lane >= STRIP * two) & (lane < STRIP * (two + 1)), tiles[2], part)
        return rolled(part, -STRIP * j)

    def strips(row):
        at = (pl.ds(row, HALF), slice(None))
        one, two = near_ref[at], far_ref[at]
        left = jnp.where(odd, one, two)
        right = jnp.where(odd, two, one)
        return left, rolled(here_ref[at], STRIP), rolled(right, 2 * STRIP)

    rims = [penalty(x_base + HALF * g + sub) for g in range(FRAME // HALF)]

    for pair in range(PLANES // 2):
        for offset in range(5):
            if pair >= 4 and offset in (0, 4):
                tiles = strips(SHARED_AT + HALF * (pair - 4))
            else:
                tiles = strips(A_AT[offset] + HALF * pair)
            for j in range(4):
                p, h = divmod(j, 2)
                group = 2 * offset + h
                if pair >= 4 and group in (0, 9):
                    continue
                speed = merged(tiles, j)
                at = (2 * pair + p, pl.ds(HALF * group, HALF), slice(None))
                slow = speed + rims[group]
                e1_ref[at] = jnp.exp2(slow * RATE)
                e2_ref[at] = jnp.exp2(slow * (ROOT2 * RATE))
                e3_ref[at] = jnp.exp2(slow * (ROOT3 * RATE))
                if 3 <= group < 7:
                    here = (2 * pair + p, pl.ds(HALF * (group - 3), HALF), slice(None))
                    earth_ref[here] = speed

    for offset in range(3):
        for v in range(4):
            tiles = strips(S_AT[offset] + HALF * v)
            for i in range(4):
                src_ref[ROWS * offset + 4 * v + i] = merged(tiles, i)
        tiles = strips(S_AT[offset] + 32)
        for h in range(2):
            inside = rims[2 + 2 * offset + h] < 0.5
            refl_ref[pl.ds(ROWS * offset + HALF * h, HALF), :] = jnp.where(
                inside, merged(tiles, h), jnp.float32(-1.0)
            )

    for r in range(48):
        wsel_ref[r] = zero + 1.0

    def along_y(value):
        return weight_minus * pltpu.roll(value, 1, 1) + weight_plus * pltpu.roll(
            value, LANES - 1, 1
        )

    def down_plane(k, w_ref, next_ref, first, last, select):
        level = k.astype(jnp.float32)
        w_before, w_now = w_ref[first - 1 + PAD], w_ref[first + PAD]
        q_before, q_now = along_y(w_before), along_y(w_now)
        for r in range(first, last):
            w_after = w_ref[r + 1 + PAD]
            q_after = along_y(w_after)
            part1 = row_of(e1_ref, k, r) * w_now
            part2 = row_of(e2_ref, k, r) * (q_now + (w_before + w_after))
            part3 = row_of(e3_ref, k, r) * (q_before + q_after)
            w_next = part1 + part2 + part3
            next_ref[r + PAD] = w_next
            if 31 <= r < 49:
                head_ref[k, r - 31] = part1 + ROOT2 * part2 + ROOT3 * part3
            if select and 16 <= r < 64:
                hit = row_of(refl_ref, None, r - 16) == level
                wsel_ref[r - 16] = jnp.where(hit, w_next, wsel_ref[r - 16])
            w_before, q_before, w_now, q_now = w_now, q_now, w_after, q_after

    def down(first, last, select):
        def two(i, carry):
            down_plane(2 * i, wa_ref, wb_ref, first, last, select)
            down_plane(2 * i + 1, wb_ref, wa_ref, first, last, select)
            return carry

        return two

    lax.fori_loop(0, 2, down(1, 79, False), 0)
    lax.fori_loop(2, 4, down(5, 75, True), 0)
    lax.fori_loop(4, 6, down(9, 71, True), 0)
    lax.fori_loop(6, 8, down(13, 67, True), 0)

    for ref in (ma_ref, mb_ref):
        ref[15 + PAD] = zero
        ref[64 + PAD] = zero

    for r in range(48):
        share = src_ref[r] / wsel_ref[r]
        wsel_ref[r] = share
        hit = row_of(refl_ref, None, r) == float(PLANES - 1)
        ma_ref[r + 16 + PAD] = jnp.where(hit, share, jnp.float32(0.0))
    for i in range(18):
        col_ref[i : i + 1, :] = jnp.sum(src_ref[15 + i], axis=0, keepdims=True)

    def gradient_rows(k, mu_ref):
        for i in range(18):
            product = mu_ref[31 + i + PAD] * head_ref[k, i]
            grad_ref[k, i : i + 1, :] = jnp.sum(product, axis=0, keepdims=True)

    def up(k, mu_ref, next_ref, first, last):
        gradient_rows(k, mu_ref)
        level = (k - 1).astype(jnp.float32)

        def spread(r):
            mu = mu_ref[r + PAD]
            return row_of(e1_ref, k, r) * mu, row_of(e2_ref, k, r) * mu, row_of(e3_ref, k, r) * mu

        _, u2_before, u3_before = spread(first - 1)
        u1, u2, u3 = spread(first)
        for r in range(first, last):
            n1, n2, n3 = spread(r + 1)
            both = u2 + (u3_before + n3)
            side = pltpu.roll(weight_plus * both, 1, 1) + pltpu.roll(
                weight_minus * both, LANES - 1, 1
            )
            hit = row_of(refl_ref, None, r - 16) == level
            own = jnp.where(hit, wsel_ref[r - 16], jnp.float32(0.0))
            next_ref[r + PAD] = (u1 + own) + (u2_before + n2) + side
            u2_before, u3_before, u1, u2, u3 = u2, u3, n1, n2, n3

    def up_two(top, first, last):
        def two(step, carry):
            k = top - 2 * step
            up(k, ma_ref, mb_ref, first, last)
            up(k - 1, mb_ref, ma_ref, first, last)
            return carry

        return two

    lax.fori_loop(0, 2, up_two(15, 17, 63), 0)
    lax.fori_loop(0, 2, up_two(11, 21, 59), 0)
    lax.fori_loop(0, 2, up_two(7, 25, 55), 0)
    up_two(3, 29, 51)(jnp.int32(0), 0)
    up(jnp.int32(1), ma_ref, mb_ref, 31, 49)
    gradient_rows(0, mb_ref)

    for pair in range(PLANES // 2):
        parts = []
        for p in range(2):
            k = 2 * pair + p
            shown = jnp.where(
                float(k) <= refl_ref[15:33, :], col_ref[0:18, :], jnp.float32(0.0)
            )
            raw_ref[k, 0:18, :] = jnp.where(
                earth_ref[k, 7:25, :] < AIR_TEST, grad_ref[k, 0:18, :] + shown, jnp.float32(0.0)
            )
            for h in range(2):
                mid = raw_ref[k, HALF * h + 1 : HALF * h + 9, :]
                column = (raw_ref[k, HALF * h : HALF * h + 8, :] + mid) + raw_ref[
                    k, HALF * h + 2 : HALF * h + 10, :
                ]
                total = column + (pltpu.roll(column, 1, 1) + pltpu.roll(column, LANES - 1, 1))
                smooth = 0.4375 * mid + 0.0625 * total
                parts.append(rolled(smooth, STRIP * (2 * p + h - 1)))
        out_ref[pl.ds(HALF * pair, HALF), :] = quarters(parts, lane)


def unpack_kernel(in_ref, out_ref):
    lane = lane_index()
    for c in range(2):
        tiles = [in_ref[pl.ds(HALF * (4 * c + q), HALF), :] for q in range(4)]
        for j in range(4):
            parts = [rolled(tiles[q], STRIP * (q - j)) for q in range(4)]
            out_ref[j // 2, pl.ds(HALF * (j % 2), HALF), pl.ds(LANES * c, LANES)] = quarters(
                parts, lane
            )


def in_vmem(count):
    return [pl.BlockSpec(memory_space=pltpu.VMEM)] * count


def line(count, shift):
    return [(i, i + shift) for i in range(count) if 0 <= i + shift < count]


def sweep_call(shot_cells, near, column, far, nx_total, ny_total):
    def kernel(*refs):
        sweep_kernel(*refs, nx_total=nx_total, ny_total=ny_total)

    field = (FULL, SHOTS, LANES)
    return pl.pallas_call(
        kernel,
        out_shape=jax.ShapeDtypeStruct((TILE, LANES), jnp.float32),
        in_specs=in_vmem(4),
        out_specs=in_vmem(1)[0],
        scratch_shapes=[
            *[pltpu.VMEM(field, jnp.float32)] * 2,
            *[pltpu.VMEM((PLANES, FULL, LANES), jnp.float32)] * 3,
            pltpu.VMEM((PLANES, 18, SHOTS, LANES), jnp.float32),
            *[pltpu.VMEM(field, jnp.float32)] * 2,
            pltpu.VMEM((48, SHOTS, LANES), jnp.float32),
            pltpu.VMEM((56, LANES), jnp.float32),
            pltpu.VMEM((48, SHOTS, LANES), jnp.float32),
            pltpu.VMEM((PLANES, 32, LANES), jnp.float32),
            pltpu.VMEM((PLANES, 24, LANES), jnp.float32),
            pltpu.VMEM((24, LANES), jnp.float32),
            pltpu.VMEM((PLANES, 24, LANES), jnp.float32),
        ],
        compiler_params=pltpu.CompilerParams(vmem_limit_bytes=SWEEP_VMEM),
        name="sweep",
    )(shot_cells, near, column, far)


def local(slowness, air_mask, reflector, shot_cells, receiver_mask, residual):
    depth_count = lax.axis_size("depth")
    x_count = lax.axis_size("gx")
    y_count = lax.axis_size("gy")
    nx_total = ROWS * x_count
    ny_total = STRIP * depth_count * y_count
    f32 = jnp.float32

    stay = [
        pltpu.with_memory_space_constraint(a, pltpu.HBM)
        for a in (slowness, air_mask, reflector, receiver_mask, residual)
    ]
    packed = pl.pallas_call(
        pack_kernel,
        out_shape=jax.ShapeDtypeStruct((4 * TILE, LANES), f32),
        in_specs=[pl.BlockSpec(memory_space=pltpu.HBM)] * 5,
        out_specs=in_vmem(1)[0],
        scratch_shapes=[
            *[
                pltpu.VMEM(arg.shape, arg.dtype)
                for arg in (slowness, air_mask, reflector, receiver_mask, residual)
            ],
            pltpu.VMEM((2, SHOTS, ROWS + 8, LANES), f32),
            pltpu.VMEM((2, ROWS + 8, LANES), f32),
            pltpu.SemaphoreType.DMA((5,)),
        ],
        compiler_params=pltpu.CompilerParams(vmem_limit_bytes=SMALL_VMEM),
        name="pack",
    )(*stay)

    pairs = [
        [d * x_count + 2 * i + m for d in range(depth_count) for m in range(2)]
        for i in range(x_count // 2)
    ]
    got = lax.all_to_all(
        packed.reshape(16, 2 * HALF, LANES),
        ("depth", "gx"),
        0,
        0,
        tiled=True,
        axis_index_groups=pairs,
    )
    own, up, down = pl.pallas_call(
        stage_kernel,
        out_shape=tuple(jax.ShapeDtypeStruct((n, HALF, LANES), f32) for n in (26, 19, 19)),
        in_specs=in_vmem(1),
        out_specs=tuple(in_vmem(3)),
        compiler_params=pltpu.CompilerParams(vmem_limit_bytes=SMALL_VMEM),
        name="stage",
    )(got.reshape(32, HALF, LANES))
    above = lax.ppermute(up, "gx", line(x_count, 2))
    below = lax.ppermute(down, "gx", line(x_count, -2))
    column = pl.pallas_call(
        arrange_kernel,
        out_shape=jax.ShapeDtypeStruct((COLUMN, LANES), f32),
        in_specs=in_vmem(3),
        out_specs=in_vmem(1)[0],
        compiler_params=pltpu.CompilerParams(vmem_limit_bytes=SMALL_VMEM),
        name="arrange",
    )(above, own, below)

    def place(q):
        return (q % depth_count) * y_count + q // depth_count

    def swapped(first):
        pairs = [(q, q + 1) for q in range(first, depth_count * y_count - 1, 2)]
        return [(place(i), place(j)) for a, b in pairs for i, j in ((a, b), (b, a))]

    near = lax.ppermute(column, ("depth", "gy"), swapped(0))
    far = lax.ppermute(column, ("depth", "gy"), swapped(1))

    strips_out = sweep_call(shot_cells, near, column, far, nx_total, ny_total)
    parts = lax.all_to_all(
        strips_out.reshape(8, HALF, LANES), "depth", 0, 0, tiled=True
    ).reshape(TILE, LANES)
    return pl.pallas_call(
        unpack_kernel,
        out_shape=jax.ShapeDtypeStruct(slowness.shape, f32),
        in_specs=in_vmem(1),
        out_specs=in_vmem(1)[0],
        compiler_params=pltpu.CompilerParams(vmem_limit_bytes=SMALL_VMEM),
        name="unpack",
    )(parts)


def solution(mesh):
    in_specs = (
        P("depth", "gx", "gy"),
        P("depth", "gx", "gy"),
        P("gx", "gy"),
        P(),
        P(None, "gx", "gy"),
        P(None, "gx", "gy"),
    )
    out_specs = P("depth", "gx", "gy")
    return jax.shard_map(local, mesh=mesh, in_specs=in_specs, out_specs=out_specs, check_vma=False)
```

```python
import math

import jax
import jax.numpy as jnp
from jax import lax
from jax.experimental import pallas as pl
from jax.experimental.pallas import tpu as pltpu
from jax.sharding import PartitionSpec as P

SOFTMIN_TEMPER = 0.5
SURF = 0.7
AIR_SLOW = 2.5
AIR_TEST = 2.0
STEP_PENALTY = 10000.0
RATE = -1.0 / (SOFTMIN_TEMPER * math.log(2.0))
ROOT2 = math.sqrt(2.0)
ROOT3 = math.sqrt(3.0)

LANES = 128
STRIP = 32
ROWS = 16
PLANES = 16
SHOTS = 8
FRAME = 80
PAD = 8
FULL = FRAME + 2 * PAD
TILE = 64
A_AT = (0, 32, 96, 160, 224)
SHARED_AT = 256
S_AT = (288, 328, 368)
COLUMN = 408
MIDDLE = 40
HALF = 8
SWEEP_VMEM = 16 * 1024 * 1024
SMALL_VMEM = 4 * 1024 * 1024


def position(axis):
    return lax.axis_index(axis)


def rolled(value, shift):
    shift = shift % LANES
    return value if shift == 0 else pltpu.roll(value, shift, value.ndim - 1)


def lane_index(rows=8):
    return lax.broadcasted_iota(jnp.int32, (rows, LANES), 1)


def quarters(parts, lane):
    out = parts[0]
    for j in range(1, len(parts)):
        out = jnp.where(lane >= STRIP * j, parts[j], out)
    return out


def pack_kernel(*refs):
    out_ref, live_ref, level_ref, sems = refs[5], refs[11], refs[12], refs[13]
    copies = [pltpu.make_async_copy(refs[i], refs[6 + i], sems.at[i]) for i in range(5)]
    for copy in copies:
        copy.start()
    for copy in copies:
        copy.wait()
    slow_ref, air_ref, refl_ref, mask_ref, resid_ref = refs[6:11]
    lane = lane_index()
    sub = lax.broadcasted_iota(jnp.int32, (8, LANES), 0)
    first = 2 * position("depth")
    speed = {}
    for p in range(2):
        for h in range(2):
            for c in range(2):
                at = (p, pl.ds(HALF * h, HALF), pl.ds(LANES * c, LANES))
                speed[p, h, c] = jnp.where(air_ref[at] == 1, jnp.float32(AIR_SLOW), slow_ref[at])
    for h in range(2):
        for c in range(2):
            here = pl.ds(HALF * h, HALF)
            at = (here, pl.ds(LANES * c, LANES))
            level_ref[c, here, :] = refl_ref[at].astype(jnp.float32)
            for shot in range(SHOTS):
                live_ref[c, shot, here, :] = jnp.where(
                    mask_ref[shot, *at] == 1, resid_ref[shot, *at], jnp.float32(0.0)
                )
    rows = {}
    for i in range(2):
        for c in range(2):
            at = (pl.ds(first + i, 8, stride=0), slice(None))
            rows[2 + i, c] = level_ref[c, *at]
            row = live_ref[c, 0, *at]
            for shot in range(1, SHOTS):
                row = jnp.where(sub >= shot, live_ref[c, shot, *at], row)
            rows[i, c] = row
    for target in range(8):
        c, q = divmod(target, 4)
        planes = quarters(
            [rolled(speed[j // 2, j % 2, c], STRIP * (j - q)) for j in range(4)], lane
        )
        sources = quarters([rolled(rows[j, c], STRIP * (j - q)) for j in range(4)], lane)
        for member in range(2):
            at = 2 * HALF * (2 * target + member)
            out_ref[pl.ds(at, HALF), :] = planes
            out_ref[pl.ds(at + HALF, HALF), :] = sources


def stage_kernel(got_ref, own_ref, up_ref, down_ref):
    lane = lane_index()
    sub = lax.broadcasted_iota(jnp.int32, (8, LANES), 0)
    odd_quarter = (lane // STRIP) % 2 == 1
    speed = [[got_ref[4 * d + 2 * m] for d in range(8)] for m in range(2)]
    source = []
    for m in range(2):
        parts = [got_ref[4 * d + 2 * m + 1] for d in range(8)]
        tiles = [
            jnp.where(lane < 2 * STRIP, parts[2 * v], rolled(parts[2 * v + 1], 2 * STRIP))
            for v in range(4)
        ]
        levels = []
        for h in range(2):
            rows = parts[4 * h]
            for d in range(1, 4):
                rows = jnp.where(sub >= 2 * d, parts[4 * h + d], rows)
            even, odd = rolled(rows, 2 * STRIP), rolled(rows, STRIP)
            levels.append(jnp.where(sub % 2 == 1, odd, even))
        tiles.append(jnp.where(lane < STRIP, levels[0], rolled(levels[1], STRIP)))
        source.append(tiles)
    outer_up = [
        jnp.where(odd_quarter, speed[0][d], rolled(speed[0][d + 1], -STRIP)) for d in (4, 6)
    ]
    outer_down = [
        jnp.where(odd_quarter, rolled(speed[1][d + 1], STRIP), speed[1][d]) for d in (4, 6)
    ]
    for ref, tiles in (
        (own_ref, [*speed[0], *speed[1], *source[0], *source[1]]),
        (up_ref, [*speed[0][:4], *outer_up, *speed[1], *source[1]]),
        (down_ref, [*speed[0], *speed[1][:4], *outer_down, *source[0]]),
    ):
        for i, tile in enumerate(tiles):
            ref[i] = tile


def arrange_kernel(above_ref, own_ref, below_ref, out_ref):
    lane = lane_index()
    second = position("gx") % 2 == 1
    odd_quarter = (lane // STRIP) % 2 == 1

    def outer(ref, first, shift):
        tiles = [ref[first + i] for i in range(4)]
        for i in (4, 5):
            part = ref[first + i]
            moved = rolled(part, shift)
            tiles += [part, moved]
        return tiles

    speeds = [
        outer(above_ref, 0, STRIP),
        [above_ref[6 + i] for i in range(8)],
        [own_ref[i] for i in range(8)],
        [own_ref[8 + i] for i in range(8)],
        [below_ref[i] for i in range(8)],
        outer(below_ref, 8, -STRIP),
    ]
    sources = [
        [ref[first + i] for i in range(5)]
        for ref, first in ((above_ref, 14), (own_ref, 16), (own_ref, 21), (below_ref, 14))
    ]

    def picked(choices, i, part):
        return jnp.where(second, choices[i + 1][part], choices[i][part])

    for offset in range(5):
        for part in range(4 if offset in (0, 4) else 8):
            out_ref[pl.ds(A_AT[offset] + HALF * part, HALF), :] = picked(speeds, offset, part)
    for part in range(4, 8):
        out_ref[pl.ds(SHARED_AT + HALF * (part - 4), HALF), :] = jnp.where(
            odd_quarter, picked(speeds, 0, part), picked(speeds, 4, part)
        )
    for offset in range(3):
        for part in range(5):
            at = pl.ds(S_AT[offset] + HALF * part, HALF)
            out_ref[at, :] = picked(sources, offset, part)


def frame_of(nx_total, ny_total):
    x_base = position("gx") * ROWS - 2 * ROWS
    y_base = position("gy") * (8 * STRIP) + position("depth") * STRIP - STRIP
    y_cell = y_base + lane_index()
    y_inside = (y_cell >= 0) & (y_cell < ny_total)

    def penalty(x_cell):
        inside = (x_cell >= 0) & (x_cell < nx_total) & y_inside
        return jnp.where(inside, jnp.float32(0.0), jnp.float32(STEP_PENALTY))

    return x_base, y_cell, penalty


def start_kernel(shot_ref, start_ref, weight_ref, nx_total, ny_total):
    x_base, y_cell, penalty = frame_of(nx_total, ny_total)
    zero = jnp.zeros((8, LANES), jnp.float32)
    shot_x = jnp.broadcast_to(shot_ref[:, 0:1].astype(jnp.float32), (8, LANES))
    shot_y = jnp.broadcast_to(shot_ref[:, 1:2].astype(jnp.float32), (8, LANES))
    y_square = (y_cell.astype(jnp.float32) - shot_y) ** 2

    def surface(r):
        x_cell = (x_base + r).astype(jnp.float32)
        return SURF * jnp.sqrt((x_cell - shot_x) ** 2 + y_square)

    def weight(diff):
        return jnp.exp2(diff * RATE)

    def near(diff):
        return jnp.clip(diff, -1.0, 1.0)

    middle = surface(MIDDLE)
    weight_ref[0] = weight(near(pltpu.roll(middle, 1, 1) - middle))
    weight_ref[1] = weight(near(pltpu.roll(middle, LANES - 1, 1) - middle))
    for r in range(FRAME):
        start_ref[r + PAD] = weight((surface(r) - middle) + penalty(x_base + r))
    start_ref[PAD - 1] = zero
    start_ref[PAD + FRAME] = zero


def sweep_kernel(
    start_ref,
    weight_ref,
    near_ref,
    here_ref,
    far_ref,
    out_ref,
    wa_ref,
    wb_ref,
    e1_ref,
    e2_ref,
    e3_ref,
    head_ref,
    ma_ref,
    mb_ref,
    src_ref,
    refl_ref,
    wsel_ref,
    earth_ref,
    grad_ref,
    col_ref,
    raw_ref,
    nx_total,
    ny_total,
):
    lane = lane_index()
    sub = lax.broadcasted_iota(jnp.int32, (8, LANES), 0)
    odd = position("depth") % 2 == 1
    zero = jnp.zeros((8, LANES), jnp.float32)
    x_base, _, penalty = frame_of(nx_total, ny_total)

    def row_of(ref, lead, r):
        if lead is None:
            return ref[pl.ds(r, 8, stride=0), :]
        return ref[lead, pl.ds(r, 8, stride=0), :]

    weight_minus, weight_plus = weight_ref[0], weight_ref[1]
    for ref in (wa_ref, wb_ref):
        ref[PAD - 1] = zero
        ref[PAD + FRAME] = zero

    def merged(tiles, j):
        part = tiles[0]
        one, two = (j + 1) % 4, (j + 2) % 4
        part = jnp.where((lane >= STRIP * one) & (lane < STRIP * (one + 1)), tiles[1], part)
        part = jnp.where((lane >= STRIP * two) & (lane < STRIP * (two + 1)), tiles[2], part)
        return rolled(part, -STRIP * j)

    def strips(row):
        at = (pl.ds(row, HALF), slice(None))
        one, two = near_ref[at], far_ref[at]
        left = jnp.where(odd, one, two)
        right = jnp.where(odd, two, one)
        return left, rolled(here_ref[at], STRIP), rolled(right, 2 * STRIP)

    rims = [penalty(x_base + HALF * g + sub) for g in range(FRAME // HALF)]

    for pair in range(PLANES // 2):
        for offset in range(5):
            if pair >= 4 and offset in (0, 4):
                tiles = strips(SHARED_AT + HALF * (pair - 4))
            else:
                tiles = strips(A_AT[offset] + HALF * pair)
            for j in range(4):
                p, h = divmod(j, 2)
                group = 2 * offset + h
                if pair >= 4 and group in (0, 9):
                    continue
                speed = merged(tiles, j)
                at = (2 * pair + p, pl.ds(HALF * group, HALF), slice(None))
                slow = speed + rims[group]
                e1_ref[at] = jnp.exp2(slow * RATE)
                e2_ref[at] = jnp.exp2(slow * (ROOT2 * RATE))
                e3_ref[at] = jnp.exp2(slow * (ROOT3 * RATE))
                if 3 <= group < 7:
                    here = (2 * pair + p, pl.ds(HALF * (group - 3), HALF), slice(None))
                    earth_ref[here] = speed

    for offset in range(3):
        for v in range(4):
            tiles = strips(S_AT[offset] + HALF * v)
            for i in range(4):
                src_ref[ROWS * offset + 4 * v + i] = merged(tiles, i)
        tiles = strips(S_AT[offset] + 32)
        for h in range(2):
            inside = rims[2 + 2 * offset + h] < 0.5
            refl_ref[pl.ds(ROWS * offset + HALF * h, HALF), :] = jnp.where(
                inside, merged(tiles, h), jnp.float32(-1.0)
            )

    for r in range(48):
        wsel_ref[r] = zero + 1.0

    def along_y(value):
        return weight_minus * pltpu.roll(value, 1, 1) + weight_plus * pltpu.roll(
            value, LANES - 1, 1
        )

    def down_plane(k, w_ref, next_ref, first, last, select):
        level = k.astype(jnp.float32)
        w_before, w_now = w_ref[first - 1 + PAD], w_ref[first + PAD]
        q_before, q_now = along_y(w_before), along_y(w_now)
        for r in range(first, last):
            w_after = w_ref[r + 1 + PAD]
            q_after = along_y(w_after)
            part1 = row_of(e1_ref, k, r) * w_now
            part2 = row_of(e2_ref, k, r) * (q_now + (w_before + w_after))
            part3 = row_of(e3_ref, k, r) * (q_before + q_after)
            w_next = part1 + part2 + part3
            next_ref[r + PAD] = w_next
            if 31 <= r < 49:
                head_ref[k, r - 31] = part1 + ROOT2 * part2 + ROOT3 * part3
            if select and 16 <= r < 64:
                hit = row_of(refl_ref, None, r - 16) == level
                wsel_ref[r - 16] = jnp.where(hit, w_next, wsel_ref[r - 16])
            w_before, q_before, w_now, q_now = w_now, q_now, w_after, q_after

    def down(first, last, select):
        def two(i, carry):
            down_plane(2 * i, wa_ref, wb_ref, first, last, select)
            down_plane(2 * i + 1, wb_ref, wa_ref, first, last, select)
            return carry

        return two

    down_plane(jnp.int32(0), start_ref, wb_ref, 1, 79, False)
    down_plane(jnp.int32(1), wb_ref, wa_ref, 2, 78, False)
    down_plane(jnp.int32(2), wa_ref, wb_ref, 3, 77, False)
    down_plane(jnp.int32(3), wb_ref, wa_ref, 4, 76, False)
    lax.fori_loop(2, 4, down(5, 75, True), 0)
    lax.fori_loop(4, 6, down(9, 71, True), 0)
    lax.fori_loop(6, 8, down(13, 67, True), 0)

    for ref in (ma_ref, mb_ref):
        ref[15 + PAD] = zero
        ref[64 + PAD] = zero

    for r in range(48):
        share = src_ref[r] / wsel_ref[r]
        wsel_ref[r] = share
        hit = row_of(refl_ref, None, r) == float(PLANES - 1)
        ma_ref[r + 16 + PAD] = jnp.where(hit, share, jnp.float32(0.0))
    for i in range(18):
        col_ref[i : i + 1, :] = jnp.sum(src_ref[15 + i], axis=0, keepdims=True)

    def gradient_rows(k, mu_ref):
        for i in range(18):
            product = mu_ref[31 + i + PAD] * head_ref[k, i]
            grad_ref[k, i : i + 1, :] = jnp.sum(product, axis=0, keepdims=True)

    def up(k, mu_ref, next_ref, first, last):
        gradient_rows(k, mu_ref)
        level = (k - 1).astype(jnp.float32)

        def spread(r):
            mu = mu_ref[r + PAD]
            return row_of(e1_ref, k, r) * mu, row_of(e2_ref, k, r) * mu, row_of(e3_ref, k, r) * mu

        _, u2_before, u3_before = spread(first - 1)
        u1, u2, u3 = spread(first)
        for r in range(first, last):
            n1, n2, n3 = spread(r + 1)
            both = u2 + (u3_before + n3)
            side = pltpu.roll(weight_plus * both, 1, 1) + pltpu.roll(
                weight_minus * both, LANES - 1, 1
            )
            hit = row_of(refl_ref, None, r - 16) == level
            own = jnp.where(hit, wsel_ref[r - 16], jnp.float32(0.0))
            next_ref[r + PAD] = (u1 + own) + (u2_before + n2) + side
            u2_before, u3_before, u1, u2, u3 = u2, u3, n1, n2, n3

    def up_two(top, first, last):
        def two(step, carry):
            k = top - 2 * step
            up(k, ma_ref, mb_ref, first, last)
            up(k - 1, mb_ref, ma_ref, first, last)
            return carry

        return two

    lax.fori_loop(0, 2, up_two(15, 17, 63), 0)
    lax.fori_loop(0, 2, up_two(11, 21, 59), 0)
    lax.fori_loop(0, 2, up_two(7, 25, 55), 0)
    up_two(3, 29, 51)(jnp.int32(0), 0)
    up(jnp.int32(1), ma_ref, mb_ref, 31, 49)
    gradient_rows(0, mb_ref)

    for pair in range(PLANES // 2):
        parts = []
        for p in range(2):
            k = 2 * pair + p
            shown = jnp.where(
                float(k) <= refl_ref[15:33, :], col_ref[0:18, :], jnp.float32(0.0)
            )
            raw_ref[k, 0:18, :] = jnp.where(
                earth_ref[k, 7:25, :] < AIR_TEST, grad_ref[k, 0:18, :] + shown, jnp.float32(0.0)
            )
            for h in range(2):
                mid = raw_ref[k, HALF * h + 1 : HALF * h + 9, :]
                column = (raw_ref[k, HALF * h : HALF * h + 8, :] + mid) + raw_ref[
                    k, HALF * h + 2 : HALF * h + 10, :
                ]
                total = column + (pltpu.roll(column, 1, 1) + pltpu.roll(column, LANES - 1, 1))
                smooth = 0.4375 * mid + 0.0625 * total
                parts.append(rolled(smooth, STRIP * (2 * p + h - 1)))
        out_ref[pl.ds(HALF * pair, HALF), :] = quarters(parts, lane)


def unpack_kernel(in_ref, out_ref):
    lane = lane_index()
    for c in range(2):
        tiles = [in_ref[pl.ds(HALF * (4 * c + q), HALF), :] for q in range(4)]
        for j in range(4):
            parts = [rolled(tiles[q], STRIP * (q - j)) for q in range(4)]
            out_ref[j // 2, pl.ds(HALF * (j % 2), HALF), pl.ds(LANES * c, LANES)] = quarters(
                parts, lane
            )


def in_vmem(count):
    return [pl.BlockSpec(memory_space=pltpu.VMEM)] * count


def line(count, shift):
    return [(i, i + shift) for i in range(count) if 0 <= i + shift < count]


def sweep_call(start, weights, near, column, far, nx_total, ny_total):
    def kernel(*refs):
        sweep_kernel(*refs, nx_total=nx_total, ny_total=ny_total)

    field = (FULL, SHOTS, LANES)
    return pl.pallas_call(
        kernel,
        out_shape=jax.ShapeDtypeStruct((TILE, LANES), jnp.float32),
        in_specs=in_vmem(5),
        out_specs=in_vmem(1)[0],
        scratch_shapes=[
            *[pltpu.VMEM(field, jnp.float32)] * 2,
            *[pltpu.VMEM((PLANES, FULL, LANES), jnp.float32)] * 3,
            pltpu.VMEM((PLANES, 18, SHOTS, LANES), jnp.float32),
            *[pltpu.VMEM(field, jnp.float32)] * 2,
            pltpu.VMEM((48, SHOTS, LANES), jnp.float32),
            pltpu.VMEM((56, LANES), jnp.float32),
            pltpu.VMEM((48, SHOTS, LANES), jnp.float32),
            pltpu.VMEM((PLANES, 32, LANES), jnp.float32),
            pltpu.VMEM((PLANES, 24, LANES), jnp.float32),
            pltpu.VMEM((24, LANES), jnp.float32),
            pltpu.VMEM((PLANES, 24, LANES), jnp.float32),
        ],
        compiler_params=pltpu.CompilerParams(vmem_limit_bytes=SWEEP_VMEM),
        name="sweep",
    )(start, weights, near, column, far)


def local(slowness, air_mask, reflector, shot_cells, receiver_mask, residual):
    depth_count = lax.axis_size("depth")
    x_count = lax.axis_size("gx")
    y_count = lax.axis_size("gy")
    nx_total = ROWS * x_count
    ny_total = STRIP * depth_count * y_count
    f32 = jnp.float32

    stay = [
        pltpu.with_memory_space_constraint(a, pltpu.HBM)
        for a in (slowness, air_mask, reflector, receiver_mask, residual)
    ]
    packed = pl.pallas_call(
        pack_kernel,
        out_shape=jax.ShapeDtypeStruct((4 * TILE, LANES), f32),
        in_specs=[pl.BlockSpec(memory_space=pltpu.HBM)] * 5,
        out_specs=in_vmem(1)[0],
        scratch_shapes=[
            *[
                pltpu.VMEM(arg.shape, arg.dtype)
                for arg in (slowness, air_mask, reflector, receiver_mask, residual)
            ],
            pltpu.VMEM((2, SHOTS, ROWS + 8, LANES), f32),
            pltpu.VMEM((2, ROWS + 8, LANES), f32),
            pltpu.SemaphoreType.DMA((5,)),
        ],
        compiler_params=pltpu.CompilerParams(vmem_limit_bytes=SMALL_VMEM),
        name="pack",
    )(*stay)

    pairs = [
        [d * x_count + 2 * i + m for d in range(depth_count) for m in range(2)]
        for i in range(x_count // 2)
    ]
    got = lax.all_to_all(
        packed.reshape(16, 2 * HALF, LANES),
        ("depth", "gx"),
        0,
        0,
        tiled=True,
        axis_index_groups=pairs,
    )
    own, up, down = pl.pallas_call(
        stage_kernel,
        out_shape=tuple(jax.ShapeDtypeStruct((n, HALF, LANES), f32) for n in (26, 19, 19)),
        in_specs=in_vmem(1),
        out_specs=tuple(in_vmem(3)),
        compiler_params=pltpu.CompilerParams(vmem_limit_bytes=SMALL_VMEM),
        name="stage",
    )(got.reshape(32, HALF, LANES))
    above = lax.ppermute(up, "gx", line(x_count, 2))
    below = lax.ppermute(down, "gx", line(x_count, -2))
    column = pl.pallas_call(
        arrange_kernel,
        out_shape=jax.ShapeDtypeStruct((COLUMN, LANES), f32),
        in_specs=in_vmem(3),
        out_specs=in_vmem(1)[0],
        compiler_params=pltpu.CompilerParams(vmem_limit_bytes=SMALL_VMEM),
        name="arrange",
    )(above, own, below)

    shots, column = lax.optimization_barrier((shot_cells, column))

    def start_body(*refs):
        start_kernel(*refs, nx_total=nx_total, ny_total=ny_total)

    start, weights = pl.pallas_call(
        start_body,
        out_shape=(
            jax.ShapeDtypeStruct((FULL, SHOTS, LANES), f32),
            jax.ShapeDtypeStruct((2, SHOTS, LANES), f32),
        ),
        in_specs=in_vmem(1),
        out_specs=tuple(in_vmem(2)),
        compiler_params=pltpu.CompilerParams(vmem_limit_bytes=SMALL_VMEM),
        cost_estimate=pl.CostEstimate(
            flops=20 * FRAME * 1024, bytes_accessed=4 * FULL * 1024, transcendentals=FRAME * 2048
        ),
        name="start",
    )(shots)

    def place(q):
        return (q % depth_count) * y_count + q // depth_count

    def swapped(first):
        pairs = [(q, q + 1) for q in range(first, depth_count * y_count - 1, 2)]
        return [(place(i), place(j)) for a, b in pairs for i, j in ((a, b), (b, a))]

    near = lax.ppermute(column, ("depth", "gy"), swapped(0))
    far = lax.ppermute(column, ("depth", "gy"), swapped(1))

    strips_out = sweep_call(start, weights, near, column, far, nx_total, ny_total)
    parts = lax.all_to_all(
        strips_out.reshape(8, HALF, LANES), "depth", 0, 0, tiled=True
    ).reshape(TILE, LANES)
    return pl.pallas_call(
        unpack_kernel,
        out_shape=jax.ShapeDtypeStruct(slowness.shape, f32),
        in_specs=in_vmem(1),
        out_specs=in_vmem(1)[0],
        compiler_params=pltpu.CompilerParams(vmem_limit_bytes=SMALL_VMEM),
        name="unpack",
    )(parts)


def solution(mesh):
    in_specs = (
        P("depth", "gx", "gy"),
        P("depth", "gx", "gy"),
        P("gx", "gy"),
        P(),
        P(None, "gx", "gy"),
        P(None, "gx", "gy"),
    )
    out_specs = P("depth", "gx", "gy")
    return jax.shard_map(local, mesh=mesh, in_specs=in_specs, out_specs=out_specs, check_vma=False)
```

```python
import functools
import math

import jax
import jax.numpy as jnp
from jax import lax
from jax.experimental import pallas as pl
from jax.experimental.pallas import tpu as pltpu
from jax.sharding import PartitionSpec as P

SOFTMIN_TEMPER = 0.5
SURF = 0.7
AIR_SLOW = 2.5
AIR_TEST = 2.0
STEP_PENALTY = 10000.0
RATE = -1.0 / (SOFTMIN_TEMPER * math.log(2.0))
ROOT2 = math.sqrt(2.0)
ROOT3 = math.sqrt(3.0)

LANES = 128
STRIP = 32
ROWS = 16
PLANES = 16
SHOTS = 8
FRAME = 80
PAD = 8
FULL = FRAME + 2 * PAD
TILE = 64
A_AT = (0, 32, 96, 160, 224)
SHARED_AT = 256
S_AT = (288, 328, 368)
COLUMN = 408
MIDDLE = 40
HALF = 8
SWEEP_VMEM = 16 * 1024 * 1024
SMALL_VMEM = 4 * 1024 * 1024


def position(axis):
    return lax.axis_index(axis)


def rolled(value, shift):
    shift = shift % LANES
    return value if shift == 0 else pltpu.roll(value, shift, value.ndim - 1)


def lane_index(rows=8):
    return lax.broadcasted_iota(jnp.int32, (rows, LANES), 1)


def quarters(parts, lane):
    out = parts[0]
    for j in range(1, len(parts)):
        out = jnp.where(lane >= STRIP * j, parts[j], out)
    return out


def pack_kernel(*refs):
    out_ref, live_ref, level_ref, sems = refs[5], refs[11], refs[12], refs[13]
    copies = [pltpu.make_async_copy(refs[i], refs[6 + i], sems.at[i]) for i in range(5)]
    for copy in copies:
        copy.start()
    for copy in copies:
        copy.wait()
    slow_ref, air_ref, refl_ref, mask_ref, resid_ref = refs[6:11]
    lane = lane_index()
    sub = lax.broadcasted_iota(jnp.int32, (8, LANES), 0)
    first = 2 * position("depth")
    speed = {}
    for p in range(2):
        for h in range(2):
            for c in range(2):
                at = (p, pl.ds(HALF * h, HALF), pl.ds(LANES * c, LANES))
                speed[p, h, c] = jnp.where(air_ref[at] == 1, jnp.float32(AIR_SLOW), slow_ref[at])
    for h in range(2):
        for c in range(2):
            here = pl.ds(HALF * h, HALF)
            at = (here, pl.ds(LANES * c, LANES))
            level_ref[c, here, :] = refl_ref[at].astype(jnp.float32)
            for shot in range(SHOTS):
                live_ref[c, shot, here, :] = jnp.where(
                    mask_ref[shot, *at] == 1, resid_ref[shot, *at], jnp.float32(0.0)
                )
    rows = {}
    for i in range(2):
        for c in range(2):
            at = (pl.ds(first + i, 8, stride=0), slice(None))
            rows[2 + i, c] = level_ref[c, *at]
            row = live_ref[c, 0, *at]
            for shot in range(1, SHOTS):
                row = jnp.where(sub >= shot, live_ref[c, shot, *at], row)
            rows[i, c] = row
    for target in range(8):
        c, q = divmod(target, 4)
        planes = quarters(
            [rolled(speed[j // 2, j % 2, c], STRIP * (j - q)) for j in range(4)], lane
        )
        sources = quarters([rolled(rows[j, c], STRIP * (j - q)) for j in range(4)], lane)
        for member in range(2):
            at = 2 * HALF * (2 * target + member)
            out_ref[pl.ds(at, HALF), :] = planes
            out_ref[pl.ds(at + HALF, HALF), :] = sources


def stage_kernel(got_ref, own_ref, up_ref, down_ref):
    lane = lane_index()
    sub = lax.broadcasted_iota(jnp.int32, (8, LANES), 0)
    odd_quarter = (lane // STRIP) % 2 == 1
    speed = [[got_ref[4 * d + 2 * m] for d in range(8)] for m in range(2)]
    source = []
    for m in range(2):
        parts = [got_ref[4 * d + 2 * m + 1] for d in range(8)]
        tiles = [
            jnp.where(lane < 2 * STRIP, parts[2 * v], rolled(parts[2 * v + 1], 2 * STRIP))
            for v in range(4)
        ]
        levels = []
        for h in range(2):
            rows = parts[4 * h]
            for d in range(1, 4):
                rows = jnp.where(sub >= 2 * d, parts[4 * h + d], rows)
            even, odd = rolled(rows, 2 * STRIP), rolled(rows, STRIP)
            levels.append(jnp.where(sub % 2 == 1, odd, even))
        tiles.append(jnp.where(lane < STRIP, levels[0], rolled(levels[1], STRIP)))
        source.append(tiles)
    outer_up = [
        jnp.where(odd_quarter, speed[0][d], rolled(speed[0][d + 1], -STRIP)) for d in (4, 6)
    ]
    outer_down = [
        jnp.where(odd_quarter, rolled(speed[1][d + 1], STRIP), speed[1][d]) for d in (4, 6)
    ]
    for ref, tiles in (
        (own_ref, [*speed[0], *speed[1], *source[0], *source[1]]),
        (up_ref, [*speed[0][:4], *outer_up, *speed[1], *source[1]]),
        (down_ref, [*speed[0], *speed[1][:4], *outer_down, *source[0]]),
    ):
        for i, tile in enumerate(tiles):
            ref[i] = tile


def arrange_kernel(above_ref, own_ref, below_ref, out_ref):
    lane = lane_index()
    second = position("gx") % 2 == 1
    odd_quarter = (lane // STRIP) % 2 == 1

    def outer(ref, first, shift):
        tiles = [ref[first + i] for i in range(4)]
        for i in (4, 5):
            part = ref[first + i]
            moved = rolled(part, shift)
            tiles += [part, moved]
        return tiles

    speeds = [
        outer(above_ref, 0, STRIP),
        [above_ref[6 + i] for i in range(8)],
        [own_ref[i] for i in range(8)],
        [own_ref[8 + i] for i in range(8)],
        [below_ref[i] for i in range(8)],
        outer(below_ref, 8, -STRIP),
    ]
    sources = [
        [ref[first + i] for i in range(5)]
        for ref, first in ((above_ref, 14), (own_ref, 16), (own_ref, 21), (below_ref, 14))
    ]

    def picked(choices, i, part):
        return jnp.where(second, choices[i + 1][part], choices[i][part])

    for offset in range(5):
        for part in range(4 if offset in (0, 4) else 8):
            out_ref[pl.ds(A_AT[offset] + HALF * part, HALF), :] = picked(speeds, offset, part)
    for part in range(4, 8):
        out_ref[pl.ds(SHARED_AT + HALF * (part - 4), HALF), :] = jnp.where(
            odd_quarter, picked(speeds, 0, part), picked(speeds, 4, part)
        )
    for offset in range(3):
        for part in range(5):
            at = pl.ds(S_AT[offset] + HALF * part, HALF)
            out_ref[at, :] = picked(sources, offset, part)


def frame_of(nx_total, ny_total):
    x_base = position("gx") * ROWS - 2 * ROWS
    y_base = position("gy") * (8 * STRIP) + position("depth") * STRIP - STRIP
    y_cell = y_base + lane_index()
    y_inside = (y_cell >= 0) & (y_cell < ny_total)

    def penalty(x_cell):
        inside = (x_cell >= 0) & (x_cell < nx_total) & y_inside
        return jnp.where(inside, jnp.float32(0.0), jnp.float32(STEP_PENALTY))

    return x_base, y_cell, penalty


def start_kernel(shot_ref, start_ref, weight_ref, nx_total, ny_total):
    x_base, y_cell, penalty = frame_of(nx_total, ny_total)
    zero = jnp.zeros((8, LANES), jnp.float32)
    shot_x = jnp.broadcast_to(shot_ref[:, 0:1].astype(jnp.float32), (8, LANES))
    shot_y = jnp.broadcast_to(shot_ref[:, 1:2].astype(jnp.float32), (8, LANES))
    y_square = (y_cell.astype(jnp.float32) - shot_y) ** 2

    def surface(r):
        x_cell = (x_base + r).astype(jnp.float32)
        return SURF * jnp.sqrt((x_cell - shot_x) ** 2 + y_square)

    def weight(diff):
        return jnp.exp2(diff * RATE)

    def near(diff):
        return jnp.clip(diff, -1.0, 1.0)

    middle = surface(MIDDLE)
    weight_ref[0] = weight(near(pltpu.roll(middle, 1, 1) - middle))
    weight_ref[1] = weight(near(pltpu.roll(middle, LANES - 1, 1) - middle))
    for r in range(FRAME):
        start_ref[r + PAD] = weight((surface(r) - middle) + penalty(x_base + r))
    start_ref[PAD - 1] = zero
    start_ref[PAD + FRAME] = zero


def sweep_kernel(
    start_ref,
    weight_ref,
    near_ref,
    here_ref,
    far_ref,
    out_ref,
    wa_ref,
    wb_ref,
    e1_ref,
    e2_ref,
    e3_ref,
    head_ref,
    ma_ref,
    mb_ref,
    src_ref,
    refl_ref,
    wsel_ref,
    earth_ref,
    grad_ref,
    col_ref,
    raw_ref,
    nx_total,
    ny_total,
):
    lane = lane_index()
    sub = lax.broadcasted_iota(jnp.int32, (8, LANES), 0)
    odd = position("depth") % 2 == 1
    zero = jnp.zeros((8, LANES), jnp.float32)
    x_base, _, penalty = frame_of(nx_total, ny_total)

    def row_of(ref, lead, r):
        if lead is None:
            return ref[pl.ds(r, 8, stride=0), :]
        return ref[lead, pl.ds(r, 8, stride=0), :]

    weight_minus, weight_plus = weight_ref[0], weight_ref[1]
    for ref in (wa_ref, wb_ref):
        ref[PAD - 1] = zero
        ref[PAD + FRAME] = zero

    def copy_start(b, carry):
        for i in range(16):
            wa_ref[PAD + b * 16 + i] = start_ref[PAD + b * 16 + i]
        return carry

    lax.fori_loop(0, FRAME // 16, copy_start, 0)

    def merged(tiles, j):
        part = tiles[0]
        one, two = (j + 1) % 4, (j + 2) % 4
        part = jnp.where((lane >= STRIP * one) & (lane < STRIP * (one + 1)), tiles[1], part)
        part = jnp.where((lane >= STRIP * two) & (lane < STRIP * (two + 1)), tiles[2], part)
        return rolled(part, -STRIP * j)

    def strips(row):
        at = (pl.ds(row, HALF), slice(None))
        one, two = near_ref[at], far_ref[at]
        left = jnp.where(odd, one, two)
        right = jnp.where(odd, two, one)
        return left, rolled(here_ref[at], STRIP), rolled(right, 2 * STRIP)

    rims = [penalty(x_base + HALF * g + sub) for g in range(FRAME // HALF)]

    def exponents(first, step, carry):
        for i in range(2):
            pair = first + 2 * step + i
            for offset in range(5):
                if first and offset in (0, 4):
                    tiles = strips(pl.multiple_of(SHARED_AT + HALF * (pair - 4), HALF))
                else:
                    tiles = strips(pl.multiple_of(A_AT[offset] + HALF * pair, HALF))
                for j in range(4):
                    p, h = divmod(j, 2)
                    group = 2 * offset + h
                    if first and group in (0, 9):
                        continue
                    slow = merged(tiles, j) + rims[group]
                    at = (2 * pair + p, pl.ds(HALF * group, HALF), slice(None))
                    e1_ref[at] = jnp.exp2(slow * RATE)
                    e2_ref[at] = jnp.exp2(slow * (ROOT2 * RATE))
                    e3_ref[at] = jnp.exp2(slow * (ROOT3 * RATE))
                    if 3 <= group < 7:
                        here = (2 * pair + p, pl.ds(HALF * (group - 3), HALF), slice(None))
                        earth_ref[here] = slow
        return carry

    for first in (0, 4):
        lax.fori_loop(0, 2, functools.partial(exponents, first), 0)

    for offset in range(3):
        for v in range(4):
            tiles = strips(S_AT[offset] + HALF * v)
            for i in range(4):
                src_ref[ROWS * offset + 4 * v + i] = merged(tiles, i)
        tiles = strips(S_AT[offset] + 32)
        for h in range(2):
            inside = rims[2 + 2 * offset + h] < 0.5
            refl_ref[pl.ds(ROWS * offset + HALF * h, HALF), :] = jnp.where(
                inside, merged(tiles, h), jnp.float32(-1.0)
            )

    for r in range(48):
        wsel_ref[r] = zero + 1.0

    def along_y(value):
        return weight_minus * pltpu.roll(value, 1, 1) + weight_plus * pltpu.roll(
            value, LANES - 1, 1
        )

    def down_plane(k, w_ref, next_ref, first, last, select):
        level = k.astype(jnp.float32)
        w_before, w_now = w_ref[first - 1 + PAD], w_ref[first + PAD]
        q_before, q_now = along_y(w_before), along_y(w_now)
        for r in range(first, last):
            w_after = w_ref[r + 1 + PAD]
            q_after = along_y(w_after)
            part1 = row_of(e1_ref, k, r) * w_now
            part2 = row_of(e2_ref, k, r) * (q_now + (w_before + w_after))
            part3 = row_of(e3_ref, k, r) * (q_before + q_after)
            w_next = part1 + part2 + part3
            next_ref[r + PAD] = w_next
            if 31 <= r < 49:
                head_ref[k, r - 31] = part1 + ROOT2 * part2 + ROOT3 * part3
            if select and 16 <= r < 64:
                hit = row_of(refl_ref, None, r - 16) == level
                wsel_ref[r - 16] = jnp.where(hit, w_next, wsel_ref[r - 16])
            w_before, q_before, w_now, q_now = w_now, q_now, w_after, q_after

    def down(first, last, select):
        def two(i, carry):
            down_plane(2 * i, wa_ref, wb_ref, first, last, select)
            down_plane(2 * i + 1, wb_ref, wa_ref, first, last, select)
            return carry

        return two

    lax.fori_loop(0, 4, down(1, 79, True), 0)
    lax.fori_loop(4, 8, down(9, 71, True), 0)

    for ref in (ma_ref, mb_ref):
        ref[15 + PAD] = zero
        ref[64 + PAD] = zero

    for r in range(48):
        share = src_ref[r] / wsel_ref[r]
        wsel_ref[r] = share
        hit = row_of(refl_ref, None, r) == float(PLANES - 1)
        ma_ref[r + 16 + PAD] = jnp.where(hit, share, jnp.float32(0.0))
    for i in range(18):
        col_ref[i : i + 1, :] = jnp.sum(src_ref[15 + i], axis=0, keepdims=True)

    def gradient_rows(k, mu_ref):
        for i in range(18):
            product = mu_ref[31 + i + PAD] * head_ref[k, i]
            grad_ref[k, i : i + 1, :] = jnp.sum(product, axis=0, keepdims=True)

    def up(k, mu_ref, next_ref, first, last):
        gradient_rows(k, mu_ref)
        level = (k - 1).astype(jnp.float32)

        def spread(r):
            mu = mu_ref[r + PAD]
            return row_of(e1_ref, k, r) * mu, row_of(e2_ref, k, r) * mu, row_of(e3_ref, k, r) * mu

        _, u2_before, u3_before = spread(first - 1)
        u1, u2, u3 = spread(first)
        for r in range(first, last):
            n1, n2, n3 = spread(r + 1)
            both = u2 + (u3_before + n3)
            side = pltpu.roll(weight_plus * both, 1, 1) + pltpu.roll(
                weight_minus * both, LANES - 1, 1
            )
            hit = row_of(refl_ref, None, r - 16) == level
            own = jnp.where(hit, wsel_ref[r - 16], jnp.float32(0.0))
            next_ref[r + PAD] = (u1 + own) + (u2_before + n2) + side
            u2_before, u3_before, u1, u2, u3 = u2, u3, n1, n2, n3

    def up_two(top, first, last):
        def two(step, carry):
            k = top - 2 * step
            up(k, ma_ref, mb_ref, first, last)
            up(k - 1, mb_ref, ma_ref, first, last)
            return carry

        return two

    lax.fori_loop(0, 2, up_two(15, 17, 63), 0)
    lax.fori_loop(0, 2, up_two(11, 21, 59), 0)
    lax.fori_loop(0, 2, up_two(7, 25, 55), 0)
    up_two(3, 29, 51)(jnp.int32(0), 0)
    up(jnp.int32(1), ma_ref, mb_ref, 31, 49)
    gradient_rows(0, mb_ref)

    for pair in range(PLANES // 2):
        parts = []
        for p in range(2):
            k = 2 * pair + p
            shown = jnp.where(
                float(k) <= refl_ref[15:33, :], col_ref[0:18, :], jnp.float32(0.0)
            )
            raw_ref[k, 0:18, :] = jnp.where(
                earth_ref[k, 7:25, :] < AIR_TEST, grad_ref[k, 0:18, :] + shown, jnp.float32(0.0)
            )
            for h in range(2):
                mid = raw_ref[k, HALF * h + 1 : HALF * h + 9, :]
                column = (raw_ref[k, HALF * h : HALF * h + 8, :] + mid) + raw_ref[
                    k, HALF * h + 2 : HALF * h + 10, :
                ]
                total = column + (pltpu.roll(column, 1, 1) + pltpu.roll(column, LANES - 1, 1))
                smooth = 0.4375 * mid + 0.0625 * total
                parts.append(rolled(smooth, STRIP * (2 * p + h - 1)))
        out_ref[pl.ds(HALF * pair, HALF), :] = quarters(parts, lane)


def unpack_kernel(in_ref, out_ref):
    lane = lane_index()
    for c in range(2):
        tiles = [in_ref[pl.ds(HALF * (4 * c + q), HALF), :] for q in range(4)]
        for j in range(4):
            parts = [rolled(tiles[q], STRIP * (q - j)) for q in range(4)]
            out_ref[j // 2, pl.ds(HALF * (j % 2), HALF), pl.ds(LANES * c, LANES)] = quarters(
                parts, lane
            )


def in_vmem(count):
    return [pl.BlockSpec(memory_space=pltpu.VMEM)] * count


def line(count, shift):
    return [(i, i + shift) for i in range(count) if 0 <= i + shift < count]


def sweep_call(start, weights, near, column, far, nx_total, ny_total):
    def kernel(*refs):
        sweep_kernel(*refs, nx_total=nx_total, ny_total=ny_total)

    field = (FULL, SHOTS, LANES)
    return pl.pallas_call(
        kernel,
        out_shape=jax.ShapeDtypeStruct((TILE, LANES), jnp.float32),
        in_specs=in_vmem(5),
        out_specs=in_vmem(1)[0],
        scratch_shapes=[
            *[pltpu.VMEM(field, jnp.float32)] * 2,
            *[pltpu.VMEM((PLANES, FULL, LANES), jnp.float32)] * 3,
            pltpu.VMEM((PLANES, 18, SHOTS, LANES), jnp.float32),
            *[pltpu.VMEM(field, jnp.float32)] * 2,
            pltpu.VMEM((48, SHOTS, LANES), jnp.float32),
            pltpu.VMEM((56, LANES), jnp.float32),
            pltpu.VMEM((48, SHOTS, LANES), jnp.float32),
            pltpu.VMEM((PLANES, 32, LANES), jnp.float32),
            pltpu.VMEM((PLANES, 24, LANES), jnp.float32),
            pltpu.VMEM((24, LANES), jnp.float32),
            pltpu.VMEM((PLANES, 24, LANES), jnp.float32),
        ],
        compiler_params=pltpu.CompilerParams(vmem_limit_bytes=SWEEP_VMEM),
        name="sweep",
    )(start, weights, near, column, far)


def local(slowness, air_mask, reflector, shot_cells, receiver_mask, residual):
    depth_count = lax.axis_size("depth")
    x_count = lax.axis_size("gx")
    y_count = lax.axis_size("gy")
    nx_total = ROWS * x_count
    ny_total = STRIP * depth_count * y_count
    f32 = jnp.float32

    stay = [
        pltpu.with_memory_space_constraint(a, pltpu.HBM)
        for a in (slowness, air_mask, reflector, receiver_mask, residual)
    ]
    packed = pl.pallas_call(
        pack_kernel,
        out_shape=jax.ShapeDtypeStruct((4 * TILE, LANES), f32),
        in_specs=[pl.BlockSpec(memory_space=pltpu.HBM)] * 5,
        out_specs=in_vmem(1)[0],
        scratch_shapes=[
            *[
                pltpu.VMEM(arg.shape, arg.dtype)
                for arg in (slowness, air_mask, reflector, receiver_mask, residual)
            ],
            pltpu.VMEM((2, SHOTS, ROWS + 8, LANES), f32),
            pltpu.VMEM((2, ROWS + 8, LANES), f32),
            pltpu.SemaphoreType.DMA((5,)),
        ],
        compiler_params=pltpu.CompilerParams(vmem_limit_bytes=SMALL_VMEM),
        name="pack",
    )(*stay)

    pairs = [
        [d * x_count + 2 * i + m for d in range(depth_count) for m in range(2)]
        for i in range(x_count // 2)
    ]
    got = lax.all_to_all(
        packed.reshape(16, 2 * HALF, LANES),
        ("depth", "gx"),
        0,
        0,
        tiled=True,
        axis_index_groups=pairs,
    )
    own, up, down = pl.pallas_call(
        stage_kernel,
        out_shape=tuple(jax.ShapeDtypeStruct((n, HALF, LANES), f32) for n in (26, 19, 19)),
        in_specs=in_vmem(1),
        out_specs=tuple(in_vmem(3)),
        compiler_params=pltpu.CompilerParams(vmem_limit_bytes=SMALL_VMEM),
        name="stage",
    )(got.reshape(32, HALF, LANES))
    above = lax.ppermute(up, "gx", line(x_count, 2))
    below = lax.ppermute(down, "gx", line(x_count, -2))
    column = pl.pallas_call(
        arrange_kernel,
        out_shape=jax.ShapeDtypeStruct((COLUMN, LANES), f32),
        in_specs=in_vmem(3),
        out_specs=in_vmem(1)[0],
        compiler_params=pltpu.CompilerParams(vmem_limit_bytes=SMALL_VMEM),
        name="arrange",
    )(above, own, below)

    shots, column = lax.optimization_barrier((shot_cells, column))

    def start_body(*refs):
        start_kernel(*refs, nx_total=nx_total, ny_total=ny_total)

    start, weights = pl.pallas_call(
        start_body,
        out_shape=(
            jax.ShapeDtypeStruct((FULL, SHOTS, LANES), f32),
            jax.ShapeDtypeStruct((2, SHOTS, LANES), f32),
        ),
        in_specs=in_vmem(1),
        out_specs=tuple(in_vmem(2)),
        compiler_params=pltpu.CompilerParams(vmem_limit_bytes=SMALL_VMEM),
        cost_estimate=pl.CostEstimate(
            flops=20 * FRAME * 1024, bytes_accessed=4 * FULL * 1024, transcendentals=FRAME * 2048
        ),
        name="start",
    )(shots)

    def place(q):
        return (q % depth_count) * y_count + q // depth_count

    def swapped(first):
        pairs = [(q, q + 1) for q in range(first, depth_count * y_count - 1, 2)]
        return [(place(i), place(j)) for a, b in pairs for i, j in ((a, b), (b, a))]

    near = lax.ppermute(column, ("depth", "gy"), swapped(0))
    far = lax.ppermute(column, ("depth", "gy"), swapped(1))

    strips_out = sweep_call(start, weights, near, column, far, nx_total, ny_total)
    parts = lax.all_to_all(
        strips_out.reshape(8, HALF, LANES), "depth", 0, 0, tiled=True
    ).reshape(TILE, LANES)
    return pl.pallas_call(
        unpack_kernel,
        out_shape=jax.ShapeDtypeStruct(slowness.shape, f32),
        in_specs=in_vmem(1),
        out_specs=in_vmem(1)[0],
        compiler_params=pltpu.CompilerParams(vmem_limit_bytes=SMALL_VMEM),
        name="unpack",
    )(parts)


def solution(mesh):
    in_specs = (
        P("depth", "gx", "gy"),
        P("depth", "gx", "gy"),
        P("gx", "gy"),
        P(),
        P(None, "gx", "gy"),
        P(None, "gx", "gy"),
    )
    out_specs = P("depth", "gx", "gy")
    return jax.shard_map(local, mesh=mesh, in_specs=in_specs, out_specs=out_specs, check_vma=False)
```

```python
import functools
import math

import jax
import jax.numpy as jnp
from jax import lax
from jax.experimental import pallas as pl
from jax.experimental.pallas import tpu as pltpu
from jax.sharding import PartitionSpec as P

SOFTMIN_TEMPER = 0.5
SURF = 0.7
AIR_SLOW = 2.5
AIR_TEST = 2.0
STEP_PENALTY = 10000.0
RATE = -1.0 / (SOFTMIN_TEMPER * math.log(2.0))
ROOT2 = math.sqrt(2.0)
ROOT3 = math.sqrt(3.0)

LANES = 128
STRIP = 32
ROWS = 16
PLANES = 16
SHOTS = 8
FRAME = 80
PAD = 8
FULL = FRAME + 2 * PAD
TILE = 64
A_AT = (0, 32, 96, 160, 224)
SHARED_AT = 256
S_AT = (288, 328, 368)
COLUMN = 408
MIDDLE = 40
HALF = 8
SWEEP_VMEM = 16 * 1024 * 1024
SMALL_VMEM = 4 * 1024 * 1024


def position(axis):
    return lax.axis_index(axis)


def rolled(value, shift):
    shift = shift % LANES
    return value if shift == 0 else pltpu.roll(value, shift, value.ndim - 1)


def lane_index(rows=8):
    return lax.broadcasted_iota(jnp.int32, (rows, LANES), 1)


def quarters(parts, lane):
    out = parts[0]
    for j in range(1, len(parts)):
        out = jnp.where(lane >= STRIP * j, parts[j], out)
    return out


def pack_kernel(*refs):
    out_ref, live_ref, level_ref, sems = refs[5], refs[11], refs[12], refs[13]
    half = pl.ds(pl.multiple_of(HALF * (position("depth") // 4), HALF), HALF)
    parts = [refs[0], refs[1], refs[2].at[half], refs[3].at[:, half], refs[4].at[:, half]]
    copies = [pltpu.make_async_copy(parts[i], refs[6 + i], sems.at[i]) for i in range(5)]
    for copy in copies:
        copy.start()
    for copy in copies:
        copy.wait()
    slow_ref, air_ref, refl_ref, mask_ref, resid_ref = refs[6:11]
    lane = lane_index()
    sub = lax.broadcasted_iota(jnp.int32, (8, LANES), 0)
    first = 2 * (position("depth") % 4)
    speed = {}
    for p in range(2):
        for h in range(2):
            for c in range(2):
                at = (p, pl.ds(HALF * h, HALF), pl.ds(LANES * c, LANES))
                speed[p, h, c] = jnp.where(air_ref[at] == 1, jnp.float32(AIR_SLOW), slow_ref[at])
    for c in range(2):
        here = pl.ds(0, HALF)
        at = (slice(None), pl.ds(LANES * c, LANES))
        level_ref[c, here, :] = refl_ref[at].astype(jnp.float32)
        for shot in range(SHOTS):
            live_ref[c, shot, here, :] = jnp.where(
                mask_ref[shot, *at] == 1, resid_ref[shot, *at], jnp.float32(0.0)
            )
    rows = {}
    for i in range(2):
        for c in range(2):
            at = (pl.ds(first + i, 8, stride=0), slice(None))
            rows[2 + i, c] = level_ref[c, *at]
            row = live_ref[c, 0, *at]
            for shot in range(1, SHOTS):
                row = jnp.where(sub >= shot, live_ref[c, shot, *at], row)
            rows[i, c] = row
    for target in range(8):
        c, q = divmod(target, 4)
        planes = quarters(
            [rolled(speed[j // 2, j % 2, c], STRIP * (j - q)) for j in range(4)], lane
        )
        sources = quarters([rolled(rows[j, c], STRIP * (j - q)) for j in range(4)], lane)
        for member in range(2):
            at = 2 * HALF * (2 * target + member)
            out_ref[pl.ds(at, HALF), :] = planes
            out_ref[pl.ds(at + HALF, HALF), :] = sources


def stage_kernel(got_ref, own_ref, up_ref, down_ref):
    lane = lane_index()
    sub = lax.broadcasted_iota(jnp.int32, (8, LANES), 0)
    odd_quarter = (lane // STRIP) % 2 == 1
    speed = [[got_ref[4 * d + 2 * m] for d in range(8)] for m in range(2)]
    source = []
    for m in range(2):
        parts = [got_ref[4 * d + 2 * m + 1] for d in range(8)]
        tiles = [
            jnp.where(lane < 2 * STRIP, parts[2 * v], rolled(parts[2 * v + 1], 2 * STRIP))
            for v in range(4)
        ]
        levels = []
        for h in range(2):
            rows = parts[4 * h]
            for d in range(1, 4):
                rows = jnp.where(sub >= 2 * d, parts[4 * h + d], rows)
            even, odd = rolled(rows, 2 * STRIP), rolled(rows, STRIP)
            levels.append(jnp.where(sub % 2 == 1, odd, even))
        tiles.append(jnp.where(lane < STRIP, levels[0], rolled(levels[1], STRIP)))
        source.append(tiles)
    outer_up = [
        jnp.where(odd_quarter, speed[0][d], rolled(speed[0][d + 1], -STRIP)) for d in (4, 6)
    ]
    outer_down = [
        jnp.where(odd_quarter, rolled(speed[1][d + 1], STRIP), speed[1][d]) for d in (4, 6)
    ]
    for ref, tiles in (
        (own_ref, [*speed[0], *speed[1], *source[0], *source[1]]),
        (up_ref, [*speed[0][:4], *outer_up, *speed[1], *source[1]]),
        (down_ref, [*speed[0], *speed[1][:4], *outer_down, *source[0]]),
    ):
        for i, tile in enumerate(tiles):
            ref[i] = tile


def arrange_kernel(above_ref, own_ref, below_ref, out_ref):
    lane = lane_index()
    second = position("gx") % 2 == 1
    odd_quarter = (lane // STRIP) % 2 == 1

    def outer(ref, first, shift):
        tiles = [ref[first + i] for i in range(4)]
        for i in (4, 5):
            part = ref[first + i]
            moved = rolled(part, shift)
            tiles += [part, moved]
        return tiles

    speeds = [
        outer(above_ref, 0, STRIP),
        [above_ref[6 + i] for i in range(8)],
        [own_ref[i] for i in range(8)],
        [own_ref[8 + i] for i in range(8)],
        [below_ref[i] for i in range(8)],
        outer(below_ref, 8, -STRIP),
    ]
    sources = [
        [ref[first + i] for i in range(5)]
        for ref, first in ((above_ref, 14), (own_ref, 16), (own_ref, 21), (below_ref, 14))
    ]

    def picked(choices, i, part):
        return jnp.where(second, choices[i + 1][part], choices[i][part])

    for offset in range(5):
        for part in range(4 if offset in (0, 4) else 8):
            out_ref[pl.ds(A_AT[offset] + HALF * part, HALF), :] = picked(speeds, offset, part)
    for part in range(4, 8):
        out_ref[pl.ds(SHARED_AT + HALF * (part - 4), HALF), :] = jnp.where(
            odd_quarter, picked(speeds, 0, part), picked(speeds, 4, part)
        )
    for offset in range(3):
        for part in range(5):
            at = pl.ds(S_AT[offset] + HALF * part, HALF)
            out_ref[at, :] = picked(sources, offset, part)


def frame_of(nx_total, ny_total):
    x_base = position("gx") * ROWS - 2 * ROWS
    y_base = position("gy") * (8 * STRIP) + position("depth") * STRIP - STRIP
    y_cell = y_base + lane_index()
    y_inside = (y_cell >= 0) & (y_cell < ny_total)

    def penalty(x_cell):
        inside = (x_cell >= 0) & (x_cell < nx_total) & y_inside
        return jnp.where(inside, jnp.float32(0.0), jnp.float32(STEP_PENALTY))

    return x_base, y_cell, penalty


def start_kernel(shot_ref, start_ref, weight_ref, nx_total, ny_total):
    x_base, y_cell, penalty = frame_of(nx_total, ny_total)
    zero = jnp.zeros((8, LANES), jnp.float32)
    shot_x = jnp.broadcast_to(shot_ref[:, 0:1].astype(jnp.float32), (8, LANES))
    shot_y = jnp.broadcast_to(shot_ref[:, 1:2].astype(jnp.float32), (8, LANES))
    y_square = (y_cell.astype(jnp.float32) - shot_y) ** 2

    def surface(r):
        x_cell = (x_base + r).astype(jnp.float32)
        return SURF * jnp.sqrt((x_cell - shot_x) ** 2 + y_square)

    def weight(diff):
        return jnp.exp2(diff * RATE)

    def near(diff):
        return jnp.clip(diff, -1.0, 1.0)

    middle = surface(MIDDLE)
    weight_ref[0] = weight(near(pltpu.roll(middle, 1, 1) - middle))
    weight_ref[1] = weight(near(pltpu.roll(middle, LANES - 1, 1) - middle))
    for r in range(FRAME):
        start_ref[r + PAD] = weight((surface(r) - middle) + penalty(x_base + r))
    start_ref[PAD - 1] = zero
    start_ref[PAD + FRAME] = zero


def sweep_kernel(
    start_ref,
    weight_ref,
    near_ref,
    here_ref,
    far_ref,
    out_ref,
    wa_ref,
    wb_ref,
    e1_ref,
    e2_ref,
    e3_ref,
    head_ref,
    ma_ref,
    mb_ref,
    src_ref,
    refl_ref,
    wsel_ref,
    earth_ref,
    grad_ref,
    col_ref,
    raw_ref,
    nx_total,
    ny_total,
):
    lane = lane_index()
    sub = lax.broadcasted_iota(jnp.int32, (8, LANES), 0)
    odd = position("depth") % 2 == 1
    zero = jnp.zeros((8, LANES), jnp.float32)
    x_base, _, penalty = frame_of(nx_total, ny_total)

    def row_of(ref, lead, r):
        if lead is None:
            return ref[pl.ds(r, 8, stride=0), :]
        return ref[lead, pl.ds(r, 8, stride=0), :]

    weight_minus, weight_plus = weight_ref[0], weight_ref[1]
    for ref in (wa_ref, wb_ref):
        ref[PAD - 1] = zero
        ref[PAD + FRAME] = zero

    def copy_start(b, carry):
        for i in range(16):
            wa_ref[PAD + b * 16 + i] = start_ref[PAD + b * 16 + i]
        return carry

    lax.fori_loop(0, FRAME // 16, copy_start, 0)

    def merged(tiles, j):
        part = tiles[0]
        one, two = (j + 1) % 4, (j + 2) % 4
        part = jnp.where((lane >= STRIP * one) & (lane < STRIP * (one + 1)), tiles[1], part)
        part = jnp.where((lane >= STRIP * two) & (lane < STRIP * (two + 1)), tiles[2], part)
        return rolled(part, -STRIP * j)

    def strips(row):
        at = (pl.ds(row, HALF), slice(None))
        one, two = near_ref[at], far_ref[at]
        left = jnp.where(odd, one, two)
        right = jnp.where(odd, two, one)
        return left, rolled(here_ref[at], STRIP), rolled(right, 2 * STRIP)

    rims = [penalty(x_base + HALF * g + sub) for g in range(FRAME // HALF)]

    def exponents(first, step, carry):
        for i in range(2):
            pair = first + 2 * step + i
            for offset in range(5):
                if first and offset in (0, 4):
                    tiles = strips(pl.multiple_of(SHARED_AT + HALF * (pair - 4), HALF))
                else:
                    tiles = strips(pl.multiple_of(A_AT[offset] + HALF * pair, HALF))
                for j in range(4):
                    p, h = divmod(j, 2)
                    group = 2 * offset + h
                    if first and group in (0, 9):
                        continue
                    slow = merged(tiles, j) + rims[group]
                    at = (2 * pair + p, pl.ds(HALF * group, HALF), slice(None))
                    e1_ref[at] = jnp.exp2(slow * RATE)
                    e2_ref[at] = jnp.exp2(slow * (ROOT2 * RATE))
                    e3_ref[at] = jnp.exp2(slow * (ROOT3 * RATE))
                    if 3 <= group < 7:
                        here = (2 * pair + p, pl.ds(HALF * (group - 3), HALF), slice(None))
                        earth_ref[here] = slow
        return carry

    for first in (0, 4):
        lax.fori_loop(0, 2, functools.partial(exponents, first), 0)

    for offset in range(3):
        for v in range(4):
            tiles = strips(S_AT[offset] + HALF * v)
            for i in range(4):
                src_ref[ROWS * offset + 4 * v + i] = merged(tiles, i)
        tiles = strips(S_AT[offset] + 32)
        for h in range(2):
            inside = rims[2 + 2 * offset + h] < 0.5
            refl_ref[pl.ds(ROWS * offset + HALF * h, HALF), :] = jnp.where(
                inside, merged(tiles, h), jnp.float32(-1.0)
            )

    for r in range(48):
        wsel_ref[r] = zero + 1.0

    def along_y(value):
        return weight_minus * pltpu.roll(value, 1, 1) + weight_plus * pltpu.roll(
            value, LANES - 1, 1
        )

    def down_plane(k, w_ref, next_ref, first, last, select):
        level = k.astype(jnp.float32)
        w_before, w_now = w_ref[first - 1 + PAD], w_ref[first + PAD]
        q_before, q_now = along_y(w_before), along_y(w_now)
        for r in range(first, last):
            w_after = w_ref[r + 1 + PAD]
            q_after = along_y(w_after)
            part1 = row_of(e1_ref, k, r) * w_now
            part2 = row_of(e2_ref, k, r) * (q_now + (w_before + w_after))
            part3 = row_of(e3_ref, k, r) * (q_before + q_after)
            w_next = part1 + part2 + part3
            next_ref[r + PAD] = w_next
            if 31 <= r < 49:
                head_ref[k, r - 31] = part1 + ROOT2 * part2 + ROOT3 * part3
            if select and 16 <= r < 64:
                hit = row_of(refl_ref, None, r - 16) == level
                wsel_ref[r - 16] = jnp.where(hit, w_next, wsel_ref[r - 16])
            w_before, q_before, w_now, q_now = w_now, q_now, w_after, q_after

    def down(first, last, select):
        def two(i, carry):
            down_plane(2 * i, wa_ref, wb_ref, first, last, select)
            down_plane(2 * i + 1, wb_ref, wa_ref, first, last, select)
            return carry

        return two

    lax.fori_loop(0, 4, down(1, 79, True), 0)
    lax.fori_loop(4, 8, down(9, 71, True), 0)

    for ref in (ma_ref, mb_ref):
        ref[15 + PAD] = zero
        ref[64 + PAD] = zero

    for r in range(48):
        share = src_ref[r] / wsel_ref[r]
        wsel_ref[r] = share
        hit = row_of(refl_ref, None, r) == float(PLANES - 1)
        ma_ref[r + 16 + PAD] = jnp.where(hit, share, jnp.float32(0.0))
    for i in range(18):
        col_ref[i : i + 1, :] = jnp.sum(src_ref[15 + i], axis=0, keepdims=True)

    def gradient_rows(k, mu_ref):
        for i in range(18):
            product = mu_ref[31 + i + PAD] * head_ref[k, i]
            grad_ref[k, i : i + 1, :] = jnp.sum(product, axis=0, keepdims=True)

    def up(k, mu_ref, next_ref, first, last):
        gradient_rows(k, mu_ref)
        level = (k - 1).astype(jnp.float32)

        def spread(r):
            mu = mu_ref[r + PAD]
            return row_of(e1_ref, k, r) * mu, row_of(e2_ref, k, r) * mu, row_of(e3_ref, k, r) * mu

        _, u2_before, u3_before = spread(first - 1)
        u1, u2, u3 = spread(first)
        for r in range(first, last):
            n1, n2, n3 = spread(r + 1)
            both = u2 + (u3_before + n3)
            side = pltpu.roll(weight_plus * both, 1, 1) + pltpu.roll(
                weight_minus * both, LANES - 1, 1
            )
            hit = row_of(refl_ref, None, r - 16) == level
            own = jnp.where(hit, wsel_ref[r - 16], jnp.float32(0.0))
            next_ref[r + PAD] = (u1 + own) + (u2_before + n2) + side
            u2_before, u3_before, u1, u2, u3 = u2, u3, n1, n2, n3

    def up_two(top, first, last):
        def two(step, carry):
            k = top - 2 * step
            up(k, ma_ref, mb_ref, first, last)
            up(k - 1, mb_ref, ma_ref, first, last)
            return carry

        return two

    lax.fori_loop(0, 2, up_two(15, 17, 63), 0)
    lax.fori_loop(0, 2, up_two(11, 21, 59), 0)
    lax.fori_loop(0, 2, up_two(7, 25, 55), 0)
    up_two(3, 29, 51)(jnp.int32(0), 0)
    up(jnp.int32(1), ma_ref, mb_ref, 31, 49)
    gradient_rows(0, mb_ref)

    for pair in range(PLANES // 2):
        parts = []
        for p in range(2):
            k = 2 * pair + p
            shown = jnp.where(
                float(k) <= refl_ref[15:33, :], col_ref[0:18, :], jnp.float32(0.0)
            )
            raw_ref[k, 0:18, :] = jnp.where(
                earth_ref[k, 7:25, :] < AIR_TEST, grad_ref[k, 0:18, :] + shown, jnp.float32(0.0)
            )
            for h in range(2):
                mid = raw_ref[k, HALF * h + 1 : HALF * h + 9, :]
                column = (raw_ref[k, HALF * h : HALF * h + 8, :] + mid) + raw_ref[
                    k, HALF * h + 2 : HALF * h + 10, :
                ]
                total = column + (pltpu.roll(column, 1, 1) + pltpu.roll(column, LANES - 1, 1))
                smooth = 0.4375 * mid + 0.0625 * total
                parts.append(rolled(smooth, STRIP * (2 * p + h - 1)))
        out_ref[pl.ds(HALF * pair, HALF), :] = quarters(parts, lane)


def unpack_kernel(in_ref, out_ref):
    lane = lane_index()
    for c in range(2):
        tiles = [in_ref[pl.ds(HALF * (4 * c + q), HALF), :] for q in range(4)]
        for j in range(4):
            parts = [rolled(tiles[q], STRIP * (q - j)) for q in range(4)]
            out_ref[j // 2, pl.ds(HALF * (j % 2), HALF), pl.ds(LANES * c, LANES)] = quarters(
                parts, lane
            )


def in_vmem(count):
    return [pl.BlockSpec(memory_space=pltpu.VMEM)] * count


def line(count, shift):
    return [(i, i + shift) for i in range(count) if 0 <= i + shift < count]


def sweep_call(start, weights, near, column, far, nx_total, ny_total):
    def kernel(*refs):
        sweep_kernel(*refs, nx_total=nx_total, ny_total=ny_total)

    field = (FULL, SHOTS, LANES)
    return pl.pallas_call(
        kernel,
        out_shape=jax.ShapeDtypeStruct((TILE, LANES), jnp.float32),
        in_specs=in_vmem(5),
        out_specs=in_vmem(1)[0],
        scratch_shapes=[
            *[pltpu.VMEM(field, jnp.float32)] * 2,
            *[pltpu.VMEM((PLANES, FULL, LANES), jnp.float32)] * 3,
            pltpu.VMEM((PLANES, 18, SHOTS, LANES), jnp.float32),
            *[pltpu.VMEM(field, jnp.float32)] * 2,
            pltpu.VMEM((48, SHOTS, LANES), jnp.float32),
            pltpu.VMEM((56, LANES), jnp.float32),
            pltpu.VMEM((48, SHOTS, LANES), jnp.float32),
            pltpu.VMEM((PLANES, 32, LANES), jnp.float32),
            pltpu.VMEM((PLANES, 24, LANES), jnp.float32),
            pltpu.VMEM((24, LANES), jnp.float32),
            pltpu.VMEM((PLANES, 24, LANES), jnp.float32),
        ],
        compiler_params=pltpu.CompilerParams(vmem_limit_bytes=SWEEP_VMEM),
        name="sweep",
    )(start, weights, near, column, far)


def local(slowness, air_mask, reflector, shot_cells, receiver_mask, residual):
    depth_count = lax.axis_size("depth")
    x_count = lax.axis_size("gx")
    y_count = lax.axis_size("gy")
    nx_total = ROWS * x_count
    ny_total = STRIP * depth_count * y_count
    f32 = jnp.float32

    stay = [
        pltpu.with_memory_space_constraint(a, pltpu.HBM)
        for a in (slowness, air_mask, reflector, receiver_mask, residual)
    ]
    packed = pl.pallas_call(
        pack_kernel,
        out_shape=jax.ShapeDtypeStruct((4 * TILE, LANES), f32),
        in_specs=[pl.BlockSpec(memory_space=pltpu.HBM)] * 5,
        out_specs=in_vmem(1)[0],
        scratch_shapes=[
            *[
                pltpu.VMEM((*arg.shape[:-2], rows, arg.shape[-1]), arg.dtype)
                for arg, rows in (
                    (slowness, ROWS),
                    (air_mask, ROWS),
                    (reflector, HALF),
                    (receiver_mask, HALF),
                    (residual, HALF),
                )
            ],
            pltpu.VMEM((2, SHOTS, HALF + 8, LANES), f32),
            pltpu.VMEM((2, HALF + 8, LANES), f32),
            pltpu.SemaphoreType.DMA((5,)),
        ],
        compiler_params=pltpu.CompilerParams(vmem_limit_bytes=SMALL_VMEM),
        name="pack",
    )(*stay)

    pairs = [
        [d * x_count + 2 * i + m for d in range(depth_count) for m in range(2)]
        for i in range(x_count // 2)
    ]
    got = lax.all_to_all(
        packed.reshape(16, 2 * HALF, LANES),
        ("depth", "gx"),
        0,
        0,
        tiled=True,
        axis_index_groups=pairs,
    )
    own, up, down = pl.pallas_call(
        stage_kernel,
        out_shape=tuple(jax.ShapeDtypeStruct((n, HALF, LANES), f32) for n in (26, 19, 19)),
        in_specs=in_vmem(1),
        out_specs=tuple(in_vmem(3)),
        compiler_params=pltpu.CompilerParams(vmem_limit_bytes=SMALL_VMEM),
        name="stage",
    )(got.reshape(32, HALF, LANES))
    above = lax.ppermute(up, "gx", line(x_count, 2))
    below = lax.ppermute(down, "gx", line(x_count, -2))
    column = pl.pallas_call(
        arrange_kernel,
        out_shape=jax.ShapeDtypeStruct((COLUMN, LANES), f32),
        in_specs=in_vmem(3),
        out_specs=in_vmem(1)[0],
        compiler_params=pltpu.CompilerParams(vmem_limit_bytes=SMALL_VMEM),
        name="arrange",
    )(above, own, below)

    shots, column = lax.optimization_barrier((shot_cells, column))

    def start_body(*refs):
        start_kernel(*refs, nx_total=nx_total, ny_total=ny_total)

    start, weights = pl.pallas_call(
        start_body,
        out_shape=(
            jax.ShapeDtypeStruct((FULL, SHOTS, LANES), f32),
            jax.ShapeDtypeStruct((2, SHOTS, LANES), f32),
        ),
        in_specs=in_vmem(1),
        out_specs=tuple(in_vmem(2)),
        compiler_params=pltpu.CompilerParams(vmem_limit_bytes=SMALL_VMEM),
        cost_estimate=pl.CostEstimate(
            flops=20 * FRAME * 1024, bytes_accessed=4 * FULL * 1024, transcendentals=FRAME * 2048
        ),
        name="start",
    )(shots)

    def place(q):
        return (q % depth_count) * y_count + q // depth_count

    def swapped(first):
        pairs = [(q, q + 1) for q in range(first, depth_count * y_count - 1, 2)]
        return [(place(i), place(j)) for a, b in pairs for i, j in ((a, b), (b, a))]

    near = lax.ppermute(column, ("depth", "gy"), swapped(0))
    far = lax.ppermute(column, ("depth", "gy"), swapped(1))

    strips_out = sweep_call(start, weights, near, column, far, nx_total, ny_total)
    parts = lax.all_to_all(
        strips_out.reshape(8, HALF, LANES), "depth", 0, 0, tiled=True
    ).reshape(TILE, LANES)
    return pl.pallas_call(
        unpack_kernel,
        out_shape=jax.ShapeDtypeStruct(slowness.shape, f32),
        in_specs=in_vmem(1),
        out_specs=in_vmem(1)[0],
        compiler_params=pltpu.CompilerParams(vmem_limit_bytes=SMALL_VMEM),
        name="unpack",
    )(parts)


def solution(mesh):
    in_specs = (
        P("depth", "gx", "gy"),
        P("depth", "gx", "gy"),
        P("gx", "gy"),
        P(),
        P(None, "gx", "gy"),
        P(None, "gx", "gy"),
    )
    out_specs = P("depth", "gx", "gy")
    return jax.shard_map(local, mesh=mesh, in_specs=in_specs, out_specs=out_specs, check_vma=False)
```
